128 devices in a mesh: gx: 4 (over z_lo, core), gy: 4 (over x), gz: 8 (over y, z_hi).
Axes of the slice: x: 4, y: 4, z: 4 (z_hi: 2, z_lo: 2; z = z_hi * 2 + z_lo), core: 2. Of those that a mesh axis runs over, the one named last changes fastest.
Arguments:
- positions: float32 [4, 4, 8, 3, 256], P('gx', 'gy', 'gz'), may hold values from 0 to 1
- species: int32 [4, 4, 8, 256], P('gx', 'gy', 'gz'), may hold values from 0 to 1
- start_block: float32 [4, 4, 8, 4, 3, 256], P('gx', 'gy', 'gz'), may hold values from -560 to 560
- neighbors: int32 [4, 4, 8, 6, 256], P('gx', 'gy', 'gz'), may hold values from 0 to 1151, as said below
- ghost_lists: int32 [8, 8, 16, 16], P('gx', 'gy', 'gz'), may hold values from 0 to 255
- embedding: float32 [2, 64], replicated, may hold values from 0.5 to 1.5
- radial_in: float32 [8, 128], replicated, may hold values from -2 to 2
- radial_out: float32 [128, 64], replicated, may hold values from -0.5 to 0.5
- readout: float32 [64], replicated, may hold values from -0.75 to 0.75
Outputs:
- next_block: float32 [4, 4, 8, 4, 3, 256], P('gx', 'gy', 'gz')
- diagonal_blocks: float32 [2, 4, 4], replicated
- offdiagonal_blocks: float32 [2, 4, 4], replicated
The draws below stay inside these ranges and needn't reach their ends.
Inputs may be any that keep to these rules, and one draw needn't show every extreme that they name: `neighbors`: about two thirds of the slots name the device's own atoms, the rest ghost entries.
All inputs are finite; a program needn't handle non-finite values.
Results may differ from the reference program's by a relative error of at most 0.0003.
Values sent between devices are 32-bit elements; how exact they have to be, the bound alone decides.
A program may use at most 192 MiB of HBM per device.

```python
import math
import jax
import jax.numpy as jnp
import numpy as np
from jax import lax

ATOMS_DEV = 256
NEIGHBORS = 6
CHANNELS = 64
RADIAL_HIDDEN = 128
BASIS = 8
SPECIES = 2
VECTORS = 4
PRODUCTS = 2
GHOSTS = 16
N_GX = 4
N_GY = 4
N_GZ = 8


def draw_start_block(key, part):
    base_key = jax.random.fold_in(key, 7)
    subkeys = jax.random.split(base_key, 3)
    shape_full = (N_GX, N_GY, N_GZ, VECTORS, 3, ATOMS_DEV)
    entries = jax.random.truncated_normal(subkeys[0], -4.0, 4.0, shape_full, jnp.float32)
    atom_scale = jnp.exp(jax.random.uniform(subkeys[1], (N_GX, N_GY, N_GZ, 1, 1, ATOMS_DEV), jnp.float32, 0.0, math.log(10.0)))
    column_scale = jnp.exp(jax.random.uniform(subkeys[2], (1, 1, 1, VECTORS, 1, 1), jnp.float32, 0.0, math.log(10.0)))
    return entries * atom_scale * column_scale


def draw_neighbors(key, part):
    base_key = jax.random.fold_in(key, 11)
    subkeys = jax.random.split(base_key, 3)
    shape_full = (N_GX, N_GY, N_GZ, NEIGHBORS, ATOMS_DEV)
    own_pick = jax.random.randint(subkeys[0], shape_full, 0, ATOMS_DEV, jnp.int32)
    ghost_pick = jax.random.randint(subkeys[1], shape_full, ATOMS_DEV, ATOMS_DEV + 56 * GHOSTS, jnp.int32)
    select = jax.random.randint(subkeys[2], shape_full, 0, 100, jnp.int32)
    combined_output = jnp.where(select < 35, ghost_pick, own_pick)
    combined_output = combined_output.at[:, :, :, 0, 0].set(0)
    combined_output = combined_output.at[:, :, :, 0, 1].set(ATOMS_DEV + 56 * GHOSTS - 1)
    return combined_output


def set_ends(drawn, stream_key, low, top_value):
    dims = drawn.shape
    place = [jax.random.randint(jax.random.fold_in(stream_key, axis), (), 0, dims[axis]) for axis in range(len(dims))]
    drawn = drawn.at[tuple(place)].set(low)
    longest = dims.index(max(dims))
    place[longest] = (place[longest] + 1) % dims[longest]
    return drawn.at[tuple(place)].set(top_value)


def shard_levels(own_key, dims, cuts, least, high):
    loudness, own = 1.0, jax.random.fold_in(own_key, 6)
    for dim, blocks in cuts:
        draws = jnp.exp(jax.random.uniform(jax.random.fold_in(own, dim), (blocks,), jnp.float32, least / len(cuts), high / len(cuts)))
        loudness = loudness * jnp.repeat(draws, dims[dim] // blocks).reshape([-1 if axis == dim else 1 for axis in range(len(dims))])
    return loudness


def scatter_about(key, shape, scale, most, kind=jnp.bfloat16):
    values = jax.random.normal(key, shape, jnp.float32) * scale
    return jnp.minimum(jnp.maximum(values, -most), most).astype(kind)


def setup_inputs(seed: int = 0) -> dict:
    key_list = jax.random.split(jax.random.key(seed), 10)
    positions = jnp.clip(1.0 * jax.random.uniform(key_list[0], (N_GX, N_GY, N_GZ, 3, ATOMS_DEV), jnp.float32) ** shard_levels(key_list[0], (N_GX, N_GY, N_GZ, 3, ATOMS_DEV), ((0, 4), (1, 4), (2, 8)), -0.2, 0.2), 0.0, 1.0)
    species = set_ends(jax.random.randint(key_list[1], (N_GX, N_GY, N_GZ, ATOMS_DEV), 0, SPECIES), jax.random.fold_in(key_list[1], 1), 0, SPECIES - 1).astype(jnp.int32)
    start_block = draw_start_block(jax.random.fold_in(key_list[9], 71), 0)
    neighbors = draw_neighbors(jax.random.fold_in(key_list[9], 71), 0)
    ghost_lists = set_ends(jax.random.randint(key_list[4], (2 * N_GX, 2 * N_GY, 2 * N_GZ, GHOSTS), 0, ATOMS_DEV), jax.random.fold_in(key_list[4], 1), 0, ATOMS_DEV - 1).astype(jnp.int32)
    embedding = jnp.clip(jax.random.uniform(key_list[5], (SPECIES, CHANNELS), jnp.float32, 0.5, 1.5), 0.5, 1.5)
    radial_in = scatter_about(key_list[6], (BASIS, RADIAL_HIDDEN), BASIS ** -0.5, 2.0, jnp.float32)
    radial_out = scatter_about(key_list[7], (RADIAL_HIDDEN, CHANNELS), RADIAL_HIDDEN ** -0.5, 0.5, jnp.float32)
    readout = scatter_about(key_list[8], (CHANNELS,), CHANNELS ** -0.5, 0.75, jnp.float32)
    return dict(positions=positions, species=species, start_block=start_block, neighbors=neighbors, ghost_lists=ghost_lists, embedding=embedding, radial_in=radial_in, radial_out=radial_out, readout=readout)


SOFTEN = 0.25
CUTOFF = 4.0
HIGHEST = lax.Precision.HIGHEST

def ghost_layout():
    chosen = []
    moves = []
    octants = []
    for number in range(64):
        coords = (number // 16, number // 4 % 4, number % 4)
        if all((member in (1, 2) for member in coords)):
            continue
        chosen.append(number)
        moves.append([int(member == 3) - int(member == 0) for member in coords])
        octants.append([(member + 1) % 2 for member in coords])
    return (np.array(chosen), np.array(moves), np.array(octants))

def block_energy(atom_table, embed_table, centers, neighbor, radial_in, radial_out, readout):
    fanout = neighbor.shape[0]
    width_block = neighbor.shape[1]
    flat_neighbor = neighbor.reshape(-1)
    center_coords = jnp.take(atom_table, centers, axis=1)
    neighbor_coords = jnp.take(atom_table, flat_neighbor, axis=1).reshape(3, fanout, width_block)
    displace = neighbor_coords - center_coords[:, None, :]
    distance = jnp.sqrt(lax.optimization_barrier(jnp.sum(displace * displace, axis=0)) + SOFTEN)
    direction = displace / distance[None]
    envelope = (1.0 - (distance / CUTOFF) ** 2) ** 2
    orders = jnp.arange(1, radial_in.shape[0] + 1).astype(jnp.float32)
    flat_distance = distance.reshape(-1)
    bessel = jnp.sin(orders[:, None] * (jnp.pi / CUTOFF) * flat_distance[None, :]) / flat_distance[None, :]
    hidden = jax.nn.silu(jnp.dot(radial_in.T, bessel, precision=HIGHEST))
    radial = jnp.dot(radial_out.T, hidden, precision=HIGHEST).reshape(-1, fanout, width_block)
    pairing = jnp.take(embed_table, centers, axis=1)[:, None, :] * jnp.take(embed_table, flat_neighbor, axis=1).reshape(-1, fanout, width_block)
    feature = radial * envelope[None] * pairing
    harmonic = jnp.concatenate([jnp.ones((1, fanout, width_block), jnp.float32), direction], axis=0)
    environ = jnp.einsum('ckb,mkb->cmb', feature, harmonic, precision=HIGHEST) / fanout
    project = jnp.einsum('cmb,mkb->ckb', environ, harmonic, precision=HIGHEST)
    mixed_feature = feature * project
    return jnp.sum(readout[:, None, None] * jax.nn.silu(mixed_feature))

def table_hessian(atom_table, embed_table, centers, neighbor, tangents, radial_in, radial_out, readout):

    def energy(coords):
        return block_energy(coords, embed_table, centers, neighbor, radial_in, radial_out, readout)
    forces = jax.grad(energy)

    def apply_one(tangent):
        return jax.jvp(forces, (atom_table,), (tangent,))[1]
    return jax.vmap(apply_one)(tangents)

def gather_cells(packets, moves, octants):
    pieces = []
    for cell_number in range(moves.shape[0]):
        shift_by = tuple((int(-member) for member in moves[cell_number]))
        rolled = jnp.roll(packets, shift_by, axis=(0, 1, 2))
        first, second, third = (int(member) for member in octants[cell_number])
        pieces.append(rolled[:, :, :, :, first, second, third, :])
    return jnp.stack(pieces, axis=4)

def return_cells(contrib, moves, octants):
    full_shape = contrib.shape
    running = jnp.zeros(full_shape[:4] + (2, 2, 2, full_shape[5]), jnp.float32)
    for cell_number in range(moves.shape[0]):
        shift_by = tuple((int(member) for member in moves[cell_number]))
        shifted = jnp.roll(contrib[:, :, :, :, cell_number], shift_by, axis=(0, 1, 2))
        first, second, third = (int(member) for member in octants[cell_number])
        running = running.at[:, :, :, :, first, second, third, :].add(shifted)
    return running

def reference(positions, species, start_block, neighbors, ghost_lists, embedding, radial_in, radial_out, readout):
    chosen, moves, octants = ghost_layout()
    count_dev = N_GX * N_GY * N_GZ
    atoms_dev = positions.shape[-1]
    ghosts = ghost_lists.shape[-1]
    octant_index_lists = ghost_lists.reshape(N_GX, 2, N_GY, 2, N_GZ, 2, ghosts).transpose(0, 2, 4, 1, 3, 5, 6).reshape(count_dev, 8 * ghosts)

    def pack_octants(values):
        selected = jax.vmap(lambda source_rows, gather_index: jnp.take(source_rows, gather_index, axis=1))(values, octant_index_lists)
        return selected.reshape(N_GX, N_GY, N_GZ, values.shape[1], 2, 2, 2, ghosts)
    flat_coords = positions.reshape(count_dev, 3, atoms_dev)
    flat_species = species.reshape(count_dev, 1, atoms_dev)
    offsets = jnp.asarray(moves.T, jnp.float32)
    ghost_coords = gather_cells(pack_octants(flat_coords), moves, octants) + offsets[None, None, None, :, :, None]
    ghost_species = gather_cells(pack_octants(flat_species), moves, octants)
    atom_tables = jnp.concatenate([flat_coords, ghost_coords.reshape(count_dev, 3, -1)], axis=2)
    species_tables = jnp.concatenate([flat_species[:, 0], ghost_species.reshape(count_dev, -1)], axis=1)
    embed_tables = jnp.swapaxes(jnp.take(embedding, species_tables, axis=0), 1, 2)
    neighbor_dev = neighbors.reshape(count_dev, neighbors.shape[3], atoms_dev)
    centers = jnp.arange(atoms_dev, dtype=jnp.int32)

    def apply_hessian(block):
        flat_block = block.reshape(count_dev, 3 * VECTORS, atoms_dev)
        ghost_tangent = gather_cells(pack_octants(flat_block), moves, octants)
        tangent_tables = jnp.concatenate([flat_block, ghost_tangent.reshape(count_dev, 3 * VECTORS, -1)], axis=2)
        tangent_tables = tangent_tables.reshape(count_dev, VECTORS, 3, -1)

        def one_device(inputs):
            atom_table, embed_table, neighbor, tangents = inputs
            return table_hessian(atom_table, embed_table, centers, neighbor, tangents, radial_in, radial_out, readout)
        images = lax.map(one_device, (atom_tables, embed_tables, neighbor_dev, tangent_tables))
        images = images.reshape(count_dev, 3 * VECTORS, -1)
        local_portion = images[:, :, :atoms_dev]
        ghost_part = images[:, :, atoms_dev:].reshape(N_GX, N_GY, N_GZ, 3 * VECTORS, chosen.shape[0], ghosts)
        octant_partial_sums = return_cells(ghost_part, moves, octants).reshape(count_dev, 3 * VECTORS, 8 * ghosts)
        combined_output = jax.vmap(lambda local_rows, partial_terms, gather_index: local_rows.at[:, gather_index].add(partial_terms))(local_portion, octant_partial_sums, octant_index_lists)
        return combined_output.reshape(count_dev, VECTORS, 3, atoms_dev)
    scale_ip = 1.0 / (3.0 * atoms_dev * count_dev)

    def mean_product(left_block, right_block):
        return jnp.einsum('dkca,dlca->kl', left_block, right_block, precision=HIGHEST) * scale_ip

    def combine(weights, block):
        return jnp.einsum('ij,dica->djca', weights, block, precision=HIGHEST)

    def solve_rows(factor, block):
        matrix = jnp.moveaxis(block, 1, 0).reshape(VECTORS, -1)
        solved = jax.scipy.linalg.solve_triangular(factor, matrix, lower=True)
        return jnp.moveaxis(solved.reshape(VECTORS, count_dev, 3, atoms_dev), 0, 1)
    initial = start_block.reshape(count_dev, VECTORS, 3, atoms_dev)
    factor = jnp.linalg.cholesky(mean_product(initial, initial))
    current = solve_rows(factor, initial)
    previous = jnp.zeros_like(current)
    diagonals = []
    couplings = []
    for step_number in range(PRODUCTS):
        product_block = apply_hessian(current)
        proj_current = mean_product(current, product_block)
        proj_previous = mean_product(previous, product_block)
        residue = product_block - combine(proj_current, current) - combine(proj_previous, previous)
        factor = jnp.linalg.cholesky(mean_product(residue, residue))
        previous, current = (current, solve_rows(factor, residue))
        diagonals.append(proj_current)
        couplings.append(factor.T)
    return (current.reshape(N_GX, N_GY, N_GZ, VECTORS, 3, atoms_dev), jnp.stack(diagonals), jnp.stack(couplings))
```

```python
import functools
import math

import jax
import jax.numpy as jnp
import numpy as np
from jax import lax
from jax.experimental import pallas as pl
from jax.experimental.pallas import tpu as pltpu
from jax.sharding import PartitionSpec as P

AXES = ("gx", "gy", "gz")
SOFTEN = 0.25
CUTOFF = 4.0
F32 = jnp.float32
BF16 = jnp.bfloat16
ATOMS = 256
FAN = 6
CH = 64
HID = 128
NB = 8
COLS = 1152
ROWS = 16
HIGHEST = lax.Precision.HIGHEST
MESH = pl.DeviceIdType.MESH

SF, SF1, SF2, SP, SA, SB, SE = 0, 6, 12, 18, 24, 30, 36


def column_cells():
    lane = np.arange(128)
    octant = lane // 16
    own = np.stack([octant // 4 + 1, octant // 2 % 2 + 1, octant % 2 + 1])

    def shift(block, axis, by):
        block = block.copy()
        block[axis] += by
        return block

    def roll(block, by):
        return np.roll(block, by, axis=1)

    left, right = shift(own, 0, -2), shift(own, 0, 2)
    xs = roll(np.where(lane < 64, right, left), 64)
    bit = (lane // 32) % 2 == 1
    up = np.where(bit, own, roll(xs, -32))
    down = np.where(bit, roll(xs, 32), own)
    yb, ya = shift(up, 1, -2), shift(down, 1, 2)
    bit = (lane // 16) % 2 == 1
    pairs = ((own, xs), (yb, ya))
    up = [np.where(bit, a, roll(b, -16)) for a, b in pairs]
    down = [np.where(bit, roll(b, 16), a) for a, b in pairs]
    zb = [shift(m, 2, -2) for m in up]
    za = [shift(m, 2, 2) for m in down]
    return np.concatenate([xs, yb, ya] + zb + za, axis=1)


def table_constants():
    cells = column_cells()
    order = {}
    for number in range(64):
        m = (number // 16, number // 4 % 4, number % 4)
        if not all(x in (1, 2) for x in m):
            order[m] = len(order)
    rank = np.arange(cells.shape[1]) % 16
    ids = np.array([256 + order[tuple(int(x) for x in cells[:, n])] * 16 for n in range(cells.shape[1])]) + rank
    assert sorted(ids) == list(range(256, COLS))
    ids = np.concatenate([np.arange(256), ids]).astype(np.int32)
    moves = (cells == 3).astype(np.float32) - (cells == 0).astype(np.float32)
    offs = np.zeros((ROWS, COLS), np.float32)
    offs[12:15, 256:] = moves
    ones = np.zeros((32, 192), np.float32)
    for group in range(4):
        for k in range(FAN):
            ones[8 * group + k, (group * FAN + k) * 8 : (group * FAN + k) * 8 + 8] = 1.0
    return ids[:, None], offs, ones


def split3(x):
    high = x.astype(BF16)
    rest = x - high.astype(F32)
    mid = rest.astype(BF16)
    low = (rest - mid.astype(F32)).astype(BF16)
    return high, mid, low


def rows3(x):
    return jnp.concatenate(split3(x), axis=0)


def sum3(y):
    n = y.shape[0] // 3
    return (y[2 * n :] + y[n : 2 * n]) + y[:n]


def mm(a, b, contract=((1,), (0,))):
    return lax.dot_general(a, b, (contract, ((), ())), preferred_element_type=F32)


def mm_high(a, b):
    return jnp.dot(a, b, precision=HIGHEST, preferred_element_type=F32)


def sin_cos(x):
    q = jnp.floor(x * (2.0 / math.pi) + 0.5)
    y = x - q * 1.5703125
    y = y - q * 4.837512969970703125e-4
    y = y - q * 7.549789948768648e-8
    y2 = y * y
    s = y + y * y2 * (-1.6666654611e-1 + y2 * (8.3321608736e-3 - y2 * 1.9515295891e-4))
    c = 1.0 - 0.5 * y2 + y2 * y2 * (4.166664568298827e-2 + y2 * (-1.388731625493765e-3 + y2 * 2.443315711809948e-5))
    h = q - 4.0 * jnp.floor(q * 0.25)
    odd = (h == 1.0) | (h == 3.0)
    ss = jnp.where(odd, c, s)
    cc = jnp.where(odd, s, c)
    ss = jnp.where(h >= 2.0, -ss, ss)
    cc = jnp.where((h == 1.0) | (h == 2.0), -cc, cc)
    return ss, cc


def kernel(
    sizes, pos_ref, spc_ref, sb_ref, nbr_ref, gl_ref, emb_ref, rin_ref, rout_ref, rdo_ref, ids_ref, offs_ref, ones_ref,
    next_ref, diag_ref, off_ref,
    own, inc, tab, vtab, rtab, dt, grs, geo, sums, ub, bv, fs, acc, epv, wpad, rt2, embc, ghost, cb,
    sx, rx, sy, ry, sz, rz, arb, hsend, hrecv, asend, arecv,
):
    me = [lax.axis_index(a) for a in AXES]
    scale_ip = 1.0 / (3.0 * ATOMS * sizes[0] * sizes[1] * sizes[2])
    base = [0, sizes[0], sizes[0] + sizes[1]]

    def wrap(axis, by):
        return {AXES[axis]: lax.rem(me[axis] + by, sizes[axis])}

    barrier = pltpu.get_barrier_semaphore()
    for axis in range(3):
        for d in range(1, sizes[axis]):
            pl.semaphore_signal(barrier, inc=1, device_id=wrap(axis, d), device_id_type=MESH)

    lane = lax.broadcasted_iota(jnp.int32, (1, 128), 1)
    bit64 = (lane % 128) >= 64
    bit32 = (lane % 64) >= 32
    bit16 = (lane % 32) >= 16
    sub8 = lax.broadcasted_iota(jnp.int32, (8, 128), 0)
    lane8 = lax.broadcasted_iota(jnp.int32, (8, 128), 1)

    def roll(x, by):
        return pltpu.roll(x, by % 128, 1)

    pending = []

    def send(i, n, src, dst, axis, by):
        copy = pltpu.make_async_remote_copy(
            src_ref=src, dst_ref=dst, send_sem=hsend.at[i, n], recv_sem=hrecv.at[i, n],
            device_id=wrap(axis, by), device_id_type=MESH,
        )
        copy.start()
        pending.append(copy)
        return copy

    def ar_send(i, axis, tile):
        mine = base[axis] + me[axis]
        arb[i, mine] = tile
        for d in range(1, sizes[axis]):
            copy = pltpu.make_async_remote_copy(
                src_ref=arb.at[i, mine], dst_ref=arb.at[i, mine],
                send_sem=asend.at[i, base[axis] + d], recv_sem=arecv.at[i, mine],
                device_id=wrap(axis, d), device_id_type=MESH,
            )
            copy.start()
            pending.append(copy)

    def ar_recv(i, axis):
        for d in range(1, sizes[axis]):
            src = base[axis] + lax.rem(me[axis] + d, sizes[axis])
            pltpu.make_async_remote_copy(
                src_ref=arb.at[i, src], dst_ref=arb.at[i, src],
                send_sem=asend.at[i, base[axis] + d], recv_sem=arecv.at[i, src],
                device_id=wrap(axis, d), device_id_type=MESH,
            ).wait_recv()
        total = arb[i, base[axis]]
        for j in range(1, sizes[axis]):
            total = total + arb[i, base[axis] + j]
        return total

    def gram_rows(left, right):
        out = jnp.zeros((4, 128), F32)
        for w in range(4):
            prod = left[0:4, :] * right[w : w + 1, :]
            for c in (1, 2):
                prod = prod + left[4 * c : 4 * c + 4, :] * right[4 * c + w : 4 * c + w + 1, :]
            total = jnp.sum(prod, axis=1, keepdims=True) * scale_ip
            out = jnp.where(lane8[:4] == w, total, out)
        return out

    def entries(tile, row):
        out = [[None] * 4 for _ in range(4)]
        for w in range(4):
            col = jnp.broadcast_to(tile[:, w : w + 1], (8, 128))
            for u in range(4):
                out[u][w] = jnp.broadcast_to(col[row + u : row + u + 1, :], (8, 128))
        return out

    def place(vals):
        out = jnp.zeros((8, 128), F32)
        for n, val in enumerate(vals):
            if val is not None:
                out = jnp.where(sub8 == n, val, out)
        return out[0:4, 0:1]

    def matrix(get):
        out = jnp.zeros((8, 128), F32)
        for u in range(4):
            for w in range(4):
                val = get(u, w)
                if val is not None:
                    out = jnp.where((sub8 == u) & (lane8 == w), val, out)
        return out[0:4, 0:4]

    def cholesky(g):
        low = [[None] * 4 for _ in range(4)]
        inv_d = [None] * 4
        for j in range(4):
            total = g[j][j]
            for m in range(j):
                total = total - low[j][m] * low[j][m]
            low[j][j] = jnp.sqrt(total)
            inv_d[j] = 1.0 / low[j][j]
            for u in range(j + 1, 4):
                total = g[u][j]
                for m in range(j):
                    total = total - low[u][m] * low[j][m]
                low[u][j] = total * inv_d[j]
        inv = [[None] * 4 for _ in range(4)]
        for j in range(4):
            inv[j][j] = inv_d[j]
            for u in range(j + 1, 4):
                total = low[u][j] * inv[j][j]
                for m in range(j + 1, u):
                    total = total + low[u][m] * inv[m][j]
                inv[u][j] = -total * inv_d[u]
        return low, inv

    def columns_of(mat):
        return [place([mat[u][w] for u in range(4)]) for w in range(4)]

    def combine(cols, src, c):
        total = cols[0] * src[4 * c : 4 * c + 1, :]
        for w in range(1, 4):
            total = total + cols[w] * src[4 * c + w : 4 * c + w + 1, :]
        return total

    def fwd_x(i, block):
        sx[i] = block
        return (
            send(i, 0, sx.at[i], rx.at[i, 0], 0, 1),
            send(i, 1, sx.at[i], rx.at[i, 1], 0, sizes[0] - 1),
        )

    def fwd_x_done(i, copies):
        for copy in copies:
            copy.wait_recv()
        return roll(jnp.where(bit64, rx[i, 0], rx[i, 1]), 64)

    def fwd_y(i, block, xs):
        sy[i, 0] = jnp.where(bit32, block, roll(xs, -32))
        sy[i, 1] = jnp.where(bit32, roll(xs, 32), block)
        return (
            send(i, 2, sy.at[i, 0], ry.at[i, 0], 1, 1),
            send(i, 3, sy.at[i, 1], ry.at[i, 1], 1, sizes[1] - 1),
        )

    def fwd_y_done(i, copies):
        for copy in copies:
            copy.wait_recv()
        return ry[i, 0], ry[i, 1]

    def fwd_z(i, block, xs, yb, ya):
        for j, (a, b) in enumerate(((block, xs), (yb, ya))):
            sz[i, 0, :, 128 * j : 128 * j + 128] = jnp.where(bit16, a, roll(b, -16))
            sz[i, 1, :, 128 * j : 128 * j + 128] = jnp.where(bit16, roll(b, 16), a)
        return (
            send(i, 4, sz.at[i, 0], rz.at[i, 0], 2, 1),
            send(i, 5, sz.at[i, 1], rz.at[i, 1], 2, sizes[2] - 1),
        )

    def fwd_z_done(i, copies):
        for copy in copies:
            copy.wait_recv()
        return rz[i, 0], rz[i, 1]

    def give_back(i, con):
        sz[i, 0] = con[:, 640:896]
        sz[i, 1] = con[:, 896:1152]
        copies = (
            send(i, 4, sz.at[i, 0], rz.at[i, 1], 2, sizes[2] - 1),
            send(i, 5, sz.at[i, 1], rz.at[i, 0], 2, 1),
        )
        for copy in copies:
            copy.wait_recv()
        a_adj, b_adj = [], []
        for j in range(2):
            mu = rz[i, 1, :, 128 * j : 128 * j + 128]
            md = rz[i, 0, :, 128 * j : 128 * j + 128]
            a_adj.append(jnp.where(bit16, mu, md))
            b_adj.append(jnp.where(bit16, roll(mu, 16), roll(md, -16)))
        sy[i, 0] = con[:, 384:512] + a_adj[1]
        sy[i, 1] = con[:, 512:640] + b_adj[1]
        copies = (
            send(i, 2, sy.at[i, 0], ry.at[i, 1], 1, sizes[1] - 1),
            send(i, 3, sy.at[i, 1], ry.at[i, 0], 1, 1),
        )
        for copy in copies:
            copy.wait_recv()
        mu, md = ry[i, 1], ry[i, 0]
        mine = a_adj[0] + jnp.where(bit32, mu, md)
        sx[i] = con[:, 256:384] + b_adj[0] + jnp.where(bit32, roll(mu, 32), roll(md, -32))
        copies = (
            send(i, 0, sx.at[i], rx.at[i, 1], 0, sizes[0] - 1),
            send(i, 1, sx.at[i], rx.at[i, 0], 0, 1),
        )
        for copy in copies:
            copy.wait_recv()
        mine = mine + roll(jnp.where(bit64, rx[i, 0], rx[i, 1]), 64)
        return con[:, 0:256] + sum3(mm(rows3(mine), ghost[...], ((1,), (1,))))

    def pick(block):
        return sum3(mm(rows3(block), ghost[...]))

    for c in range(3):
        for v in range(4):
            own[4 * c + v : 4 * c + v + 1, :] = sb_ref[v, c : c + 1, :]
    own[12:15, :] = pos_ref[...]
    own[15:16, :] = spc_ref[...].astype(F32)
    atom_rows = lax.broadcasted_iota(jnp.int32, (ATOMS, 128), 0)
    ghost[...] = jnp.where(atom_rows == gl_ref[...], 1.0, 0.0).astype(BF16)
    block = pick(own[...])
    tile = jnp.concatenate([gram_rows(own, own), jnp.zeros((4, 128), F32)], axis=0)

    pl.semaphore_wait(barrier, sum(sizes) - 3)
    copies = fwd_x(0, block)
    ar_send(0, 0, tile)

    atom_lane = lax.broadcasted_iota(jnp.int32, (128, ATOMS), 1)

    def build(j, is_own):
        at = pl.ds(pl.multiple_of(j * 128, 128), 128)
        name = ids_ref[at, :]
        for k in range(FAN):
            part = jnp.where(nbr_ref[k : k + 1, :] == name, 1.0, 0.0)
            if is_own:
                part = part - jnp.where(atom_lane == name, 1.0, 0.0)
            inc[at, ATOMS * k : ATOMS * k + ATOMS] = part.astype(BF16)

    lax.fori_loop(0, 2, lambda j, z: (build(j, True), z)[1], 0)
    wpad[...] = jnp.zeros((2, 128, 128), F32)
    wpad[0, :, 0:CH] = rout_ref[...]
    wpad[1, 0:2, 0:CH] = emb_ref[...]
    wpad[1, 2:3, 0:CH] = rdo_ref[...]
    rt2[...] = wpad[0].T[0:CH, :]
    embc[...] = wpad[1].T[0:CH, :]
    wpad[1, 0:8, :] = rin_ref[...]
    wpad[1] = wpad[1].T

    xs = fwd_x_done(0, copies)
    copies = fwd_y(0, block, xs)
    ar_send(0, 1, ar_recv(0, 0))
    lax.fori_loop(2, 6, lambda j, z: (build(j, False), z)[1], 0)
    yb, ya = fwd_y_done(0, copies)
    copies = fwd_z(0, block, xs, yb, ya)
    ar_send(0, 2, ar_recv(0, 1))
    lax.fori_loop(6, 9, lambda j, z: (build(j, False), z)[1], 0)
    ga = jnp.where(own[15:16, :] < 0.5, embc[:, 0:1], embc[:, 1:2])
    epv[...] = ga
    zb, za = fwd_z_done(0, copies)

    tab[:, 0:256] = own[...]
    for at, part in ((256, xs), (384, yb), (512, ya), (640, zb), (896, za)):
        tab[:, at : at + part.shape[1]] = part + offs_ref[:, at : at + part.shape[1]]

    def gather(src):
        got = sum3(mm(rows3(src), inc[...]))
        for k in range(FAN):
            dt[:, k, :] = got[:, ATOMS * k : ATOMS * k + ATOMS]

    gather(tab[...])

    d3 = [dt[12 + h] for h in range(3)]
    dist2 = d3[0] * d3[0] + d3[1] * d3[1] + d3[2] * d3[2]
    dist = jnp.sqrt(dist2 + SOFTEN)
    inv_r = 1.0 / dist
    unit = [d * inv_r for d in d3]
    for h in range(3):
        geo[h] = unit[h]
    geo[3] = dist
    geo[4] = inv_r
    geo[5] = dt[15] + own[15:16, :]
    for h in range(3):
        for k in range(FAN):
            row = jnp.broadcast_to(unit[h][k : k + 1, :], (8, ATOMS))
            for l in range(2):
                ub[l, h * FAN + k] = row[:, 128 * l : 128 * l + 128]

    def tangents(product):
        for v in range(4):
            dv = [dt[4 * c + v] for c in range(3)]
            rp = geo[0] * dv[0] + geo[1] * dv[1] + geo[2] * dv[2]
            parts = [rp] + [(dv[h] - geo[h] * rp) * geo[4] for h in range(3)]
            for g in range(4):
                for k in range(FAN):
                    row = jnp.broadcast_to(parts[g][k : k + 1, :], (8, ATOMS))
                    for l in range(2):
                        bv[2 * v + l, g * FAN + k] = row[:, 128 * l : 128 * l + 128]

    tangents(0)

    order8 = (lax.broadcasted_iota(jnp.int32, (8, ATOMS), 0) + 1).astype(F32) * (math.pi / CUTOFF)

    def features(k, z):
        at = pl.ds(k, 1)
        r, ir, kind = geo[3, at, :], geo[4, at, :], geo[5, at, :]
        s, c = sin_cos(order8 * r)
        b0 = s * ir
        b1 = (order8 * c - b0) * ir
        b2 = -(order8 * order8) * b0 - 2.0 * b1 * ir
        rin_t = wpad[1, :, 0:8]
        z0, z1, z2 = (mm_high(rin_t, b) for b in (b0, b1, b2))
        sg = 1.0 / (1.0 + jnp.exp(-z0))
        sd = sg * (1.0 - sg)
        s1 = sg + z0 * sd
        s2 = sd * (2.0 + z0 * (1.0 - 2.0 * sg))
        h0 = z0 * sg
        h1 = s1 * z1
        h2 = s2 * z1 * z1 + s1 * z2
        r0, r1, r2 = (mm_high(rt2[...], h) for h in (h0, h1, h2))
        q = r * r * (1.0 / (CUTOFF * CUTOFF))
        sixth = FAN ** -0.5
        e0 = (1.0 - q) * (1.0 - q) * sixth
        e1 = (-4.0 / (CUTOFF * CUTOFF)) * r * (1.0 - q) * sixth
        e2 = (-4.0 / (CUTOFF * CUTOFF)) * (1.0 - 3.0 * q) * sixth
        w = epv[...] * jnp.where(kind < 0.5, embc[:, 0:1], embc[:, 1:2])
        f0 = r0 * e0 * w
        f1 = (r1 * e0 + r0 * e1) * w
        f2 = (r2 * e0 + 2.0 * r1 * e1 + r0 * e2) * w
        for slot, val in ((SF, f0), (SF1, f1), (SF2, f2)):
            for l in range(2):
                for t in range(8):
                    fs[8 * l + t, slot + k] = val[8 * t : 8 * t + 8, 128 * l : 128 * l + 128]
        return z

    lax.fori_loop(0, FAN, features, 0)

    ks = range(FAN)
    hs = range(3)

    def base_pass(i, z):
        l = i // 8
        t = lax.rem(i, 8)
        f = [fs[i, SF + k] for k in ks]
        f1 = [fs[i, SF1 + k] for k in ks]
        u = [[ub[l, h * FAN + k] for k in ks] for h in hs]
        rho = jnp.broadcast_to(embc[pl.ds(pl.multiple_of(t * 8, 8), 8), 2:3], (8, 128))
        e0 = sum(f[1:], f[0])
        e = [sum((f[k] * u[h][k] for k in ks[1:]), f[0] * u[h][0]) for h in hs]
        p, a, n = [], [], []
        for k in ks:
            pk = e0 + (e[0] * u[0][k] + e[1] * u[1][k] + e[2] * u[2][k])
            m = f[k] * pk
            sg = 1.0 / (1.0 + jnp.exp(-m))
            sd = sg * (1.0 - sg)
            ak = rho * (sg + m * sd)
            fs[i, SP + k] = pk
            fs[i, SA + k] = ak
            fs[i, SB + k] = rho * (sd * (2.0 + m * (1.0 - 2.0 * sg)))
            p.append(pk)
            a.append(ak)
            n.append(ak * f[k])
        for h in hs:
            fs[i, SE + h] = e[h]
        q0 = sum(n[1:], n[0])
        q = [sum((n[k] * u[h][k] for k in ks[1:]), n[0] * u[h][0]) for h in hs]
        for k in ks:
            fk = a[k] * p[k] + q0 + (q[0] * u[0][k] + q[1] * u[1][k] + q[2] * u[2][k])
            acc[l, k] += fk * f1[k]
            acc[2 + l, k] += fk * fs[i, SF2 + k]
            for h in hs:
                acc[l, FAN * (h + 1) + k] += n[k] * e[h] + f[k] * q[h]
                acc[2 + l, FAN * (h + 1) + k] += f1[k] * q[h]
        return z

    def clear():
        def zero(i, z):
            acc[i] = jnp.zeros((24, 8, 128), F32)
            return z
        lax.fori_loop(0, 8, zero, 0)

    ones = ones_ref[...].astype(BF16)

    def fold(v):
        out = []
        for l in range(2):
            hi, mid, lo = split3(acc[2 * v + l].reshape(192, 128))
            out.append((mm(ones, lo) + mm(ones, mid)) + mm(ones, hi))
        return jnp.concatenate(out, axis=1)

    clear()
    lax.fori_loop(0, 16, base_pass, 0)
    first, second = fold(0), fold(1)
    alpha, beta = first[0:8], second[0:8]
    force = [first[8 * h + 8 : 8 * h + 16] for h in hs]
    cross = [second[8 * h + 8 : 8 * h + 16] for h in hs]
    uv = unit[0] * force[0] + unit[1] * force[1] + unit[2] * force[2]
    sums[0] = alpha
    sums[1] = beta
    sums[2] = uv
    for h in hs:
        sums[3 + h] = force[h]
        sums[6 + h] = cross[h]

    def hvp(i, z):
        v = i // 16
        ch = lax.rem(i, 16)
        vl = 2 * v + ch // 8
        l = ch // 8
        f = [fs[ch, SF + k] for k in ks]
        rp = [bv[vl, k] for k in ks]
        u = lambda h, k: ub[l, h * FAN + k]
        du = lambda h, k: bv[vl, (h + 1) * FAN + k]
        df = [fs[ch, SF1 + k] * rp[k] for k in ks]
        de0 = sum(df[1:], df[0])
        de = []
        for h in hs:
            total = df[0] * u(h, 0) + f[0] * du(h, 0)
            for k in ks[1:]:
                total = total + (df[k] * u(h, k) + f[k] * du(h, k))
            de.append(total)
        e = [fs[ch, SE + h] for h in hs]
        dn, dfeat, n = [], [], []
        for k in ks:
            dp = de0
            for h in hs:
                dp = dp + (de[h] * u(h, k) + e[h] * du(h, k))
            pk, ak = fs[ch, SP + k], fs[ch, SA + k]
            da = fs[ch, SB + k] * (df[k] * pk + f[k] * dp)
            dn.append(da * f[k] + ak * df[k])
            n.append(ak * f[k])
            dfeat.append(da * pk + ak * dp)
        dq0 = sum(dn[1:], dn[0])
        dq = []
        for h in hs:
            total = dn[0] * u(h, 0) + n[0] * du(h, 0)
            for k in ks[1:]:
                total = total + (dn[k] * u(h, k) + n[k] * du(h, k))
            dq.append(total)
        for k in ks:
            tot = dfeat[k] + dq0 + (dq[0] * u(0, k) + dq[1] * u(1, k) + dq[2] * u(2, k))
            acc[vl, k] += fs[ch, SF1 + k] * tot
            for h in hs:
                acc[vl, FAN * (h + 1) + k] += (dn[k] * e[h] + n[k] * de[h]) + f[k] * dq[h]
        return z

    grs[12:16] = jnp.zeros((4, 8, ATOMS), F32)

    def finish_hvp():
        u3 = [geo[h] for h in hs]
        ir = geo[4]
        for v in range(4):
            got = fold(v)
            dv = [dt[4 * c + v] for c in range(3)]
            rp = u3[0] * dv[0] + u3[1] * dv[1] + u3[2] * dv[2]
            du = [(dv[h] - u3[h] * rp) * ir for h in hs]
            al, be, w0 = sums[0], sums[1], sums[2]
            fo = [sums[3 + h] for h in hs]
            cr = [sums[6 + h] for h in hs]
            dal = got[0:8] + be * rp + (cr[0] * du[0] + cr[1] * du[1] + cr[2] * du[2])
            dfo = [got[8 * h + 8 : 8 * h + 16] + rp * cr[h] for h in hs]
            duv = sum((du[h] * fo[h] + u3[h] * dfo[h] for h in hs[1:]), du[0] * fo[0] + u3[0] * dfo[0])
            back = rp * ir
            for h in hs:
                val = dal * u3[h] + al * du[h]
                val = val + ir * ((dfo[h] - du[h] * w0 - u3[h] * duv) - back * (fo[h] - u3[h] * w0))
                grs[4 * h + v] = val
        for k in ks:
            cb[:, ATOMS * k : ATOMS * k + ATOMS] = rows3(grs[:, k, :])
        return sum3(mm(cb[...], inc[...], ((1,), (1,))))

    clear()
    lax.fori_loop(0, 64, hvp, 0)
    low, inv = cholesky(entries(ar_recv(0, 2), 0))
    cols0 = columns_of(inv)
    for c in range(3):
        vtab[4 * c : 4 * c + 4, :] = combine(cols0, tab, c)
    image = give_back(1, finish_hvp())
    own[...] = image
    for c in range(3):
        rtab[4 * c : 4 * c + 4, 0:256] = combine(cols0, own, c)
    rtab[12:16, :] = jnp.zeros((4, COLS), F32)
    block = pick(rtab[:, 0:256])
    copies = fwd_x(2, block)
    tile = jnp.concatenate([gram_rows(vtab.at[:, 0:256], rtab.at[:, 0:256]), jnp.zeros((4, 128), F32)], axis=0)
    ar_send(1, 0, tile)
    xs = fwd_x_done(2, copies)
    copies = fwd_y(2, block, xs)
    ar_send(1, 1, ar_recv(1, 0))
    yb, ya = fwd_y_done(2, copies)
    copies = fwd_z(2, block, xs, yb, ya)
    ar_send(1, 2, ar_recv(1, 1))
    zb, za = fwd_z_done(2, copies)
    for at, part in ((256, xs), (384, yb), (512, ya), (640, zb), (896, za)):
        rtab[:, at : at + part.shape[1]] = part
    proj = entries(ar_recv(1, 2), 0)
    diag_ref[0] = matrix(lambda u, w: proj[u][w])
    cols = [place([proj[u][w] for w in range(4)]) for u in range(4)]
    for c in range(3):
        rtab[4 * c : 4 * c + 4, :] = rtab[4 * c : 4 * c + 4, :] - combine(cols, vtab, c)
    tile = jnp.concatenate([gram_rows(rtab.at[:, 0:256], rtab.at[:, 0:256]), jnp.zeros((4, 128), F32)], axis=0)
    ar_send(2, 0, tile)

    gather(rtab[...])
    tangents(1)
    clear()
    lax.fori_loop(0, 16, hvp, 0)
    ar_send(2, 1, ar_recv(2, 0))
    lax.fori_loop(16, 32, hvp, 0)
    ar_send(2, 2, ar_recv(2, 1))
    lax.fori_loop(32, 64, hvp, 0)
    low, inv = cholesky(entries(ar_recv(2, 2), 0))
    off_ref[0] = matrix(lambda u, w: low[w][u] if w >= u else None)
    cols1 = columns_of(inv)
    own[...] = give_back(3, finish_hvp())
    for c in range(3):
        tab[4 * c : 4 * c + 4, 0:256] = combine(cols1, rtab.at[:, 0:256], c)
    for c in range(3):
        rtab[4 * c : 4 * c + 4, 0:256] = combine(cols1, own, c)
    image = rtab.at[:, 0:256]
    tile = jnp.concatenate([gram_rows(tab.at[:, 0:256], image), gram_rows(vtab.at[:, 0:256], image)], axis=0)
    for axis in range(3):
        ar_send(3, axis, tile)
        tile = ar_recv(3, axis)
    proj = entries(tile, 0)
    prev = entries(tile, 4)
    cols = [place([proj[u][w] for w in range(4)]) for u in range(4)]
    cols_p = [place([prev[u][w] for w in range(4)]) for u in range(4)]
    for c in range(3):
        own[4 * c : 4 * c + 4, :] = (
            rtab[4 * c : 4 * c + 4, 0:256]
            - combine(cols, tab.at[:, 0:256], c)
            - combine(cols_p, vtab.at[:, 0:256], c)
        )
    tile = jnp.concatenate([gram_rows(own, own), jnp.zeros((4, 128), F32)], axis=0)
    ar_send(4, 0, tile)
    diag_ref[1] = matrix(lambda u, w: proj[u][w])
    tile = ar_recv(4, 0)
    for axis in (1, 2):
        ar_send(4, axis, tile)
        tile = ar_recv(4, axis)
    low, inv = cholesky(entries(tile, 0))
    cols = columns_of(inv)
    for c in range(3):
        last = combine(cols, own, c)
        for v in range(4):
            next_ref[v, c : c + 1, :] = last[v : v + 1, :]
    off_ref[1] = matrix(lambda u, w: low[w][u] if w >= u else None)
    for copy in pending:
        copy.wait_send()


def solution(mesh):
    sizes = tuple(mesh.shape[a] for a in AXES)
    ids, offs, ones = table_constants()
    total = sum(sizes)

    def on_device(positions, species, start_block, neighbors, ghost_lists, embedding, radial_in, radial_out, readout):
        vmem = pl.BlockSpec(memory_space=pltpu.VMEM)
        vm = lambda *shape: pltpu.VMEM(shape, F32)
        out = pl.pallas_call(
            functools.partial(kernel, sizes),
            out_shape=(
                jax.ShapeDtypeStruct((4, 3, ATOMS), F32),
                jax.ShapeDtypeStruct((2, 4, 4), F32),
                jax.ShapeDtypeStruct((2, 4, 4), F32),
            ),
            in_specs=[vmem] * 12,
            out_specs=(vmem, vmem, vmem),
            scratch_shapes=[
                vm(ROWS, ATOMS),
                pltpu.VMEM((COLS, FAN * ATOMS), BF16),
                vm(ROWS, COLS), vm(ROWS, COLS), vm(ROWS, COLS),
                vm(ROWS, 8, ATOMS), vm(ROWS, 8, ATOMS),
                vm(6, 8, ATOMS), vm(9, 8, ATOMS),
                vm(2, 18, 8, 128), vm(8, 24, 8, 128),
                vm(16, 39, 8, 128), vm(8, 24, 8, 128),
                vm(CH, ATOMS), vm(2, 128, 128), vm(CH, 128), vm(CH, 128),
                pltpu.VMEM((ATOMS, 128), BF16),
                pltpu.VMEM((3 * ROWS, FAN * ATOMS), BF16),
                vm(4, ROWS, 128), vm(4, 2, ROWS, 128),
                vm(4, 2, ROWS, 128), vm(4, 2, ROWS, 128),
                vm(4, 2, ROWS, 256), vm(4, 2, ROWS, 256),
                vm(5, total, 8, 128),
                pltpu.SemaphoreType.DMA((4, 6)), pltpu.SemaphoreType.DMA((4, 6)),
                pltpu.SemaphoreType.DMA((5, total)), pltpu.SemaphoreType.DMA((5, total)),
            ],
            compiler_params=pltpu.CompilerParams(
                collective_id=0, has_side_effects=True, vmem_limit_bytes=48 * 1024 * 1024
            ),
        )(
            positions[0, 0, 0], species[0, 0, 0][None], start_block[0, 0, 0], neighbors[0, 0, 0],
            ghost_lists.reshape(1, 128), embedding, radial_in, radial_out, readout[None],
            jnp.asarray(ids), jnp.asarray(offs), jnp.asarray(ones),
        )
        return out[0][None, None, None], out[1], out[2]

    return jax.shard_map(
        on_device,
        mesh=mesh,
        in_specs=(
            P("gx", "gy", "gz", None, None),
            P("gx", "gy", "gz", None),
            P("gx", "gy", "gz", None, None, None),
            P("gx", "gy", "gz", None, None),
            P("gx", "gy", "gz", None),
            P(), P(), P(), P(),
        ),
        out_specs=(P("gx", "gy", "gz", None, None, None), P(), P()),
        check_vma=False,
    )
```

```python
import functools
import itertools
import math

import jax
import jax.numpy as jnp
import numpy as np
from jax import lax
from jax.experimental import pallas as pl
from jax.experimental.pallas import tpu as pltpu
from jax.sharding import PartitionSpec as P

AXES = ("gx", "gy", "gz")
SOFTEN = 0.25
CUTOFF = 4.0
F32 = jnp.float32
BF16 = jnp.bfloat16
ATOMS = 256
FAN = 6
CH = 64
HID = 128
NB = 8
COLS = 1152
ROWS = 16
HIGHEST = lax.Precision.HIGHEST
MESH = pl.DeviceIdType.MESH

SF, SF1, SF2, SP, SA, SB, SE = 0, 6, 12, 18, 24, 30, 36


def neighbour_cells():
    shifts = [s for s in itertools.product((-1, 0, 1), repeat=3) if any(s)]
    shifts.sort(key=lambda s: sum(map(abs, s)))
    out, first = [], 0
    for s in shifts:
        octants = list(itertools.product(*[{1: (0,), -1: (1,), 0: (0, 1)}[x] for x in s]))
        out.append((s, first, octants))
        first += len(octants)
    return out


CELLS = neighbour_cells()
GHOST = 56


def constants():
    order = {}
    for number in range(64):
        m = (number // 16, number // 4 % 4, number % 4)
        if not all(x in (1, 2) for x in m):
            order[m] = len(order)
    out = np.zeros((32, 128), np.float32)
    ids = list(range(256))
    moves = []
    octant_of = []
    for s, _, octants in CELLS:
        for o in octants:
            m = tuple(2 * x + y + 1 for x, y in zip(s, o))
            ids += [256 + 16 * order[m] + r for r in range(16)]
            moves += [s] * 16
            octant_of.append(4 * o[0] + 2 * o[1] + o[2])
    assert sorted(ids) == list(range(COLS))
    out[0:9] = np.array(ids).reshape(9, 128)
    out[9] = -1.0
    out[9, :GHOST] = octant_of
    out[10:31] = np.array(moves).T.reshape(21, 128)
    return out


def split3(x):
    high = x.astype(BF16)
    rest = x - high.astype(F32)
    mid = rest.astype(BF16)
    low = (rest - mid.astype(F32)).astype(BF16)
    return high, mid, low


def rows3(x):
    return jnp.concatenate(split3(x), axis=0)


def sum3(y):
    n = y.shape[0] // 3
    return (y[2 * n :] + y[n : 2 * n]) + y[:n]


def mm(a, b, contract=((1,), (0,))):
    return lax.dot_general(a, b, (contract, ((), ())), preferred_element_type=F32)


def mm_high(a, b):
    return jnp.dot(a, b, precision=HIGHEST, preferred_element_type=F32)


def sin_cos(x):
    q = jnp.floor(x * (2.0 / math.pi) + 0.5)
    y = x - q * 1.5703125
    y = y - q * 4.837512969970703125e-4
    y = y - q * 7.549789948768648e-8
    y2 = y * y
    s = y + y * y2 * (-1.6666654611e-1 + y2 * (8.3321608736e-3 - y2 * 1.9515295891e-4))
    c = 1.0 - 0.5 * y2 + y2 * y2 * (4.166664568298827e-2 + y2 * (-1.388731625493765e-3 + y2 * 2.443315711809948e-5))
    h = q - 4.0 * jnp.floor(q * 0.25)
    odd = (h == 1.0) | (h == 3.0)
    ss = jnp.where(odd, c, s)
    cc = jnp.where(odd, s, c)
    ss = jnp.where(h >= 2.0, -ss, ss)
    cc = jnp.where((h == 1.0) | (h == 2.0), -cc, cc)
    return ss, cc


def kernel(
    sizes, pos_ref, spc_ref, sb_ref, nbr_ref, gl_ref, emb_ref, rin_ref, rout_ref, rdo_ref, cst_ref,
    next_ref, diag_ref, off_ref,
    own, inc, tab, v1, w1, r1, v2, dt, grs, geo, sums, ub, bv, fs, acc, epv, wpad, w2, embc, ghost, glw, cb,
    hs_buf, hr_buf, arb, hsend, hrecv, asend, arecv,
):
    gx, gy, gz = (lax.axis_index(a) for a in AXES)
    scale_ip = 1.0 / (3.0 * ATOMS * sizes[0] * sizes[1] * sizes[2])

    def beside(s):
        return {
            a: lax.rem(i + (x + n), n) for a, i, x, n in zip(AXES, (gx, gy, gz), s, sizes) if x
        }

    nx, ny, nz = sizes[0] // 2, sizes[1], sizes[2] // 2
    groups = (
        [o for o in itertools.product(range(nx), range(2), (0,), (0,), range(2)) if any(o)],
        [o for o in itertools.product((0,), (0,), range(ny), range(nz), (0,)) if any(o)],
    )
    starts = (0, len(groups[0]) + 1)

    def partner(o):
        a = lax.rem(gx // 2 + o[0], nx)
        b = lax.rem(lax.rem(gx, 2) + o[1], 2)
        c = lax.rem(gy + o[2], ny)
        d = lax.rem(gz // 2 + o[3], nz)
        e = lax.rem(lax.rem(gz, 2) + o[4], 2)
        return {"gx": 2 * a + b, "gy": c, "gz": 2 * d + e}, (4 * a + 2 * b + e, nz * c + d)

    barrier = pltpu.get_barrier_semaphore()
    for s, _, _ in CELLS:
        pl.semaphore_signal(barrier, inc=1, device_id=beside(s), device_id_type=MESH)
    for group in groups:
        for o in group:
            pl.semaphore_signal(barrier, inc=1, device_id=partner(o)[0], device_id_type=MESH)

    lane8 = lax.broadcasted_iota(jnp.int32, (8, 128), 1)
    sub8 = lax.broadcasted_iota(jnp.int32, (8, 128), 0)

    pending = []

    def ar_send(i, g, tile):
        mine = starts[g] + partner((0,) * 5)[1][g]
        arb[i, mine] = tile
        for n, o in enumerate(groups[g]):
            copy = pltpu.make_async_remote_copy(
                src_ref=arb.at[i, mine], dst_ref=arb.at[i, mine],
                send_sem=asend.at[i, starts[g] + n], recv_sem=arecv.at[i, mine],
                device_id=partner(o)[0], device_id_type=MESH,
            )
            copy.start()
            pending.append(copy)

    def ar_recv(i, g):
        for n, o in enumerate(groups[g]):
            device, at = partner(o)
            src = starts[g] + at[g]
            pltpu.make_async_remote_copy(
                src_ref=arb.at[i, src], dst_ref=arb.at[i, src],
                send_sem=asend.at[i, starts[g] + n], recv_sem=arecv.at[i, src],
                device_id=device, device_id_type=MESH,
            ).wait_recv()
        parts = [arb[i, starts[g] + j] for j in range(len(groups[g]) + 1)]
        while len(parts) > 1:
            parts = [a + b for a, b in zip(parts[::2], parts[1::2])] + parts[len(parts) // 2 * 2 :]
        return parts[0]

    def halo_send(i, sign):
        copies = []
        for n, (s, first, octants) in enumerate(CELLS):
            at = pl.ds(first, len(octants))
            copy = pltpu.make_async_remote_copy(
                src_ref=hs_buf.at[i, at], dst_ref=hr_buf.at[i, at],
                send_sem=hsend.at[i, n], recv_sem=hrecv.at[i, n],
                device_id=beside(tuple(sign * x for x in s)), device_id_type=MESH,
            )
            copy.start()
            copies.append(copy)
        pending.extend(copies)
        return copies

    def halo_wait(copies):
        for copy in copies:
            copy.wait_recv()

    def turn(x):
        for b in (2, 1, 0):
            by = 1 << b
            sbit = (sub8 & by) != 0
            lbit = (lane8 & (16 * by)) != 0
            low = pltpu.roll(pltpu.roll(x, by, 0), 128 - 16 * by, 1)
            high = low if b == 2 else pltpu.roll(pltpu.roll(x, 8 - by, 0), 16 * by, 1)
            x = jnp.where(sbit == lbit, x, jnp.where(sbit, low, high))
        return x

    def pack(i, src):
        got = sum3(mm(rows3(src), ghost[...]))
        flat = jnp.concatenate([turn(got[0:8]), turn(got[8:16])], axis=1)
        hs_buf[i] = mm(spread, rows3(flat))

    def unpack(i, dst, shifted):
        for j in range(7):
            at = pl.ds(256 + 128 * j, 128)
            for t in range(2):
                part = turn(hr_buf[i, 8 * j : 8 * j + 8, 128 * t : 128 * t + 128])
                if t == 1 and shifted:
                    rows = [jnp.zeros((4, 128), F32)] + [cst_ref[10 + 7 * h + j : 11 + 7 * h + j, :] for h in range(3)]
                    part = part + jnp.concatenate(rows + [jnp.zeros((1, 128), F32)], axis=0)
                dst[8 * t : 8 * t + 8, at] = part

    def pack_back(i, con):
        for j in range(7):
            for t in range(2):
                part = con[8 * t : 8 * t + 8, 128 * j : 128 * j + 128]
                hs_buf[i, 8 * j : 8 * j + 8, 128 * t : 128 * t + 128] = turn(part)

    def unpack_back(i):
        hi, mid, lo = split3(hr_buf[i])
        flat = (mm(collect, lo) + mm(collect, mid)) + mm(collect, hi)
        both = jnp.concatenate([turn(flat[:, 0:128]), turn(flat[:, 128:256])], axis=0)
        return sum3(mm(rows3(both), ghost[...], ((1,), (1,))))

    def gram_rows(left, right):
        out = jnp.zeros((4, 128), F32)
        for w in range(4):
            prod = left[0:4, :] * right[w : w + 1, :]
            for c in (1, 2):
                prod = prod + left[4 * c : 4 * c + 4, :] * right[4 * c + w : 4 * c + w + 1, :]
            total = jnp.sum(prod, axis=1, keepdims=True) * scale_ip
            out = jnp.where(lane8[:4] == w, total, out)
        return out

    def entries(tile, row):
        out = [[None] * 4 for _ in range(4)]
        for w in range(4):
            col = jnp.broadcast_to(tile[:, w : w + 1], (8, 128))
            for u in range(4):
                out[u][w] = jnp.broadcast_to(col[row + u : row + u + 1, :], (8, 128))
        return out

    def place(vals):
        out = jnp.zeros((8, 128), F32)
        for n, val in enumerate(vals):
            if val is not None:
                out = jnp.where(sub8 == n, val, out)
        return out[0:4, 0:1]

    def matrix(get):
        out = jnp.zeros((8, 128), F32)
        for u in range(4):
            for w in range(4):
                val = get(u, w)
                if val is not None:
                    out = jnp.where((sub8 == u) & (lane8 == w), val, out)
        return out[0:4, 0:4]

    def cholesky(g):
        low = [[None] * 4 for _ in range(4)]
        inv_d = [None] * 4
        for j in range(4):
            total = g[j][j]
            for m in range(j):
                total = total - low[j][m] * low[j][m]
            low[j][j] = jnp.sqrt(total)
            inv_d[j] = 1.0 / low[j][j]
            for u in range(j + 1, 4):
                total = g[u][j]
                for m in range(j):
                    total = total - low[u][m] * low[j][m]
                low[u][j] = total * inv_d[j]
        inv = [[None] * 4 for _ in range(4)]
        for j in range(4):
            inv[j][j] = inv_d[j]
            for u in range(j + 1, 4):
                total = low[u][j] * inv[j][j]
                for m in range(j + 1, u):
                    total = total + low[u][m] * inv[m][j]
                inv[u][j] = -total * inv_d[u]
        return low, inv

    def columns_of(mat):
        return [place([mat[u][w] for u in range(4)]) for w in range(4)]

    def combine(cols, src, c):
        total = cols[0] * src[4 * c : 4 * c + 1, :]
        for w in range(1, 4):
            total = total + cols[w] * src[4 * c + w : 4 * c + w + 1, :]
        return total

    for c in range(3):
        own[4 * c : 4 * c + 4, :] = sb_ref[c]
        own[12 + c : 13 + c, :] = pos_ref[c]
    own[15:16, :] = spc_ref[...].astype(F32)
    glw[...] = jnp.zeros((8, 128), jnp.int32)
    for n in range(8):
        glw[n : n + 1, 0:16] = gl_ref[n // 4, n // 2 % 2, n % 2 : n % 2 + 1, :]
    names = glw[0:1, :]
    for n in range(1, 8):
        names = names + pltpu.roll(glw[n : n + 1, :], 16 * n, 1)
    atom_rows = lax.broadcasted_iota(jnp.int32, (ATOMS, 128), 0)
    ghost[...] = jnp.where(atom_rows == names, 1.0, 0.0).astype(BF16)
    wpad[1] = jnp.zeros((128, 128), F32)
    wpad[1, 0:32, :] = cst_ref[...]
    wpad[1] = wpad[1].T
    octant_col = wpad[1, 0:GHOST, 9:10]
    lane24 = lax.rem(lax.broadcasted_iota(jnp.int32, (GHOST, 24), 1), 8).astype(F32)
    spread = jnp.where(lane24 == octant_col, 1.0, 0.0).astype(BF16)
    collect = jnp.where(sub8.astype(F32) == cst_ref[9:10, :], 1.0, 0.0).astype(BF16)[:, 0:GHOST]
    pack(0, own[...])
    zeros4 = jnp.zeros((4, 128), F32)
    tile = jnp.concatenate([gram_rows(own, own), zeros4], axis=0)

    pl.semaphore_wait(barrier, len(CELLS) + len(groups[0]) + len(groups[1]))
    copies = halo_send(0, -1)
    ar_send(0, 0, tile)

    atom_lane = lax.broadcasted_iota(jnp.int32, (128, ATOMS), 1).astype(F32)

    def build(j, is_own):
        name = wpad[1, :, j : j + 1]
        for k in range(FAN):
            part = jnp.where(nbr_ref[k].astype(F32) == name, 1.0, 0.0)
            if is_own:
                part = part - jnp.where(atom_lane == name, 1.0, 0.0)
            inc[128 * j : 128 * j + 128, ATOMS * k : ATOMS * k + ATOMS] = part.astype(BF16)

    wpad[0] = jnp.zeros((128, 128), F32)
    hi, mid, lo = (x.astype(F32) for x in split3(rin_ref[...]))
    for n, part in enumerate((hi, mid, lo, hi, mid, hi)):
        wpad[0, 8 * n : 8 * n + 8, :] = part
    wpad[0, 48:50, 0:CH] = emb_ref[...]
    wpad[0, 50:51, 0:CH] = rdo_ref[...]
    wpad[0] = wpad[0].T
    embc[:, 0:3] = wpad[0, 0:CH, 48:51]
    hi, mid, lo = split3(rout_ref[...])
    w2[...] = jnp.concatenate([hi, mid, hi], axis=1)
    epv[...] = jnp.where(own[15:16, :] < 0.5, embc[:, 0:1], embc[:, 1:2])
    for j in range(9):
        build(j, j < 2)
    ar_send(0, 1, ar_recv(0, 0))
    tab[:, 0:256] = own[...]
    halo_wait(copies)
    unpack(0, tab, True)

    def gather(src):
        got = sum3(mm(rows3(src), inc[...]))
        for k in range(FAN):
            dt[:, k, :] = got[:, ATOMS * k : ATOMS * k + ATOMS]

    gather(tab[...])

    d3 = [dt[12 + h] for h in range(3)]
    dist2 = d3[0] * d3[0] + d3[1] * d3[1] + d3[2] * d3[2]
    dist = jnp.sqrt(dist2 + SOFTEN)
    inv_r = 1.0 / dist
    unit = [d * inv_r for d in d3]
    for h in range(3):
        geo[h] = unit[h]
    geo[3] = dist
    geo[4] = inv_r
    geo[5] = dt[15] + own[15:16, :]
    for h in range(3):
        for k in range(FAN):
            row = jnp.broadcast_to(unit[h][k : k + 1, :], (8, ATOMS))
            for l in range(2):
                ub[l, h * FAN + k] = row[:, 128 * l : 128 * l + 128]

    def tangents(product):
        for v in range(4):
            dv = [dt[4 * c + v] for c in range(3)]
            rp = geo[0] * dv[0] + geo[1] * dv[1] + geo[2] * dv[2]
            parts = [rp] + [(dv[h] - geo[h] * rp) * geo[4] for h in range(3)]
            for g in range(4):
                for k in range(FAN):
                    row = jnp.broadcast_to(parts[g][k : k + 1, :], (8, ATOMS))
                    for l in range(2):
                        bv[2 * v + l, g * FAN + k] = row[:, 128 * l : 128 * l + 128]

    tangents(0)

    order8 = (lax.broadcasted_iota(jnp.int32, (8, ATOMS), 0) + 1).astype(F32) * (math.pi / CUTOFF)

    PAIR = 2
    order_w = jnp.concatenate([order8] * PAIR, axis=1)

    def features(pair, z):
        rows = [[geo[n, pl.ds(PAIR * pair + m, 1), :] for m in range(PAIR)] for n in (3, 4, 5)]
        r, ir, kind = (jnp.concatenate(x, axis=1) for x in rows)
        s, c = sin_cos(order_w * r)
        b0 = s * ir
        b1 = (order_w * c - b0) * ir
        b2 = -(order_w * order_w) * b0 - 2.0 * b1 * ir
        rin_t = wpad[0, :, 0:48].astype(BF16)

        def first(b):
            hi, mid, lo = split3(b)
            return mm(rin_t, jnp.concatenate([hi, hi, hi, mid, mid, lo], axis=0))

        def second(h):
            hi = h.astype(BF16)
            mid = (h - hi.astype(F32)).astype(BF16)
            return mm(w2[...], jnp.concatenate([hi, hi, mid], axis=0))

        z0, z1, z2 = first(b0), first(b1), first(b2)
        sg = 1.0 / (1.0 + jnp.exp(-z0))
        sd = sg * (1.0 - sg)
        s1 = sg + z0 * sd
        s2 = sd * (2.0 + z0 * (1.0 - 2.0 * sg))
        r0, r1_, r2 = second(z0 * sg), second(s1 * z1), second(s2 * z1 * z1 + s1 * z2)
        q = r * r * (1.0 / (CUTOFF * CUTOFF))
        sixth = FAN ** -0.5
        e0 = (1.0 - q) * (1.0 - q) * sixth
        e1 = (-4.0 / (CUTOFF * CUTOFF)) * r * (1.0 - q) * sixth
        e2 = (-4.0 / (CUTOFF * CUTOFF)) * (1.0 - 3.0 * q) * sixth
        w = jnp.concatenate([epv[...]] * PAIR, axis=1) * jnp.where(kind < 0.5, embc[:, 0:1], embc[:, 1:2])
        f0 = r0 * e0 * w
        f1 = (r1_ * e0 + r0 * e1) * w
        f2 = (r2 * e0 + 2.0 * r1_ * e1 + r0 * e2) * w
        for slot, val in ((SF, f0), (SF1, f1), (SF2, f2)):
            for m in range(PAIR):
                for l in range(2):
                    for t in range(8):
                        at = ATOMS * m + 128 * l
                        fs[8 * l + t, slot + PAIR * pair + m] = val[8 * t : 8 * t + 8, at : at + 128]
        return z

    lax.fori_loop(0, FAN // PAIR, features, 0)

    ks = range(FAN)
    hs = range(3)

    def base_pass(i, z):
        l = i // 8
        t = lax.rem(i, 8)
        f = [fs[i, SF + k] for k in ks]
        f1 = [fs[i, SF1 + k] for k in ks]
        u = [[ub[l, h * FAN + k] for k in ks] for h in hs]
        rho = jnp.broadcast_to(embc[pl.ds(pl.multiple_of(t * 8, 8), 8), 2:3], (8, 128))
        e0 = sum(f[1:], f[0])
        e = [sum((f[k] * u[h][k] for k in ks[1:]), f[0] * u[h][0]) for h in hs]
        p, a, n = [], [], []
        for k in ks:
            pk = e0 + (e[0] * u[0][k] + e[1] * u[1][k] + e[2] * u[2][k])
            m = f[k] * pk
            sg = 1.0 / (1.0 + jnp.exp(-m))
            sd = sg * (1.0 - sg)
            ak = rho * (sg + m * sd)
            fs[i, SP + k] = pk
            fs[i, SA + k] = ak
            fs[i, SB + k] = rho * (sd * (2.0 + m * (1.0 - 2.0 * sg)))
            p.append(pk)
            a.append(ak)
            n.append(ak * f[k])
        for h in hs:
            fs[i, SE + h] = e[h]
        q0 = sum(n[1:], n[0])
        q = [sum((n[k] * u[h][k] for k in ks[1:]), n[0] * u[h][0]) for h in hs]
        for k in ks:
            fk = a[k] * p[k] + q0 + (q[0] * u[0][k] + q[1] * u[1][k] + q[2] * u[2][k])
            acc[l, k] += fk * f1[k]
            acc[2 + l, k] += fk * fs[i, SF2 + k]
            for h in hs:
                acc[l, FAN * (h + 1) + k] += n[k] * e[h] + f[k] * q[h]
                acc[2 + l, FAN * (h + 1) + k] += f1[k] * q[h]
        return z

    def clear():
        def zero(i, z):
            acc[i] = jnp.zeros((24, 8, 128), F32)
            return z
        lax.fori_loop(0, 8, zero, 0)

    one_row = lax.broadcasted_iota(jnp.int32, (32, 192), 0)
    one_col = lax.broadcasted_iota(jnp.int32, (32, 192), 1) // 8
    ones = jnp.where((one_row % 8 < FAN) & (one_row // 8 * FAN + one_row % 8 == one_col), 1.0, 0.0).astype(BF16)

    def fold(v):
        out = []
        for l in range(2):
            hi, mid, lo = split3(acc[2 * v + l].reshape(192, 128))
            out.append((mm(ones, lo) + mm(ones, mid)) + mm(ones, hi))
        return jnp.concatenate(out, axis=1)

    clear()
    lax.fori_loop(0, 16, base_pass, 0)
    first, second = fold(0), fold(1)
    alpha, beta = first[0:8], second[0:8]
    force = [first[8 * h + 8 : 8 * h + 16] for h in hs]
    cross = [second[8 * h + 8 : 8 * h + 16] for h in hs]
    uv = unit[0] * force[0] + unit[1] * force[1] + unit[2] * force[2]
    sums[0] = alpha
    sums[1] = beta
    sums[2] = uv
    for h in hs:
        sums[3 + h] = force[h]
        sums[6 + h] = cross[h]

    def hvp(i, z):
        v = i // 16
        ch = lax.rem(i, 16)
        vl = 2 * v + ch // 8
        l = ch // 8
        f = [fs[ch, SF + k] for k in ks]
        rp = [bv[vl, k] for k in ks]
        u = lambda h, k: ub[l, h * FAN + k]
        du = lambda h, k: bv[vl, (h + 1) * FAN + k]
        df = [fs[ch, SF1 + k] * rp[k] for k in ks]
        de0 = sum(df[1:], df[0])
        de = []
        for h in hs:
            total = df[0] * u(h, 0) + f[0] * du(h, 0)
            for k in ks[1:]:
                total = total + (df[k] * u(h, k) + f[k] * du(h, k))
            de.append(total)
        e = [fs[ch, SE + h] for h in hs]
        dn, dfeat, n = [], [], []
        for k in ks:
            dp = de0
            for h in hs:
                dp = dp + (de[h] * u(h, k) + e[h] * du(h, k))
            pk, ak = fs[ch, SP + k], fs[ch, SA + k]
            da = fs[ch, SB + k] * (df[k] * pk + f[k] * dp)
            dn.append(da * f[k] + ak * df[k])
            n.append(ak * f[k])
            dfeat.append(da * pk + ak * dp)
        dq0 = sum(dn[1:], dn[0])
        dq = []
        for h in hs:
            total = dn[0] * u(h, 0) + n[0] * du(h, 0)
            for k in ks[1:]:
                total = total + (dn[k] * u(h, k) + n[k] * du(h, k))
            dq.append(total)
        for k in ks:
            tot = dfeat[k] + dq0 + (dq[0] * u(0, k) + dq[1] * u(1, k) + dq[2] * u(2, k))
            acc[vl, k] += fs[ch, SF1 + k] * tot
            for h in hs:
                acc[vl, FAN * (h + 1) + k] += (dn[k] * e[h] + n[k] * de[h]) + f[k] * dq[h]
        return z

    grs[12:16] = jnp.zeros((4, 8, ATOMS), F32)

    def finish_hvp():
        u3 = [geo[h] for h in hs]
        ir = geo[4]
        for v in range(4):
            got = fold(v)
            dv = [dt[4 * c + v] for c in range(3)]
            rp = u3[0] * dv[0] + u3[1] * dv[1] + u3[2] * dv[2]
            du = [(dv[h] - u3[h] * rp) * ir for h in hs]
            al, be, w0 = sums[0], sums[1], sums[2]
            fo = [sums[3 + h] for h in hs]
            cr = [sums[6 + h] for h in hs]
            dal = got[0:8] + be * rp + (cr[0] * du[0] + cr[1] * du[1] + cr[2] * du[2])
            dfo = [got[8 * h + 8 : 8 * h + 16] + rp * cr[h] for h in hs]
            duv = sum((du[h] * fo[h] + u3[h] * dfo[h] for h in hs[1:]), du[0] * fo[0] + u3[0] * dfo[0])
            back = rp * ir
            for h in hs:
                val = dal * u3[h] + al * du[h]
                val = val + ir * ((dfo[h] - du[h] * w0 - u3[h] * duv) - back * (fo[h] - u3[h] * w0))
                grs[4 * h + v] = val
        for k in ks:
            cb[:, ATOMS * k : ATOMS * k + ATOMS] = rows3(grs[:, k, :])

    def scatter(at):
        return sum3(mm(cb[...], inc[at, :], ((1,), (1,))))

    def give_back(i):
        finish_hvp()
        pack_back(i, scatter(pl.ds(256, COLS - 256)))
        copies = halo_send(i, 1)
        return copies, scatter(pl.ds(0, 256))

    def combine_all(dst, cols, src, minus=None):
        for c in range(3):
            got = combine(cols, src, c)
            dst[4 * c : 4 * c + 4, :] = got if minus is None else minus[4 * c : 4 * c + 4, :] - got

    def transposed(proj):
        return [place([proj[u][w] for w in range(4)]) for u in range(4)]

    clear()
    lax.fori_loop(0, 64, hvp, 0)
    low, inv = cholesky(entries(ar_recv(0, 1), 0))
    cols0 = columns_of(inv)
    copies, local = give_back(1)
    combine_all(v1, cols0, own)
    w1[12:16, :] = jnp.zeros((4, ATOMS), F32)
    halo_wait(copies)
    own[...] = local + unpack_back(1)
    combine_all(w1, cols0, own)
    pack(2, w1[...])
    copies = halo_send(2, -1)
    ar_send(1, 0, jnp.concatenate([gram_rows(v1, w1), zeros4], axis=0))
    tab[:, 0:256] = w1[...]
    clear()
    ar_send(1, 1, ar_recv(1, 0))
    halo_wait(copies)
    unpack(2, tab, False)

    gather(tab[...])
    tangents(1)
    lax.fori_loop(0, 16, hvp, 0)
    proj = entries(ar_recv(1, 1), 0)
    cols_a = transposed(proj)
    combine_all(r1, cols_a, v1, w1)
    ar_send(2, 0, jnp.concatenate([gram_rows(r1, r1), zeros4], axis=0))
    diag_ref[0] = matrix(lambda u, w: proj[u][w])
    lax.fori_loop(16, 64, hvp, 0)
    ar_send(2, 1, ar_recv(2, 0))
    copies, local = give_back(3)
    low, inv = cholesky(entries(ar_recv(2, 1), 0))
    cols1 = columns_of(inv)
    off_ref[0] = matrix(lambda u, w: low[w][u] if w >= u else None)
    combine_all(v2, cols1, r1)
    halo_wait(copies)
    own[...] = local + unpack_back(3)
    combine_all(r1, cols_a, w1, own)
    combine_all(own, cols1, r1)
    gram_w = pltpu.roll(jnp.concatenate([gram_rows(own, own), zeros4], axis=0), 4, 1)
    tile = jnp.concatenate([gram_rows(v2, own), gram_rows(v1, own)], axis=0) + gram_w
    for g in range(2):
        ar_send(3, g, tile)
        tile = ar_recv(3, g)
    proj = entries(tile, 0)
    prev = entries(tile, 4)
    gram = entries(pltpu.roll(tile, 124, 1), 0)
    for u in range(4):
        for w in range(u + 1):
            total = gram[u][w]
            for m in range(4):
                total = total - (proj[m][u] * proj[m][w] + prev[m][u] * prev[m][w])
            gram[u][w] = total
    combine_all(r1, transposed(proj), v2, own)
    combine_all(own, transposed(prev), v1, r1)
    low, inv = cholesky(gram)
    cols = columns_of(inv)
    for c in range(3):
        next_ref[c] = combine(cols, own, c)
    diag_ref[1] = matrix(lambda u, w: proj[u][w])
    off_ref[1] = matrix(lambda u, w: low[w][u] if w >= u else None)
    for copy in pending:
        copy.wait_send()


def solution(mesh):
    sizes = tuple(mesh.shape[a] for a in AXES)
    cst = constants()
    slots = 2 * sizes[0] + sizes[1] * sizes[2] // 2

    def on_device(positions, species, start_block, neighbors, ghost_lists, embedding, radial_in, radial_out, readout):
        vmem = pl.BlockSpec(memory_space=pltpu.VMEM)
        vm = lambda *shape: pltpu.VMEM(shape, F32)
        dma = lambda *shape: pltpu.SemaphoreType.DMA(shape)
        out = pl.pallas_call(
            functools.partial(kernel, sizes),
            out_shape=(
                jax.ShapeDtypeStruct((3, 4, ATOMS), F32),
                jax.ShapeDtypeStruct((2, 4, 4), F32),
                jax.ShapeDtypeStruct((2, 4, 4), F32),
            ),
            in_specs=[vmem] * 10,
            out_specs=(vmem, vmem, vmem),
            scratch_shapes=[
                vm(ROWS, ATOMS),
                pltpu.VMEM((COLS, FAN * ATOMS), BF16),
                vm(ROWS, COLS),
                vm(ROWS, ATOMS), vm(ROWS, ATOMS), vm(ROWS, ATOMS), vm(ROWS, ATOMS),
                vm(ROWS, 8, ATOMS), vm(ROWS, 8, ATOMS),
                vm(6, 8, ATOMS), vm(9, 8, ATOMS),
                vm(2, 18, 8, 128), vm(8, 24, 8, 128),
                vm(16, 39, 8, 128), vm(8, 24, 8, 128),
                vm(CH, ATOMS), vm(2, 128, 128),
                pltpu.VMEM((CH, 3 * HID), BF16), vm(CH, 128),
                pltpu.VMEM((ATOMS, 128), BF16), pltpu.VMEM((8, 128), jnp.int32),
                pltpu.VMEM((3 * ROWS, FAN * ATOMS), BF16),
                vm(4, GHOST, 256), vm(4, GHOST, 256),
                vm(4, slots, 8, 128),
                dma(4, 26), dma(4, 26), dma(4, slots), dma(4, slots),
            ],
            compiler_params=pltpu.CompilerParams(
                collective_id=0, has_side_effects=True, vmem_limit_bytes=48 * 1024 * 1024
            ),
        )(
            positions.reshape(3, 1, ATOMS), species.reshape(1, ATOMS),
            jnp.transpose(start_block[0, 0, 0], (1, 0, 2)), neighbors.reshape(FAN, 1, ATOMS),
            ghost_lists, embedding, radial_in, radial_out.T, readout[None], jnp.asarray(cst),
        )
        return jnp.transpose(out[0], (1, 0, 2))[None, None, None], out[1], out[2]

    return jax.shard_map(
        on_device,
        mesh=mesh,
        in_specs=(
            P("gx", "gy", "gz", None, None),
            P("gx", "gy", "gz", None),
            P("gx", "gy", "gz", None, None, None),
            P("gx", "gy", "gz", None, None),
            P("gx", "gy", "gz", None),
            P(), P(), P(), P(),
        ),
        out_specs=(P("gx", "gy", "gz", None, None, None), P(), P()),
        check_vma=False,
    )
```

```python
import functools
import itertools
import math

import jax
import jax.numpy as jnp
import numpy as np
from jax import lax
from jax.experimental import pallas as pl
from jax.experimental.pallas import tpu as pltpu
from jax.sharding import PartitionSpec as P

AXES = ("gx", "gy", "gz")
SOFTEN = 0.25
CUTOFF = 4.0
F32 = jnp.float32
BF16 = jnp.bfloat16
ATOMS = 256
FAN = 6
CH = 64
HID = 128
NB = 8
COLS = 1152
ROWS = 16
HIGHEST = lax.Precision.HIGHEST
MESH = pl.DeviceIdType.MESH

SF, SF1, SF2, SP, SA, SB, SE = 0, 6, 12, 18, 24, 30, 36


def neighbour_cells():
    shifts = [s for s in itertools.product((-1, 0, 1), repeat=3) if any(s)]
    shifts.sort(key=lambda s: sum(map(abs, s)))
    out, first = [], 0
    for s in shifts:
        octants = list(itertools.product(*[{1: (0,), -1: (1,), 0: (0, 1)}[x] for x in s]))
        out.append((s, first, octants))
        first += len(octants)
    return out


CELLS = neighbour_cells()
GHOST = 56


def constants():
    order = {}
    for number in range(64):
        m = (number // 16, number // 4 % 4, number % 4)
        if not all(x in (1, 2) for x in m):
            order[m] = len(order)
    out = np.zeros((32, 128), np.float32)
    ids = list(range(256))
    moves = []
    octant_of = []
    for s, _, octants in CELLS:
        for o in octants:
            m = tuple(2 * x + y + 1 for x, y in zip(s, o))
            ids += [256 + 16 * order[m] + r for r in range(16)]
            moves += [s] * 16
            octant_of.append(4 * o[0] + 2 * o[1] + o[2])
    assert sorted(ids) == list(range(COLS))
    out[0:9] = np.array(ids).reshape(9, 128)
    out[9] = -1.0
    out[9, :GHOST] = octant_of
    out[10:31] = np.array(moves).T.reshape(21, 128)
    return out


def split3(x):
    high = x.astype(BF16)
    rest = x - high.astype(F32)
    mid = rest.astype(BF16)
    low = (rest - mid.astype(F32)).astype(BF16)
    return high, mid, low


def rows3(x):
    return jnp.concatenate(split3(x), axis=0)


def sum3(y):
    n = y.shape[0] // 3
    return (y[2 * n :] + y[n : 2 * n]) + y[:n]


def mm(a, b, contract=((1,), (0,))):
    return lax.dot_general(a, b, (contract, ((), ())), preferred_element_type=F32)


def mm_high(a, b):
    return jnp.dot(a, b, precision=HIGHEST, preferred_element_type=F32)


def sin_cos(x):
    q = jnp.floor(x * (2.0 / math.pi) + 0.5)
    y = x - q * 1.5703125
    y = y - q * 4.837512969970703125e-4
    y = y - q * 7.549789948768648e-8
    y2 = y * y
    s = y + y * y2 * (-1.6666654611e-1 + y2 * (8.3321608736e-3 - y2 * 1.9515295891e-4))
    c = 1.0 - 0.5 * y2 + y2 * y2 * (4.166664568298827e-2 + y2 * (-1.388731625493765e-3 + y2 * 2.443315711809948e-5))
    h = q - 4.0 * jnp.floor(q * 0.25)
    odd = (h == 1.0) | (h == 3.0)
    ss = jnp.where(odd, c, s)
    cc = jnp.where(odd, s, c)
    ss = jnp.where(h >= 2.0, -ss, ss)
    cc = jnp.where((h == 1.0) | (h == 2.0), -cc, cc)
    return ss, cc


def kernel(
    sizes, *refs,
):
    hbm, (next_ref, diag_ref, off_ref) = refs[:10], refs[10:13]
    arrived, *local = refs[13:24]
    pos_ref, spc_ref, sb_ref, nbr_ref, gl_ref, emb_ref, rin_ref, rout_ref, rdo_ref, cst_ref = local
    (
        own, inc, inc_t, tab, v1, w1, r1, v2, dt, grs, geo, sums, ub, bv, fs, acc, epv, wpad, w2, embc, ghost, glw, cb,
        hs_buf, hr_buf, arb, hsend, hrecv, asend, arecv,
    ) = refs[24:]
    fetch = [pltpu.make_async_copy(a, b, arrived.at[n]) for n, (a, b) in enumerate(zip(hbm, local))]
    for copy in fetch:
        copy.start()
    gx, gy, gz = (lax.axis_index(a) for a in AXES)
    scale_ip = 1.0 / (3.0 * ATOMS * sizes[0] * sizes[1] * sizes[2])

    def beside(s):
        return {
            a: lax.rem(i + (x + n), n) for a, i, x, n in zip(AXES, (gx, gy, gz), s, sizes) if x
        }

    nx, ny, nz = sizes[0] // 2, sizes[1], sizes[2] // 2
    groups = (
        [o for o in itertools.product(range(nx), range(2), (0,), (0,), range(2)) if any(o)],
        [o for o in itertools.product((0,), (0,), range(ny), range(nz), (0,)) if any(o)],
    )
    starts = (0, len(groups[0]) + 1)

    def partner(o):
        a = lax.rem(gx // 2 + o[0], nx)
        b = lax.rem(lax.rem(gx, 2) + o[1], 2)
        c = lax.rem(gy + o[2], ny)
        d = lax.rem(gz // 2 + o[3], nz)
        e = lax.rem(lax.rem(gz, 2) + o[4], 2)
        return {"gx": 2 * a + b, "gy": c, "gz": 2 * d + e}, (4 * a + 2 * b + e, nz * c + d)

    barrier = pltpu.get_barrier_semaphore()
    for s, _, _ in CELLS:
        pl.semaphore_signal(barrier, inc=1, device_id=beside(s), device_id_type=MESH)
    for group in groups:
        for o in group:
            pl.semaphore_signal(barrier, inc=1, device_id=partner(o)[0], device_id_type=MESH)

    lane8 = lax.broadcasted_iota(jnp.int32, (8, 128), 1)
    sub8 = lax.broadcasted_iota(jnp.int32, (8, 128), 0)

    def ar_send(i, g, tile):
        mine = starts[g] + partner((0,) * 5)[1][g]
        arb[i, mine] = tile
        for o in groups[g]:
            pltpu.make_async_remote_copy(
                src_ref=arb.at[i, mine], dst_ref=arb.at[i, mine],
                send_sem=asend.at[i, g], recv_sem=arecv.at[i, g],
                device_id=partner(o)[0], device_id_type=MESH,
            ).start()

    def ar_all(i, g):
        part = arb.at[i, pl.ds(starts[g], len(groups[g]))]
        return pltpu.make_async_remote_copy(
            src_ref=part, dst_ref=part, send_sem=asend.at[i, g], recv_sem=arecv.at[i, g],
            device_id=partner(groups[g][0])[0], device_id_type=MESH,
        )

    def ar_recv(i, g):
        ar_all(i, g).wait_recv()
        parts = [arb[i, starts[g] + j] for j in range(len(groups[g]) + 1)]
        while len(parts) > 1:
            parts = [a + b for a, b in zip(parts[::2], parts[1::2])] + parts[len(parts) // 2 * 2 :]
        return parts[0]

    def halo_send(i, sign):
        for s, first, octants in CELLS:
            at = pl.ds(first, len(octants))
            pltpu.make_async_remote_copy(
                src_ref=hs_buf.at[i, at], dst_ref=hr_buf.at[i, at],
                send_sem=hsend.at[i], recv_sem=hrecv.at[i],
                device_id=beside(tuple(sign * x for x in s)), device_id_type=MESH,
            ).start()

    def halo_all(i):
        return pltpu.make_async_remote_copy(
            src_ref=hs_buf.at[i], dst_ref=hr_buf.at[i], send_sem=hsend.at[i], recv_sem=hrecv.at[i],
            device_id=beside(CELLS[0][0]), device_id_type=MESH,
        )

    def halo_wait(i):
        halo_all(i).wait_recv()

    def turn(x):
        for b in (2, 1, 0):
            by = 1 << b
            sbit = (sub8 & by) != 0
            lbit = (lane8 & (16 * by)) != 0
            low = pltpu.roll(pltpu.roll(x, by, 0), 128 - 16 * by, 1)
            high = low if b == 2 else pltpu.roll(pltpu.roll(x, 8 - by, 0), 16 * by, 1)
            x = jnp.where(sbit == lbit, x, jnp.where(sbit, low, high))
        return x

    def pack(i, src):
        got = sum3(mm(rows3(src), ghost[...]))
        flat = jnp.concatenate([turn(got[0:8]), turn(got[8:16])], axis=1)
        hs_buf[i] = mm(spread, rows3(flat))

    def unpack(i, dst, shifted):
        for j in range(7):
            at = pl.ds(256 + 128 * j, 128)
            for t in range(2):
                part = turn(hr_buf[i, 8 * j : 8 * j + 8, 128 * t : 128 * t + 128])
                if t == 1 and shifted:
                    rows = [jnp.zeros((4, 128), F32)] + [cst_ref[10 + 7 * h + j : 11 + 7 * h + j, :] for h in range(3)]
                    part = part + jnp.concatenate(rows + [jnp.zeros((1, 128), F32)], axis=0)
                dst[8 * t : 8 * t + 8, at] = part

    def pack_back(i, con):
        for j in range(7):
            for t in range(2):
                part = con[8 * t : 8 * t + 8, 128 * j : 128 * j + 128]
                hs_buf[i, 8 * j : 8 * j + 8, 128 * t : 128 * t + 128] = turn(part)

    def unpack_back(i):
        hi, mid, lo = split3(hr_buf[i])
        flat = (mm(collect, lo) + mm(collect, mid)) + mm(collect, hi)
        both = jnp.concatenate([turn(flat[:, 0:128]), turn(flat[:, 128:256])], axis=0)
        return sum3(mm(rows3(both), ghost[...], ((1,), (1,))))

    def gram_rows(left, right):
        out = jnp.zeros((4, 128), F32)
        for w in range(4):
            prod = left[0:4, :] * right[w : w + 1, :]
            for c in (1, 2):
                prod = prod + left[4 * c : 4 * c + 4, :] * right[4 * c + w : 4 * c + w + 1, :]
            total = jnp.sum(prod, axis=1, keepdims=True) * scale_ip
            out = jnp.where(lane8[:4] == w, total, out)
        return out

    def entries(tile, row):
        out = [[None] * 4 for _ in range(4)]
        for w in range(4):
            col = jnp.broadcast_to(tile[:, w : w + 1], (8, 128))
            for u in range(4):
                out[u][w] = jnp.broadcast_to(col[row + u : row + u + 1, :], (8, 128))
        return out

    def place(vals):
        out = jnp.zeros((8, 128), F32)
        for n, val in enumerate(vals):
            if val is not None:
                out = jnp.where(sub8 == n, val, out)
        return out[0:4, 0:1]

    def matrix(get):
        out = jnp.zeros((8, 128), F32)
        for u in range(4):
            for w in range(4):
                val = get(u, w)
                if val is not None:
                    out = jnp.where((sub8 == u) & (lane8 == w), val, out)
        return out[0:4, 0:4]

    def cholesky(g):
        low = [[None] * 4 for _ in range(4)]
        inv_d = [None] * 4
        for j in range(4):
            total = g[j][j]
            for m in range(j):
                total = total - low[j][m] * low[j][m]
            low[j][j] = jnp.sqrt(total)
            inv_d[j] = 1.0 / low[j][j]
            for u in range(j + 1, 4):
                total = g[u][j]
                for m in range(j):
                    total = total - low[u][m] * low[j][m]
                low[u][j] = total * inv_d[j]
        inv = [[None] * 4 for _ in range(4)]
        for j in range(4):
            inv[j][j] = inv_d[j]
            for u in range(j + 1, 4):
                total = low[u][j] * inv[j][j]
                for m in range(j + 1, u):
                    total = total + low[u][m] * inv[m][j]
                inv[u][j] = -total * inv_d[u]
        return low, inv

    def columns_of(mat):
        return [place([mat[u][w] for u in range(4)]) for w in range(4)]

    def combine(cols, src, c):
        total = cols[0] * src[4 * c : 4 * c + 1, :]
        for w in range(1, 4):
            total = total + cols[w] * src[4 * c + w : 4 * c + w + 1, :]
        return total

    for copy in fetch:
        copy.wait()

    for c in range(3):
        own[4 * c : 4 * c + 4, :] = sb_ref[c]
        own[12 + c : 13 + c, :] = pos_ref[c]
    own[15:16, :] = spc_ref[...].astype(F32)
    glw[...] = jnp.zeros((8, 128), jnp.int32)
    for n in range(8):
        glw[n : n + 1, 0:16] = gl_ref[n // 4, n // 2 % 2, n % 2 : n % 2 + 1, :]
    names = glw[0:1, :]
    for n in range(1, 8):
        names = names + pltpu.roll(glw[n : n + 1, :], 16 * n, 1)
    atom_rows = lax.broadcasted_iota(jnp.int32, (ATOMS, 128), 0)
    ghost[...] = jnp.where(atom_rows == names, 1.0, 0.0).astype(BF16)
    wpad[1] = jnp.zeros((128, 128), F32)
    wpad[1, 0:32, :] = cst_ref[...]
    wpad[1] = wpad[1].T
    octant_col = wpad[1, 0:GHOST, 9:10]
    lane24 = lax.rem(lax.broadcasted_iota(jnp.int32, (GHOST, 24), 1), 8).astype(F32)
    spread = jnp.where(lane24 == octant_col, 1.0, 0.0).astype(BF16)
    collect = jnp.where(sub8.astype(F32) == cst_ref[9:10, :], 1.0, 0.0).astype(BF16)[:, 0:GHOST]
    pack(0, own[...])
    zeros4 = jnp.zeros((4, 128), F32)
    tile = jnp.concatenate([gram_rows(own, own), zeros4], axis=0)

    pl.semaphore_wait(barrier, len(CELLS) + len(groups[0]) + len(groups[1]))
    halo_send(0, -1)
    ar_send(0, 0, tile)

    atom_lane = lax.broadcasted_iota(jnp.int32, (128, ATOMS), 1).astype(F32)

    def build(j, is_own):
        name = wpad[1, :, j : j + 1]
        for k in range(FAN):
            part = jnp.where(nbr_ref[k].astype(F32) == name, 1.0, 0.0)
            if is_own:
                part = part - jnp.where(atom_lane == name, 1.0, 0.0)
            inc[128 * j : 128 * j + 128, ATOMS * k : ATOMS * k + ATOMS] = part.astype(BF16)

    atom_sub = lax.broadcasted_iota(jnp.int32, (128, 128), 0).astype(F32)

    def build_t(k, l):
        at = pl.ds(ATOMS * k + 128 * l, 128)
        name = wpad[2 + l, :, k : k + 1]
        for j in range(9):
            entry = cst_ref[j : j + 1, :]
            part = jnp.where(entry == name, 1.0, 0.0)
            if j < 2:
                part = part - jnp.where(atom_sub + 128.0 * l == entry, 1.0, 0.0)
            inc_t[at, 128 * j : 128 * j + 128] = part.astype(BF16)

    wpad[0] = jnp.zeros((128, 128), F32)
    hi, mid, lo = (x.astype(F32) for x in split3(rin_ref[...]))
    for n, part in enumerate((hi, mid, lo, hi, mid, hi)):
        wpad[0, 8 * n : 8 * n + 8, :] = part
    wpad[0, 48:50, 0:CH] = emb_ref[...]
    wpad[0, 50:51, 0:CH] = rdo_ref[...]
    wpad[0] = wpad[0].T
    embc[:, 0:3] = wpad[0, 0:CH, 48:51]
    hi, mid, lo = split3(rout_ref[...])
    w2[...] = jnp.concatenate([hi, mid, hi], axis=1)
    epv[...] = jnp.where(own[15:16, :] < 0.5, embc[:, 0:1], embc[:, 1:2])
    for l in range(2):
        wpad[2 + l] = jnp.zeros((128, 128), F32)
        for k in range(FAN):
            wpad[2 + l, k : k + 1, :] = nbr_ref[k, :, 128 * l : 128 * l + 128].astype(F32)
        wpad[2 + l] = wpad[2 + l].T
    for j in range(9):
        build(j, j < 2)
    for k in range(FAN):
        for l in range(2):
            build_t(k, l)
    ar_send(0, 1, ar_recv(0, 0))
    tab[:, 0:256] = own[...]
    halo_wait(0)
    unpack(0, tab, True)

    def gather(src):
        got = sum3(mm(rows3(src), inc[...]))
        for k in range(FAN):
            dt[:, k, :] = got[:, ATOMS * k : ATOMS * k + ATOMS]

    gather(tab[...])

    d3 = [dt[12 + h] for h in range(3)]
    dist2 = d3[0] * d3[0] + d3[1] * d3[1] + d3[2] * d3[2]
    dist = jnp.sqrt(dist2 + SOFTEN)
    inv_r = 1.0 / dist
    unit = [d * inv_r for d in d3]
    for h in range(3):
        geo[h] = unit[h]
    geo[3] = dist
    geo[4] = inv_r
    geo[5] = dt[15] + own[15:16, :]
    for h in range(3):
        for k in range(FAN):
            row = jnp.broadcast_to(unit[h][k : k + 1, :], (8, ATOMS))
            for l in range(2):
                ub[l, h * FAN + k] = row[:, 128 * l : 128 * l + 128]

    def tangents(product):
        for v in range(4):
            dv = [dt[4 * c + v] for c in range(3)]
            rp = geo[0] * dv[0] + geo[1] * dv[1] + geo[2] * dv[2]
            parts = [rp] + [(dv[h] - geo[h] * rp) * geo[4] for h in range(3)]
            for g in range(4):
                for k in range(FAN):
                    row = jnp.broadcast_to(parts[g][k : k + 1, :], (8, ATOMS))
                    for l in range(2):
                        bv[2 * v + l, g * FAN + k] = row[:, 128 * l : 128 * l + 128]

    tangents(0)

    order8 = (lax.broadcasted_iota(jnp.int32, (8, ATOMS), 0) + 1).astype(F32) * (math.pi / CUTOFF)

    PAIR = 3
    order_w = jnp.concatenate([order8] * PAIR, axis=1)

    def features(pair, z):
        rows = [[geo[n, pl.ds(PAIR * pair + m, 1), :] for m in range(PAIR)] for n in (3, 4, 5)]
        r, ir, kind = (jnp.concatenate(x, axis=1) for x in rows)
        s, c = sin_cos(order_w * r)
        b0 = s * ir
        b1 = (order_w * c - b0) * ir
        b2 = -(order_w * order_w) * b0 - 2.0 * b1 * ir
        rin_t = wpad[0, :, 0:48].astype(BF16)

        def first(b):
            hi, mid, lo = split3(b)
            return mm(rin_t, jnp.concatenate([hi, hi, hi, mid, mid, lo], axis=0))

        def second(h):
            hi = h.astype(BF16)
            mid = (h - hi.astype(F32)).astype(BF16)
            return mm(w2[...], jnp.concatenate([hi, hi, mid], axis=0))

        z0, z1, z2 = first(b0), first(b1), first(b2)
        sg = 1.0 / (1.0 + jnp.exp(-z0))
        sd = sg * (1.0 - sg)
        s1 = sg + z0 * sd
        s2 = sd * (2.0 + z0 * (1.0 - 2.0 * sg))
        r0, r1_, r2 = second(z0 * sg), second(s1 * z1), second(s2 * z1 * z1 + s1 * z2)
        q = r * r * (1.0 / (CUTOFF * CUTOFF))
        sixth = FAN ** -0.5
        e0 = (1.0 - q) * (1.0 - q) * sixth
        e1 = (-4.0 / (CUTOFF * CUTOFF)) * r * (1.0 - q) * sixth
        e2 = (-4.0 / (CUTOFF * CUTOFF)) * (1.0 - 3.0 * q) * sixth
        w = jnp.concatenate([epv[...]] * PAIR, axis=1) * jnp.where(kind < 0.5, embc[:, 0:1], embc[:, 1:2])
        f0 = r0 * e0 * w
        f1 = (r1_ * e0 + r0 * e1) * w
        f2 = (r2 * e0 + 2.0 * r1_ * e1 + r0 * e2) * w
        for slot, val in ((SF, f0), (SF1, f1), (SF2, f2)):
            for m in range(PAIR):
                for l in range(2):
                    for t in range(8):
                        at = ATOMS * m + 128 * l
                        fs[8 * l + t, slot + PAIR * pair + m] = val[8 * t : 8 * t + 8, at : at + 128]
        return z

    lax.fori_loop(0, FAN // PAIR, features, 0)

    ks = range(FAN)
    hs = range(3)

    def base_pass(i, z):
        l = i // 8
        t = lax.rem(i, 8)
        f = [fs[i, SF + k] for k in ks]
        f1 = [fs[i, SF1 + k] for k in ks]
        u = [[ub[l, h * FAN + k] for k in ks] for h in hs]
        rho = jnp.broadcast_to(embc[pl.ds(pl.multiple_of(t * 8, 8), 8), 2:3], (8, 128))
        e0 = sum(f[1:], f[0])
        e = [sum((f[k] * u[h][k] for k in ks[1:]), f[0] * u[h][0]) for h in hs]
        p, a, n = [], [], []
        for k in ks:
            pk = e0 + (e[0] * u[0][k] + e[1] * u[1][k] + e[2] * u[2][k])
            m = f[k] * pk
            sg = 1.0 / (1.0 + jnp.exp(-m))
            sd = sg * (1.0 - sg)
            ak = rho * (sg + m * sd)
            fs[i, SP + k] = pk
            fs[i, SA + k] = ak
            fs[i, SB + k] = rho * (sd * (2.0 + m * (1.0 - 2.0 * sg)))
            p.append(pk)
            a.append(ak)
            n.append(ak * f[k])
        for h in hs:
            fs[i, SE + h] = e[h]
        q0 = sum(n[1:], n[0])
        q = [sum((n[k] * u[h][k] for k in ks[1:]), n[0] * u[h][0]) for h in hs]
        for k in ks:
            fk = a[k] * p[k] + q0 + (q[0] * u[0][k] + q[1] * u[1][k] + q[2] * u[2][k])
            acc[l, k] += fk * f1[k]
            acc[2 + l, k] += fk * fs[i, SF2 + k]
            for h in hs:
                acc[l, FAN * (h + 1) + k] += n[k] * e[h] + f[k] * q[h]
                acc[2 + l, FAN * (h + 1) + k] += f1[k] * q[h]
        return z

    def clear():
        def zero(i, z):
            acc[i] = jnp.zeros((24, 8, 128), F32)
            return z
        lax.fori_loop(0, 8, zero, 0)

    one_row = lax.broadcasted_iota(jnp.int32, (32, 192), 0)
    one_col = lax.broadcasted_iota(jnp.int32, (32, 192), 1) // 8
    ones = jnp.where((one_row % 8 < FAN) & (one_row // 8 * FAN + one_row % 8 == one_col), 1.0, 0.0).astype(BF16)

    def fold(v):
        out = []
        for l in range(2):
            hi, mid, lo = split3(acc[2 * v + l].reshape(192, 128))
            out.append((mm(ones, lo) + mm(ones, mid)) + mm(ones, hi))
        return jnp.concatenate(out, axis=1)

    clear()
    lax.fori_loop(0, 16, base_pass, 0, unroll=2)
    first, second = fold(0), fold(1)
    alpha, beta = first[0:8], second[0:8]
    force = [first[8 * h + 8 : 8 * h + 16] for h in hs]
    cross = [second[8 * h + 8 : 8 * h + 16] for h in hs]
    uv = unit[0] * force[0] + unit[1] * force[1] + unit[2] * force[2]
    sums[0] = alpha
    sums[1] = beta
    sums[2] = uv
    for h in hs:
        sums[3 + h] = force[h]
        sums[6 + h] = cross[h]

    def hvp(i, z):
        v = i // 16
        ch = lax.rem(i, 16)
        vl = 2 * v + ch // 8
        l = ch // 8
        f = [fs[ch, SF + k] for k in ks]
        rp = [bv[vl, k] for k in ks]
        u = lambda h, k: ub[l, h * FAN + k]
        du = lambda h, k: bv[vl, (h + 1) * FAN + k]
        df = [fs[ch, SF1 + k] * rp[k] for k in ks]
        de0 = sum(df[1:], df[0])
        de = []
        for h in hs:
            total = df[0] * u(h, 0) + f[0] * du(h, 0)
            for k in ks[1:]:
                total = total + (df[k] * u(h, k) + f[k] * du(h, k))
            de.append(total)
        e = [fs[ch, SE + h] for h in hs]
        dn, dfeat, n = [], [], []
        for k in ks:
            dp = de0
            for h in hs:
                dp = dp + (de[h] * u(h, k) + e[h] * du(h, k))
            pk, ak = fs[ch, SP + k], fs[ch, SA + k]
            da = fs[ch, SB + k] * (df[k] * pk + f[k] * dp)
            dn.append(da * f[k] + ak * df[k])
            n.append(ak * f[k])
            dfeat.append(da * pk + ak * dp)
        dq0 = sum(dn[1:], dn[0])
        dq = []
        for h in hs:
            total = dn[0] * u(h, 0) + n[0] * du(h, 0)
            for k in ks[1:]:
                total = total + (dn[k] * u(h, k) + n[k] * du(h, k))
            dq.append(total)
        for k in ks:
            tot = dfeat[k] + dq0 + (dq[0] * u(0, k) + dq[1] * u(1, k) + dq[2] * u(2, k))
            acc[vl, k] += fs[ch, SF1 + k] * tot
            for h in hs:
                acc[vl, FAN * (h + 1) + k] += (dn[k] * e[h] + n[k] * de[h]) + f[k] * dq[h]
        return z

    grs[12:16] = jnp.zeros((4, 8, ATOMS), F32)

    def finish_hvp():
        u3 = [geo[h] for h in hs]
        ir = geo[4]
        for v in range(4):
            got = fold(v)
            dv = [dt[4 * c + v] for c in range(3)]
            rp = u3[0] * dv[0] + u3[1] * dv[1] + u3[2] * dv[2]
            du = [(dv[h] - u3[h] * rp) * ir for h in hs]
            al, be, w0 = sums[0], sums[1], sums[2]
            fo = [sums[3 + h] for h in hs]
            cr = [sums[6 + h] for h in hs]
            dal = got[0:8] + be * rp + (cr[0] * du[0] + cr[1] * du[1] + cr[2] * du[2])
            dfo = [got[8 * h + 8 : 8 * h + 16] + rp * cr[h] for h in hs]
            duv = sum((du[h] * fo[h] + u3[h] * dfo[h] for h in hs[1:]), du[0] * fo[0] + u3[0] * dfo[0])
            back = rp * ir
            for h in hs:
                val = dal * u3[h] + al * du[h]
                val = val + ir * ((dfo[h] - du[h] * w0 - u3[h] * duv) - back * (fo[h] - u3[h] * w0))
                grs[4 * h + v] = val
        for k in ks:
            cb[:, ATOMS * k : ATOMS * k + ATOMS] = rows3(grs[:, k, :])

    def scatter(at):
        return sum3(mm(cb[...], inc_t[:, at]))

    def give_back(i):
        finish_hvp()
        pack_back(i, scatter(pl.ds(256, COLS - 256)))
        halo_send(i, 1)
        return scatter(pl.ds(0, 256))

    def combine_all(dst, cols, src, minus=None):
        for c in range(3):
            got = combine(cols, src, c)
            dst[4 * c : 4 * c + 4, :] = got if minus is None else minus[4 * c : 4 * c + 4, :] - got

    def transposed(proj):
        return [place([proj[u][w] for w in range(4)]) for u in range(4)]

    clear()
    lax.fori_loop(0, 64, hvp, 0, unroll=2)
    low, inv = cholesky(entries(ar_recv(0, 1), 0))
    cols0 = columns_of(inv)
    local = give_back(1)
    combine_all(v1, cols0, own)
    w1[12:16, :] = jnp.zeros((4, ATOMS), F32)
    halo_wait(1)
    own[...] = local + unpack_back(1)
    combine_all(w1, cols0, own)
    pack(2, w1[...])
    halo_send(2, -1)
    ar_send(1, 0, jnp.concatenate([gram_rows(v1, w1), zeros4], axis=0))
    tab[:, 0:256] = w1[...]
    clear()
    ar_send(1, 1, ar_recv(1, 0))
    halo_wait(2)
    unpack(2, tab, False)

    gather(tab[...])
    tangents(1)
    lax.fori_loop(0, 16, hvp, 0, unroll=2)
    proj = entries(ar_recv(1, 1), 0)
    cols_a = transposed(proj)
    combine_all(r1, cols_a, v1, w1)
    ar_send(2, 0, jnp.concatenate([gram_rows(r1, r1), zeros4], axis=0))
    diag_ref[0] = matrix(lambda u, w: proj[u][w])
    lax.fori_loop(16, 64, hvp, 0, unroll=2)
    ar_send(2, 1, ar_recv(2, 0))
    local = give_back(3)
    low, inv = cholesky(entries(ar_recv(2, 1), 0))
    cols1 = columns_of(inv)
    off_ref[0] = matrix(lambda u, w: low[w][u] if w >= u else None)
    combine_all(v2, cols1, r1)
    for i in range(4):
        halo_all(i).wait_send()
    for i in range(3):
        for g in range(2):
            ar_all(i, g).wait_send()
    halo_wait(3)
    own[...] = local + unpack_back(3)
    combine_all(r1, cols_a, w1, own)
    combine_all(own, cols1, r1)
    gram_w = pltpu.roll(jnp.concatenate([gram_rows(own, own), zeros4], axis=0), 4, 1)
    tile = jnp.concatenate([gram_rows(v2, own), gram_rows(v1, own)], axis=0) + gram_w
    for g in range(2):
        ar_send(3, g, tile)
        tile = ar_recv(3, g)
    proj = entries(tile, 0)
    prev = entries(tile, 4)
    gram = entries(pltpu.roll(tile, 124, 1), 0)
    for u in range(4):
        for w in range(u + 1):
            total = gram[u][w]
            for m in range(4):
                total = total - (proj[m][u] * proj[m][w] + prev[m][u] * prev[m][w])
            gram[u][w] = total
    combine_all(r1, transposed(proj), v2, own)
    combine_all(own, transposed(prev), v1, r1)
    low, inv = cholesky(gram)
    cols = columns_of(inv)
    for c in range(3):
        next_ref[c] = combine(cols, own, c)
    diag_ref[1] = matrix(lambda u, w: proj[u][w])
    off_ref[1] = matrix(lambda u, w: low[w][u] if w >= u else None)
    for g in range(2):
        ar_all(3, g).wait_send()


def solution(mesh):
    sizes = tuple(mesh.shape[a] for a in AXES)
    cst = constants()
    slots = 2 * sizes[0] + sizes[1] * sizes[2] // 2

    def on_device(positions, species, start_block, neighbors, ghost_lists, embedding, radial_in, radial_out, readout):
        vmem = pl.BlockSpec(memory_space=pltpu.VMEM)
        vm = lambda *shape: pltpu.VMEM(shape, F32)
        dma = lambda *shape: pltpu.SemaphoreType.DMA(shape)
        operands = (
            positions.reshape(3, 1, ATOMS), species.reshape(1, ATOMS),
            jnp.transpose(start_block[0, 0, 0], (1, 0, 2)), neighbors.reshape(FAN, 1, ATOMS),
            ghost_lists, embedding, radial_in, radial_out.T, readout[None], jnp.asarray(cst),
        )
        out = pl.pallas_call(
            functools.partial(kernel, sizes),
            out_shape=(
                jax.ShapeDtypeStruct((3, 4, ATOMS), F32),
                jax.ShapeDtypeStruct((2, 4, 4), F32),
                jax.ShapeDtypeStruct((2, 4, 4), F32),
            ),
            in_specs=[pl.BlockSpec(memory_space=pltpu.HBM)] * 10,
            out_specs=(vmem, vmem, vmem),
            scratch_shapes=[dma(10)]
            + [pltpu.VMEM(x.shape, x.dtype) for x in operands]
            + [
                vm(ROWS, ATOMS),
                pltpu.VMEM((COLS, FAN * ATOMS), BF16),
                pltpu.VMEM((FAN * ATOMS, COLS), BF16),
                vm(ROWS, COLS),
                vm(ROWS, ATOMS), vm(ROWS, ATOMS), vm(ROWS, ATOMS), vm(ROWS, ATOMS),
                vm(ROWS, 8, ATOMS), vm(ROWS, 8, ATOMS),
                vm(6, 8, ATOMS), vm(9, 8, ATOMS),
                vm(2, 18, 8, 128), vm(8, 24, 8, 128),
                vm(16, 39, 8, 128), vm(8, 24, 8, 128),
                vm(CH, ATOMS), vm(4, 128, 128),
                pltpu.VMEM((CH, 3 * HID), BF16), vm(CH, 128),
                pltpu.VMEM((ATOMS, 128), BF16), pltpu.VMEM((8, 128), jnp.int32),
                pltpu.VMEM((3 * ROWS, FAN * ATOMS), BF16),
                vm(4, GHOST, 256), vm(4, GHOST, 256),
                vm(4, slots, 8, 128),
                dma(4), dma(4), dma(4, 2), dma(4, 2),
            ],
            compiler_params=pltpu.CompilerParams(
                collective_id=0, has_side_effects=True, vmem_limit_bytes=67_043_328
            ),
        )(*operands)
        return jnp.transpose(out[0], (1, 0, 2))[None, None, None], out[1], out[2]

    return jax.shard_map(
        on_device,
        mesh=mesh,
        in_specs=(
            P("gx", "gy", "gz", None, None),
            P("gx", "gy", "gz", None),
            P("gx", "gy", "gz", None, None, None),
            P("gx", "gy", "gz", None, None),
            P("gx", "gy", "gz", None),
            P(), P(), P(), P(),
        ),
        out_specs=(P("gx", "gy", "gz", None, None, None), P(), P()),
        check_vma=False,
    )
```

```python
import functools
import itertools
import math

import jax
import jax.numpy as jnp
import numpy as np
from jax import lax
from jax.experimental import pallas as pl
from jax.experimental.pallas import tpu as pltpu
from jax.sharding import PartitionSpec as P

AXES = ("gx", "gy", "gz")
SOFTEN = 0.25
CUTOFF = 4.0
F32 = jnp.float32
BF16 = jnp.bfloat16
ATOMS = 256
FAN = 6
CH = 64
HID = 128
NB = 8
COLS = 1152
ROWS = 16
HIGHEST = lax.Precision.HIGHEST
MESH = pl.DeviceIdType.MESH

SF, SF1, SF2, SP, SA, SB, SE, SN, SBP = 0, 6, 12, 18, 24, 30, 36, 39, 45


def neighbour_cells():
    shifts = [s for s in itertools.product((-1, 0, 1), repeat=3) if any(s)]
    shifts.sort(key=lambda s: sum(map(abs, s)))
    out, first = [], 0
    for s in shifts:
        octants = list(itertools.product(*[{1: (0,), -1: (1,), 0: (0, 1)}[x] for x in s]))
        out.append((s, first, octants))
        first += len(octants)
    return out


CELLS = neighbour_cells()
GHOST = 56


def constants():
    order = {}
    for number in range(64):
        m = (number // 16, number // 4 % 4, number % 4)
        if not all(x in (1, 2) for x in m):
            order[m] = len(order)
    out = np.zeros((32, 128), np.float32)
    ids = list(range(256))
    moves = []
    octant_of = []
    for s, _, octants in CELLS:
        for o in octants:
            m = tuple(2 * x + y + 1 for x, y in zip(s, o))
            ids += [256 + 16 * order[m] + r for r in range(16)]
            moves += [s] * 16
            octant_of.append(4 * o[0] + 2 * o[1] + o[2])
    assert sorted(ids) == list(range(COLS))
    out[0:9] = np.array(ids).reshape(9, 128)
    out[9] = -1.0
    out[9, :GHOST] = octant_of
    out[10:31] = np.array(moves).T.reshape(21, 128)
    return out


def split3(x):
    high = x.astype(BF16)
    rest = x - high.astype(F32)
    mid = rest.astype(BF16)
    low = (rest - mid.astype(F32)).astype(BF16)
    return high, mid, low


def rows3(x):
    return jnp.concatenate(split3(x), axis=0)


def sum3(y):
    n = y.shape[0] // 3
    return (y[2 * n :] + y[n : 2 * n]) + y[:n]


def mm(a, b, contract=((1,), (0,))):
    return lax.dot_general(a, b, (contract, ((), ())), preferred_element_type=F32)


def mm_high(a, b):
    return jnp.dot(a, b, precision=HIGHEST, preferred_element_type=F32)


def sin_cos(x):
    q = jnp.floor(x * (2.0 / math.pi) + 0.5)
    y = x - q * 1.5703125
    y = y - q * 4.837512969970703125e-4
    y = y - q * 7.549789948768648e-8
    y2 = y * y
    s = y + y * y2 * (-1.6666654611e-1 + y2 * (8.3321608736e-3 - y2 * 1.9515295891e-4))
    c = 1.0 - 0.5 * y2 + y2 * y2 * (4.166664568298827e-2 + y2 * (-1.388731625493765e-3 + y2 * 2.443315711809948e-5))
    h = q - 4.0 * jnp.floor(q * 0.25)
    odd = (h == 1.0) | (h == 3.0)
    ss = jnp.where(odd, c, s)
    cc = jnp.where(odd, s, c)
    ss = jnp.where(h >= 2.0, -ss, ss)
    cc = jnp.where((h == 1.0) | (h == 2.0), -cc, cc)
    return ss, cc


def kernel(
    sizes, *refs,
):
    hbm, (next_ref, small_ref) = refs[:10], refs[10:12]
    arrived, *local = refs[12:23]
    pos_ref, spc_ref, sb_ref, nbr_ref, gl_ref, emb_ref, rin_ref, rout_ref, rdo_ref, cst_ref = local
    (
        own, inc, inc_t, tab, v1, w1, r1, v2, dt, grs, geo, sums, ub, bv, fs, acc, epv, wpad, w2, embc, ghost, glw, cb,
        hs_buf, hr_buf, arb, hsend, hrecv, asend, arecv,
    ) = refs[23:]
    fetch = [pltpu.make_async_copy(a, b, arrived.at[n]) for n, (a, b) in enumerate(zip(hbm, local))]
    for copy in fetch:
        copy.start()
    gx, gy, gz = (lax.axis_index(a) for a in AXES)
    scale_ip = 1.0 / (3.0 * ATOMS * sizes[0] * sizes[1] * sizes[2])

    def beside(s):
        return {
            a: lax.rem(i + (x + n), n) for a, i, x, n in zip(AXES, (gx, gy, gz), s, sizes) if x
        }

    nx, ny, nz = sizes[0] // 2, sizes[1], sizes[2] // 2
    groups = (
        [o for o in itertools.product(range(nx), range(2), (0,), (0,), range(2)) if any(o)],
        [o for o in itertools.product((0,), (0,), range(ny), range(nz), (0,)) if any(o)],
    )
    starts = (0, len(groups[0]) + 1)

    def partner(o):
        a = lax.rem(gx // 2 + o[0], nx)
        b = lax.rem(lax.rem(gx, 2) + o[1], 2)
        c = lax.rem(gy + o[2], ny)
        d = lax.rem(gz // 2 + o[3], nz)
        e = lax.rem(lax.rem(gz, 2) + o[4], 2)
        return {"gx": 2 * a + b, "gy": c, "gz": 2 * d + e}, (4 * a + 2 * b + e, nz * c + d)

    far = sorted(CELLS, key=lambda x: -(5 * abs(x[0][2]) + 2 * abs(x[0][1]) + abs(x[0][0])))
    for group in groups:
        group.sort(key=lambda o: -(min(o[2], ny - o[2]) + min(o[3], nz - o[3]) + o[0] + 2 * o[4]))
    barrier = pltpu.get_barrier_semaphore()
    for s, _, _ in far:
        pl.semaphore_signal(barrier, inc=1, device_id=beside(s), device_id_type=MESH)
    for group in groups:
        for o in group:
            pl.semaphore_signal(barrier, inc=1, device_id=partner(o)[0], device_id_type=MESH)

    lane8 = lax.broadcasted_iota(jnp.int32, (8, 128), 1)
    sub8 = lax.broadcasted_iota(jnp.int32, (8, 128), 0)

    def ar_send(i, g, tile):
        mine = starts[g] + partner((0,) * 5)[1][g]
        arb[i, mine] = tile
        for o in groups[g]:
            pltpu.make_async_remote_copy(
                src_ref=arb.at[i, mine], dst_ref=arb.at[i, mine],
                send_sem=asend.at[i, g], recv_sem=arecv.at[i, g],
                device_id=partner(o)[0], device_id_type=MESH,
            ).start()

    def ar_all(i, g):
        part = arb.at[i, pl.ds(starts[g], len(groups[g]))]
        return pltpu.make_async_remote_copy(
            src_ref=part, dst_ref=part, send_sem=asend.at[i, g], recv_sem=arecv.at[i, g],
            device_id=partner(groups[g][0])[0], device_id_type=MESH,
        )

    def ar_recv(i, g):
        ar_all(i, g).wait_recv()
        parts = [arb[i, starts[g] + j] for j in range(len(groups[g]) + 1)]
        while len(parts) > 1:
            parts = [a + b for a, b in zip(parts[::2], parts[1::2])] + parts[len(parts) // 2 * 2 :]
        return parts[0]

    def halo_send(i, sign):
        for s, first, octants in far:
            at = pl.ds(first, len(octants))
            pltpu.make_async_remote_copy(
                src_ref=hs_buf.at[i, at], dst_ref=hr_buf.at[i, at],
                send_sem=hsend.at[i], recv_sem=hrecv.at[i],
                device_id=beside(tuple(sign * x for x in s)), device_id_type=MESH,
            ).start()

    def halo_all(i):
        return pltpu.make_async_remote_copy(
            src_ref=hs_buf.at[i], dst_ref=hr_buf.at[i], send_sem=hsend.at[i], recv_sem=hrecv.at[i],
            device_id=beside(CELLS[0][0]), device_id_type=MESH,
        )

    def halo_wait(i):
        halo_all(i).wait_recv()

    def turn(x):
        for b in (2, 1, 0):
            by = 1 << b
            sbit = (sub8 & by) != 0
            lbit = (lane8 & (16 * by)) != 0
            low = pltpu.roll(pltpu.roll(x, by, 0), 128 - 16 * by, 1)
            high = low if b == 2 else pltpu.roll(pltpu.roll(x, 8 - by, 0), 16 * by, 1)
            x = jnp.where(sbit == lbit, x, jnp.where(sbit, low, high))
        return x

    def pack(i, src):
        got = sum3(mm(rows3(src), ghost[...]))
        flat = jnp.concatenate([turn(got[0:8]), turn(got[8:16])], axis=1)
        hs_buf[i] = mm(spread, rows3(flat))

    def unpack(i, dst, shifted):
        for j in range(7):
            at = pl.ds(256 + 128 * j, 128)
            for t in range(2):
                part = turn(hr_buf[i, 8 * j : 8 * j + 8, 128 * t : 128 * t + 128])
                if t == 1 and shifted:
                    rows = [jnp.zeros((4, 128), F32)] + [cst_ref[10 + 7 * h + j : 11 + 7 * h + j, :] for h in range(3)]
                    part = part + jnp.concatenate(rows + [jnp.zeros((1, 128), F32)], axis=0)
                dst[8 * t : 8 * t + 8, at] = part

    def pack_back(i, con):
        for j in range(7):
            for t in range(2):
                part = con[8 * t : 8 * t + 8, 128 * j : 128 * j + 128]
                hs_buf[i, 8 * j : 8 * j + 8, 128 * t : 128 * t + 128] = turn(part)

    def unpack_back(i):
        hi, mid, lo = split3(hr_buf[i])
        flat = (mm(collect, lo) + mm(collect, mid)) + mm(collect, hi)
        both = jnp.concatenate([turn(flat[:, 0:128]), turn(flat[:, 128:256])], axis=0)
        return sum3(mm(rows3(both), ghost[...], ((1,), (1,))))

    def gram_rows(left, right):
        out = jnp.zeros((4, 128), F32)
        for w in range(4):
            prod = left[0:4, :] * right[w : w + 1, :]
            for c in (1, 2):
                prod = prod + left[4 * c : 4 * c + 4, :] * right[4 * c + w : 4 * c + w + 1, :]
            total = jnp.sum(prod, axis=1, keepdims=True) * scale_ip
            out = jnp.where(lane8[:4] == w, total, out)
        return out

    def entries(tile, row):
        out = [[None] * 4 for _ in range(4)]
        for w in range(4):
            col = jnp.broadcast_to(tile[:, w : w + 1], (8, 128))
            for u in range(4):
                out[u][w] = jnp.broadcast_to(col[row + u : row + u + 1, :], (8, 128))
        return out

    def place(vals):
        out = jnp.zeros((8, 128), F32)
        for n, val in enumerate(vals):
            if val is not None:
                out = jnp.where(sub8 == n, val, out)
        return out[0:4, 0:1]

    def matrix(get):
        out = jnp.zeros((8, 128), F32)
        for u in range(4):
            for w in range(4):
                val = get(u, w)
                if val is not None:
                    out = jnp.where((sub8 == u) & (lane8 == w), val, out)
        return out[0:4, 0:4]

    def cholesky(g):
        low = [[None] * 4 for _ in range(4)]
        inv_d = [None] * 4
        for j in range(4):
            total = g[j][j]
            for m in range(j):
                total = total - low[j][m] * low[j][m]
            inv_d[j] = lax.rsqrt(total)
            low[j][j] = total * inv_d[j]
            for u in range(j + 1, 4):
                total = g[u][j]
                for m in range(j):
                    total = total - low[u][m] * low[j][m]
                low[u][j] = total * inv_d[j]
        inv = [[None] * 4 for _ in range(4)]
        for j in range(4):
            inv[j][j] = inv_d[j]
            for u in range(j + 1, 4):
                total = low[u][j] * inv[j][j]
                for m in range(j + 1, u):
                    total = total + low[u][m] * inv[m][j]
                inv[u][j] = -total * inv_d[u]
        return low, inv

    def columns_of(mat):
        return [place([mat[u][w] for u in range(4)]) for w in range(4)]

    def combine(cols, src, c):
        total = cols[0] * src[4 * c : 4 * c + 1, :]
        for w in range(1, 4):
            total = total + cols[w] * src[4 * c + w : 4 * c + w + 1, :]
        return total

    for copy in fetch:
        copy.wait()

    for c in range(3):
        own[4 * c : 4 * c + 4, :] = sb_ref[c]
        own[12 + c : 13 + c, :] = pos_ref[c]
    own[15:16, :] = spc_ref[...].astype(F32)
    glw[...] = jnp.zeros((8, 128), jnp.int32)
    for n in range(8):
        glw[n : n + 1, 0:16] = gl_ref[n // 4, n // 2 % 2, n % 2 : n % 2 + 1, :]
    names = glw[0:1, :]
    for n in range(1, 8):
        names = names + pltpu.roll(glw[n : n + 1, :], 16 * n, 1)
    atom_rows = lax.broadcasted_iota(jnp.int32, (ATOMS, 128), 0)
    ghost[...] = jnp.where(atom_rows == names, 1.0, 0.0).astype(BF16)
    wpad[1] = jnp.zeros((128, 128), F32)
    wpad[1, 0:32, :] = cst_ref[...]
    wpad[1] = wpad[1].T
    octant_col = wpad[1, 0:GHOST, 9:10]
    lane24 = lax.rem(lax.broadcasted_iota(jnp.int32, (GHOST, 24), 1), 8).astype(F32)
    spread = jnp.where(lane24 == octant_col, 1.0, 0.0).astype(BF16)
    collect = jnp.where(sub8.astype(F32) == cst_ref[9:10, :], 1.0, 0.0).astype(BF16)[:, 0:GHOST]
    pack(0, own[...])
    zeros4 = jnp.zeros((4, 128), F32)
    tile = jnp.concatenate([gram_rows(own, own), zeros4], axis=0)

    pl.semaphore_wait(barrier, len(CELLS) + len(groups[0]) + len(groups[1]))
    halo_send(0, -1)
    ar_send(0, 0, tile)

    atom_lane = lax.broadcasted_iota(jnp.int32, (128, ATOMS), 1).astype(F32)

    def build(j, is_own):
        name = wpad[1, :, j : j + 1]
        for k in range(FAN):
            part = jnp.where(nbr_ref[k].astype(F32) == name, 1.0, 0.0)
            if is_own:
                part = part - jnp.where(atom_lane == name, 1.0, 0.0)
            inc[128 * j : 128 * j + 128, ATOMS * k : ATOMS * k + ATOMS] = part.astype(BF16)

    atom_sub = lax.broadcasted_iota(jnp.int32, (128, 128), 0).astype(F32)

    def build_t(k, l):
        at = pl.ds(ATOMS * k + 128 * l, 128)
        name = wpad[2 + l, :, k : k + 1]
        for j in range(9):
            entry = cst_ref[j : j + 1, :]
            part = jnp.where(entry == name, 1.0, 0.0)
            if j < 2:
                part = part - jnp.where(atom_sub + 128.0 * l == entry, 1.0, 0.0)
            inc_t[at, 128 * j : 128 * j + 128] = part.astype(BF16)

    wpad[0] = jnp.zeros((128, 128), F32)
    hi, mid, lo = (x.astype(F32) for x in split3(rin_ref[...]))
    for n, part in enumerate((hi, mid, lo, hi, mid, hi)):
        wpad[0, 8 * n : 8 * n + 8, :] = part
    wpad[0, 48:50, 0:CH] = emb_ref[...]
    wpad[0, 50:51, 0:CH] = rdo_ref[...]
    wpad[0] = wpad[0].T
    embc[:, 0:3] = wpad[0, 0:CH, 48:51]
    hi, mid, lo = split3(rout_ref[...])
    w2[...] = jnp.concatenate([hi, mid, hi], axis=1)
    epv[...] = jnp.where(own[15:16, :] < 0.5, embc[:, 0:1], embc[:, 1:2])
    for l in range(2):
        wpad[2 + l] = jnp.zeros((128, 128), F32)
        for k in range(FAN):
            wpad[2 + l, k : k + 1, :] = nbr_ref[k, :, 128 * l : 128 * l + 128].astype(F32)
        wpad[2 + l] = wpad[2 + l].T
    for j in range(9):
        build(j, j < 2)
    for k in range(FAN):
        for l in range(2):
            build_t(k, l)
    ar_send(0, 1, ar_recv(0, 0))
    tab[:, 0:256] = own[...]
    halo_wait(0)
    unpack(0, tab, True)

    def gather(src):
        got = sum3(mm(rows3(src), inc[...]))
        for k in range(FAN):
            dt[:, k, :] = got[:, ATOMS * k : ATOMS * k + ATOMS]

    gather(tab[...])

    d3 = [dt[12 + h] for h in range(3)]
    dist2 = d3[0] * d3[0] + d3[1] * d3[1] + d3[2] * d3[2]
    dist = jnp.sqrt(dist2 + SOFTEN)
    inv_r = 1.0 / dist
    unit = [d * inv_r for d in d3]
    for h in range(3):
        geo[h] = unit[h]
    geo[3] = dist
    geo[4] = inv_r
    geo[5] = dt[15] + own[15:16, :]
    for h in range(3):
        for k in range(FAN):
            row = jnp.broadcast_to(unit[h][k : k + 1, :], (8, ATOMS))
            for l in range(2):
                ub[l, h * FAN + k] = row[:, 128 * l : 128 * l + 128]

    def tangents(product):
        for v in range(4):
            dv = [dt[4 * c + v] for c in range(3)]
            rp = geo[0] * dv[0] + geo[1] * dv[1] + geo[2] * dv[2]
            parts = [rp] + [(dv[h] - geo[h] * rp) * geo[4] for h in range(3)]
            for g in range(4):
                for k in range(FAN):
                    row = jnp.broadcast_to(parts[g][k : k + 1, :], (8, ATOMS))
                    for l in range(2):
                        bv[2 * v + l, g * FAN + k] = row[:, 128 * l : 128 * l + 128]

    tangents(0)

    order8 = (lax.broadcasted_iota(jnp.int32, (8, ATOMS), 0) + 1).astype(F32) * (math.pi / CUTOFF)

    PAIR = 3
    order_w = jnp.concatenate([order8] * PAIR, axis=1)

    def features(pair, z):
        rows = [[geo[n, pl.ds(PAIR * pair + m, 1), :] for m in range(PAIR)] for n in (3, 4, 5)]
        r, ir, kind = (jnp.concatenate(x, axis=1) for x in rows)
        s, c = sin_cos(order_w * r)
        b0 = s * ir
        b1 = (order_w * c - b0) * ir
        b2 = -(order_w * order_w) * b0 - 2.0 * b1 * ir
        rin_t = wpad[0, :, 0:48].astype(BF16)

        def first(b):
            hi, mid, lo = split3(b)
            return mm(rin_t, jnp.concatenate([hi, hi, hi, mid, mid, lo], axis=0))

        def second(h):
            hi = h.astype(BF16)
            mid = (h - hi.astype(F32)).astype(BF16)
            return mm(w2[...], jnp.concatenate([hi, hi, mid], axis=0))

        z0, z1, z2 = first(b0), first(b1), first(b2)
        sg = 1.0 / (1.0 + jnp.exp(-z0))
        sd = sg * (1.0 - sg)
        s1 = sg + z0 * sd
        s2 = sd * (2.0 + z0 * (1.0 - 2.0 * sg))
        r0, r1_, r2 = second(z0 * sg), second(s1 * z1), second(s2 * z1 * z1 + s1 * z2)
        q = r * r * (1.0 / (CUTOFF * CUTOFF))
        sixth = FAN ** -0.5
        e0 = (1.0 - q) * (1.0 - q) * sixth
        e1 = (-4.0 / (CUTOFF * CUTOFF)) * r * (1.0 - q) * sixth
        e2 = (-4.0 / (CUTOFF * CUTOFF)) * (1.0 - 3.0 * q) * sixth
        w = jnp.concatenate([epv[...]] * PAIR, axis=1) * jnp.where(kind < 0.5, embc[:, 0:1], embc[:, 1:2])
        f0 = r0 * e0 * w
        f1 = (r1_ * e0 + r0 * e1) * w
        f2 = (r2 * e0 + 2.0 * r1_ * e1 + r0 * e2) * w
        for slot, val in ((SF, f0), (SF1, f1), (SF2, f2)):
            for m in range(PAIR):
                for l in range(2):
                    for t in range(8):
                        at = ATOMS * m + 128 * l
                        fs[8 * l + t, slot + PAIR * pair + m] = val[8 * t : 8 * t + 8, at : at + 128]
        return z

    lax.fori_loop(0, FAN // PAIR, features, 0)

    ks = range(FAN)
    hs = range(3)

    def base_pass(i, z):
        l = i // 8
        t = lax.rem(i, 8)
        f = [fs[i, SF + k] for k in ks]
        f1 = [fs[i, SF1 + k] for k in ks]
        u = [[ub[l, h * FAN + k] for k in ks] for h in hs]
        rho = jnp.broadcast_to(embc[pl.ds(pl.multiple_of(t * 8, 8), 8), 2:3], (8, 128))
        e0 = sum(f[1:], f[0])
        e = [sum((f[k] * u[h][k] for k in ks[1:]), f[0] * u[h][0]) for h in hs]
        p, a, n = [], [], []
        for k in ks:
            pk = e0 + (e[0] * u[0][k] + e[1] * u[1][k] + e[2] * u[2][k])
            m = f[k] * pk
            sg = 1.0 / (1.0 + jnp.exp(-m))
            sd = sg * (1.0 - sg)
            ak = rho * (sg + m * sd)
            fs[i, SP + k] = pk
            fs[i, SA + k] = ak
            bk = rho * (sd * (2.0 + m * (1.0 - 2.0 * sg)))
            nk = ak * f[k]
            fs[i, SB + k] = bk * f[k]
            fs[i, SBP + k] = bk * (f1[k] * pk)
            fs[i, SN + k] = nk
            p.append(pk)
            a.append(ak)
            n.append(nk)
        for h in hs:
            fs[i, SE + h] = e[h]
        q0 = sum(n[1:], n[0])
        q = [sum((n[k] * u[h][k] for k in ks[1:]), n[0] * u[h][0]) for h in hs]
        for k in ks:
            fk = a[k] * p[k] + q0 + (q[0] * u[0][k] + q[1] * u[1][k] + q[2] * u[2][k])
            acc[l, k] += fk * f1[k]
            acc[2 + l, k] += fk * fs[i, SF2 + k]
            for h in hs:
                acc[l, FAN * (h + 1) + k] += n[k] * e[h] + f[k] * q[h]
                acc[2 + l, FAN * (h + 1) + k] += f1[k] * q[h]
        return z

    def clear():
        def zero(i, z):
            acc[i] = jnp.zeros((24, 8, 128), F32)
            return z
        lax.fori_loop(0, 8, zero, 0)

    one_row = lax.broadcasted_iota(jnp.int32, (32, 192), 0)
    one_col = lax.broadcasted_iota(jnp.int32, (32, 192), 1) // 8
    ones = jnp.where((one_row % 8 < FAN) & (one_row // 8 * FAN + one_row % 8 == one_col), 1.0, 0.0).astype(BF16)

    def fold(v):
        out = []
        for l in range(2):
            hi, mid, lo = split3(acc[2 * v + l].reshape(192, 128))
            out.append((mm(ones, lo) + mm(ones, mid)) + mm(ones, hi))
        return jnp.concatenate(out, axis=1)

    clear()
    lax.fori_loop(0, 16, base_pass, 0, unroll=2)
    first, second = fold(0), fold(1)
    alpha, beta = first[0:8], second[0:8]
    force = [first[8 * h + 8 : 8 * h + 16] for h in hs]
    cross = [second[8 * h + 8 : 8 * h + 16] for h in hs]
    uv = unit[0] * force[0] + unit[1] * force[1] + unit[2] * force[2]
    sums[0] = alpha
    sums[1] = beta
    sums[2] = uv
    for h in hs:
        sums[3 + h] = force[h]
        sums[6 + h] = cross[h]

    def hvp(i, z):
        v = i // 16
        ch = lax.rem(i, 16)
        vl = 2 * v + ch // 8
        l = ch // 8
        f = [fs[ch, SF + k] for k in ks]
        rp = [bv[vl, k] for k in ks]
        u = lambda h, k: ub[l, h * FAN + k]
        du = lambda h, k: bv[vl, (h + 1) * FAN + k]
        df = [fs[ch, SF1 + k] * rp[k] for k in ks]
        de0 = sum(df[1:], df[0])
        de = []
        for h in hs:
            total = df[0] * u(h, 0) + f[0] * du(h, 0)
            for k in ks[1:]:
                total = total + (df[k] * u(h, k) + f[k] * du(h, k))
            de.append(total)
        e = [fs[ch, SE + h] for h in hs]
        dn, dfeat, n = [], [], []
        for k in ks:
            dp = de0
            for h in hs:
                dp = dp + (de[h] * u(h, k) + e[h] * du(h, k))
            pk, ak = fs[ch, SP + k], fs[ch, SA + k]
            da = fs[ch, SBP + k] * rp[k] + fs[ch, SB + k] * dp
            dn.append(da * f[k] + ak * df[k])
            n.append(fs[ch, SN + k])
            dfeat.append(da * pk + ak * dp)
        dq0 = sum(dn[1:], dn[0])
        dq = []
        for h in hs:
            total = dn[0] * u(h, 0) + n[0] * du(h, 0)
            for k in ks[1:]:
                total = total + (dn[k] * u(h, k) + n[k] * du(h, k))
            dq.append(total)
        for k in ks:
            tot = dfeat[k] + dq0 + (dq[0] * u(0, k) + dq[1] * u(1, k) + dq[2] * u(2, k))
            acc[vl, k] += fs[ch, SF1 + k] * tot
            for h in hs:
                acc[vl, FAN * (h + 1) + k] += (dn[k] * e[h] + n[k] * de[h]) + f[k] * dq[h]
        return z

    grs[12:16] = jnp.zeros((4, 8, ATOMS), F32)

    def finish_hvp():
        u3 = [geo[h] for h in hs]
        ir = geo[4]
        for v in range(4):
            got = fold(v)
            dv = [dt[4 * c + v] for c in range(3)]
            rp = u3[0] * dv[0] + u3[1] * dv[1] + u3[2] * dv[2]
            du = [(dv[h] - u3[h] * rp) * ir for h in hs]
            al, be, w0 = sums[0], sums[1], sums[2]
            fo = [sums[3 + h] for h in hs]
            cr = [sums[6 + h] for h in hs]
            dal = got[0:8] + be * rp + (cr[0] * du[0] + cr[1] * du[1] + cr[2] * du[2])
            dfo = [got[8 * h + 8 : 8 * h + 16] + rp * cr[h] for h in hs]
            duv = sum((du[h] * fo[h] + u3[h] * dfo[h] for h in hs[1:]), du[0] * fo[0] + u3[0] * dfo[0])
            back = rp * ir
            for h in hs:
                val = dal * u3[h] + al * du[h]
                val = val + ir * ((dfo[h] - du[h] * w0 - u3[h] * duv) - back * (fo[h] - u3[h] * w0))
                grs[4 * h + v] = val
        for k in ks:
            cb[:, ATOMS * k : ATOMS * k + ATOMS] = rows3(grs[:, k, :])

    def scatter(at):
        return sum3(mm(cb[...], inc_t[:, at]))

    def give_back(i):
        finish_hvp()
        pack_back(i, scatter(pl.ds(256, COLS - 256)))
        halo_send(i, 1)
        return scatter(pl.ds(0, 256))

    def combine_all(dst, cols, src, minus=None):
        for c in range(3):
            got = combine(cols, src, c)
            dst[4 * c : 4 * c + 4, :] = got if minus is None else minus[4 * c : 4 * c + 4, :] - got

    def transposed(proj):
        return [place([proj[u][w] for w in range(4)]) for u in range(4)]

    clear()
    lax.fori_loop(0, 64, hvp, 0, unroll=2)
    low, inv = cholesky(entries(ar_recv(0, 1), 0))
    cols0 = columns_of(inv)
    local = give_back(1)
    combine_all(v1, cols0, own)
    w1[12:16, :] = jnp.zeros((4, ATOMS), F32)
    halo_wait(1)
    own[...] = local + unpack_back(1)
    combine_all(w1, cols0, own)
    pack(2, w1[...])
    halo_send(2, -1)
    ar_send(1, 0, jnp.concatenate([gram_rows(v1, w1), zeros4], axis=0))
    tab[:, 0:256] = w1[...]
    clear()
    ar_send(1, 1, ar_recv(1, 0))
    halo_wait(2)
    unpack(2, tab, False)

    gather(tab[...])
    tangents(1)
    lax.fori_loop(0, 16, hvp, 0, unroll=2)
    proj = entries(ar_recv(1, 1), 0)
    cols_a = transposed(proj)
    combine_all(r1, cols_a, v1, w1)
    ar_send(2, 0, jnp.concatenate([gram_rows(r1, r1), zeros4], axis=0))
    small_ref[0] = matrix(lambda u, w: proj[u][w])
    lax.fori_loop(16, 64, hvp, 0, unroll=2)
    ar_send(2, 1, ar_recv(2, 0))
    local = give_back(3)
    low, inv = cholesky(entries(ar_recv(2, 1), 0))
    cols1 = columns_of(inv)
    small_ref[2] = matrix(lambda u, w: low[w][u] if w >= u else None)
    combine_all(v2, cols1, r1)
    for i in range(4):
        halo_all(i).wait_send()
    for i in range(3):
        for g in range(2):
            ar_all(i, g).wait_send()
    halo_wait(3)
    own[...] = local + unpack_back(3)
    combine_all(r1, cols_a, w1, own)
    combine_all(own, cols1, r1)
    gram_w = pltpu.roll(jnp.concatenate([gram_rows(own, own), zeros4], axis=0), 4, 1)
    tile = jnp.concatenate([gram_rows(v2, own), gram_rows(v1, own)], axis=0) + gram_w
    for g in range(2):
        ar_send(3, g, tile)
        tile = ar_recv(3, g)
    proj = entries(tile, 0)
    prev = entries(tile, 4)
    gram = entries(pltpu.roll(tile, 124, 1), 0)
    for u in range(4):
        for w in range(u + 1):
            total = gram[u][w]
            for m in range(4):
                total = total - (proj[m][u] * proj[m][w] + prev[m][u] * prev[m][w])
            gram[u][w] = total
    combine_all(r1, transposed(proj), v2, own)
    combine_all(own, transposed(prev), v1, r1)
    low, inv = cholesky(gram)
    cols = columns_of(inv)
    for c in range(3):
        next_ref[c] = combine(cols, own, c)
    small_ref[1] = matrix(lambda u, w: proj[u][w])
    small_ref[3] = matrix(lambda u, w: low[w][u] if w >= u else None)
    for g in range(2):
        ar_all(3, g).wait_send()


def solution(mesh):
    sizes = tuple(mesh.shape[a] for a in AXES)
    cst = constants()
    slots = 2 * sizes[0] + sizes[1] * sizes[2] // 2

    def on_device(positions, species, start_block, neighbors, ghost_lists, embedding, radial_in, radial_out, readout):
        vmem = pl.BlockSpec(memory_space=pltpu.VMEM)
        vm = lambda *shape: pltpu.VMEM(shape, F32)
        dma = lambda *shape: pltpu.SemaphoreType.DMA(shape)
        operands = (
            positions.reshape(3, 1, ATOMS), species.reshape(1, ATOMS),
            jnp.transpose(start_block[0, 0, 0], (1, 0, 2)), neighbors.reshape(FAN, 1, ATOMS),
            ghost_lists, embedding, radial_in, radial_out.T, readout[None], jnp.asarray(cst),
        )
        out = pl.pallas_call(
            functools.partial(kernel, sizes),
            out_shape=(
                jax.ShapeDtypeStruct((3, 4, ATOMS), F32),
                jax.ShapeDtypeStruct((4, 4, 4), F32),
            ),
            in_specs=[pl.BlockSpec(memory_space=pltpu.HBM)] * 10,
            out_specs=(vmem, vmem),
            scratch_shapes=[dma(10)]
            + [pltpu.VMEM(x.shape, x.dtype) for x in operands]
            + [
                vm(ROWS, ATOMS),
                pltpu.VMEM((COLS, FAN * ATOMS), BF16),
                pltpu.VMEM((FAN * ATOMS, COLS), BF16),
                vm(ROWS, COLS),
                vm(ROWS, ATOMS), vm(ROWS, ATOMS), vm(ROWS, ATOMS), vm(ROWS, ATOMS),
                vm(ROWS, 8, ATOMS), vm(ROWS, 8, ATOMS),
                vm(6, 8, ATOMS), vm(9, 8, ATOMS),
                vm(2, 18, 8, 128), vm(8, 24, 8, 128),
                vm(16, 51, 8, 128), vm(8, 24, 8, 128),
                vm(CH, ATOMS), vm(4, 128, 128),
                pltpu.VMEM((CH, 3 * HID), BF16), vm(CH, 128),
                pltpu.VMEM((ATOMS, 128), BF16), pltpu.VMEM((8, 128), jnp.int32),
                pltpu.VMEM((3 * ROWS, FAN * ATOMS), BF16),
                vm(4, GHOST, 256), vm(4, GHOST, 256),
                vm(4, slots, 8, 128),
                dma(4), dma(4), dma(4, 2), dma(4, 2),
            ],
            compiler_params=pltpu.CompilerParams(
                collective_id=0, has_side_effects=True, vmem_limit_bytes=48 * 1024 * 1024
            ),
        )(*(pltpu.with_memory_space_constraint(x, pltpu.HBM) for x in operands))
        return jnp.transpose(out[0], (1, 0, 2))[None, None, None], out[1][:2], out[1][2:]

    return jax.shard_map(
        on_device,
        mesh=mesh,
        in_specs=(
            P("gx", "gy", "gz", None, None),
            P("gx", "gy", "gz", None),
            P("gx", "gy", "gz", None, None, None),
            P("gx", "gy", "gz", None, None),
            P("gx", "gy", "gz", None),
            P(), P(), P(), P(),
        ),
        out_specs=(P("gx", "gy", "gz", None, None, None), P(), P()),
        check_vma=False,
    )
```

```python
import functools
import itertools
import math

import jax
import jax.numpy as jnp
import numpy as np
from jax import lax
from jax.experimental import pallas as pl
from jax.experimental.pallas import tpu as pltpu
from jax.sharding import PartitionSpec as P

AXES = ("gx", "gy", "gz")
SOFTEN = 0.25
CUTOFF = 4.0
F32 = jnp.float32
BF16 = jnp.bfloat16
ATOMS = 256
FAN = 6
CH = 64
HID = 128
NB = 8
COLS = 1152
ROWS = 16
HIGHEST = lax.Precision.HIGHEST
MESH = pl.DeviceIdType.MESH

SF, SF1, SF2, SP, SA, SB, SE, SN, SBP = 0, 6, 12, 18, 24, 30, 36, 39, 45


def neighbour_cells():
    shifts = [s for s in itertools.product((-1, 0, 1), repeat=3) if any(s)]
    shifts.sort(key=lambda s: sum(map(abs, s)))
    out, first = [], 0
    for s in shifts:
        octants = list(itertools.product(*[{1: (0,), -1: (1,), 0: (0, 1)}[x] for x in s]))
        out.append((s, first, octants))
        first += len(octants)
    return out


CELLS = neighbour_cells()
GHOST = 56


def constants():
    order = {}
    for number in range(64):
        m = (number // 16, number // 4 % 4, number % 4)
        if not all(x in (1, 2) for x in m):
            order[m] = len(order)
    out = np.zeros((32, 128), np.float32)
    ids = list(range(256))
    moves = []
    octant_of = []
    for s, _, octants in CELLS:
        for o in octants:
            m = tuple(2 * x + y + 1 for x, y in zip(s, o))
            ids += [256 + 16 * order[m] + r for r in range(16)]
            moves += [s] * 16
            octant_of.append(4 * o[0] + 2 * o[1] + o[2])
    assert sorted(ids) == list(range(COLS))
    out[0:9] = np.array(ids).reshape(9, 128)
    out[9] = -1.0
    out[9, :GHOST] = octant_of
    out[10:31] = np.array(moves).T.reshape(21, 128)
    return out


def split3(x):
    high = x.astype(BF16)
    rest = x - high.astype(F32)
    mid = rest.astype(BF16)
    low = (rest - mid.astype(F32)).astype(BF16)
    return high, mid, low


def stack(parts):
    return jnp.concatenate([x.astype(F32) for x in parts], axis=0).astype(BF16)


def rows3(x):
    return stack(split3(x))


def sum3(y):
    n = y.shape[0] // 3
    return (y[2 * n :] + y[n : 2 * n]) + y[:n]


def mm(a, b, contract=((1,), (0,))):
    return lax.dot_general(a, b, (contract, ((), ())), preferred_element_type=F32)


def mm_high(a, b):
    return jnp.dot(a, b, precision=HIGHEST, preferred_element_type=F32)


def sin_cos(x):
    q = jnp.floor(x * (2.0 / math.pi) + 0.5)
    y = x - q * 1.5703125
    y = y - q * 4.837512969970703125e-4
    y = y - q * 7.549789948768648e-8
    y2 = y * y
    s = y + y * y2 * (-1.6666654611e-1 + y2 * (8.3321608736e-3 - y2 * 1.9515295891e-4))
    c = 1.0 - 0.5 * y2 + y2 * y2 * (4.166664568298827e-2 + y2 * (-1.388731625493765e-3 + y2 * 2.443315711809948e-5))
    h = q - 4.0 * jnp.floor(q * 0.25)
    odd = (h == 1.0) | (h == 3.0)
    ss = jnp.where(odd, c, s)
    cc = jnp.where(odd, s, c)
    ss = jnp.where(h >= 2.0, -ss, ss)
    cc = jnp.where((h == 1.0) | (h == 2.0), -cc, cc)
    return ss, cc


def kernel(
    sizes, *refs,
):
    hbm, (next_ref, small_ref) = refs[:10], refs[10:12]
    arrived, *local = refs[12:23]
    pos_ref, spc_ref, sb_ref, nbr_ref, gl_ref, emb_ref, rin_ref, rout_ref, rdo_ref, cst_ref = local
    (
        own, inc, inc_t, tab, v1, w1, r1, v2, dt, grs, geo, sums, ub, bv, fs, acc, epv, wpad, w2, embc, ghost, glw, cb,
        hs_buf, hr_buf, arb, hsend, hrecv, asend, arecv,
    ) = refs[23:]
    fetch = [pltpu.make_async_copy(a, b, arrived.at[n]) for n, (a, b) in enumerate(zip(hbm, local))]
    for copy in fetch:
        copy.start()
    gx, gy, gz = (lax.axis_index(a) for a in AXES)
    scale_ip = 1.0 / (3.0 * ATOMS * sizes[0] * sizes[1] * sizes[2])

    def beside(s):
        return {
            a: lax.rem(i + (x + n), n) for a, i, x, n in zip(AXES, (gx, gy, gz), s, sizes) if x
        }

    nx, ny, nz = sizes[0] // 2, sizes[1], sizes[2] // 2
    groups = (
        [o for o in itertools.product(range(nx), range(2), (0,), (0,), range(2)) if any(o)],
        [o for o in itertools.product((0,), (0,), range(ny), range(nz), (0,)) if any(o)],
    )
    starts = (0, len(groups[0]) + 1)

    def partner(o):
        a = lax.rem(gx // 2 + o[0], nx)
        b = lax.rem(lax.rem(gx, 2) + o[1], 2)
        c = lax.rem(gy + o[2], ny)
        d = lax.rem(gz // 2 + o[3], nz)
        e = lax.rem(lax.rem(gz, 2) + o[4], 2)
        return {"gx": 2 * a + b, "gy": c, "gz": 2 * d + e}, (4 * a + 2 * b + e, nz * c + d)

    far = sorted(CELLS, key=lambda x: -(5 * abs(x[0][2]) + 2 * abs(x[0][1]) + abs(x[0][0])))
    for group in groups:
        group.sort(key=lambda o: -(min(o[2], ny - o[2]) + min(o[3], nz - o[3]) + o[0] + 2 * o[4]))
    barrier = pltpu.get_barrier_semaphore()
    for s, _, _ in far:
        pl.semaphore_signal(barrier, inc=1, device_id=beside(s), device_id_type=MESH)
    for group in groups:
        for o in group:
            pl.semaphore_signal(barrier, inc=1, device_id=partner(o)[0], device_id_type=MESH)

    lane8 = lax.broadcasted_iota(jnp.int32, (8, 128), 1)
    sub8 = lax.broadcasted_iota(jnp.int32, (8, 128), 0)

    def ar_send(i, g, tile):
        mine = starts[g] + partner((0,) * 5)[1][g]
        arb[i, mine] = tile
        for o in groups[g]:
            pltpu.make_async_remote_copy(
                src_ref=arb.at[i, mine], dst_ref=arb.at[i, mine],
                send_sem=asend.at[i, g], recv_sem=arecv.at[i, g],
                device_id=partner(o)[0], device_id_type=MESH,
            ).start()

    def ar_all(i, g):
        part = arb.at[i, pl.ds(starts[g], len(groups[g]))]
        return pltpu.make_async_remote_copy(
            src_ref=part, dst_ref=part, send_sem=asend.at[i, g], recv_sem=arecv.at[i, g],
            device_id=partner(groups[g][0])[0], device_id_type=MESH,
        )

    def ar_recv(i, g):
        ar_all(i, g).wait_recv()
        parts = [arb[i, starts[g] + j] for j in range(len(groups[g]) + 1)]
        while len(parts) > 1:
            parts = [a + b for a, b in zip(parts[::2], parts[1::2])] + parts[len(parts) // 2 * 2 :]
        return parts[0]

    def halo_send(i, sign):
        for s, first, octants in far:
            at = pl.ds(first, len(octants))
            pltpu.make_async_remote_copy(
                src_ref=hs_buf.at[i, at], dst_ref=hr_buf.at[i, at],
                send_sem=hsend.at[i], recv_sem=hrecv.at[i],
                device_id=beside(tuple(sign * x for x in s)), device_id_type=MESH,
            ).start()

    def halo_all(i):
        return pltpu.make_async_remote_copy(
            src_ref=hs_buf.at[i], dst_ref=hr_buf.at[i], send_sem=hsend.at[i], recv_sem=hrecv.at[i],
            device_id=beside(CELLS[0][0]), device_id_type=MESH,
        )

    def halo_wait(i):
        halo_all(i).wait_recv()

    def turn(x):
        for b in (2, 1, 0):
            by = 1 << b
            sbit = (sub8 & by) != 0
            lbit = (lane8 & (16 * by)) != 0
            low = pltpu.roll(pltpu.roll(x, by, 0), 128 - 16 * by, 1)
            high = low if b == 2 else pltpu.roll(pltpu.roll(x, 8 - by, 0), 16 * by, 1)
            x = jnp.where(sbit == lbit, x, jnp.where(sbit, low, high))
        return x

    def pack(i, src):
        got = sum3(mm(rows3(src), ghost[...]))
        flat = jnp.concatenate([turn(got[0:8]), turn(got[8:16])], axis=1)
        hs_buf[i] = mm(spread, rows3(flat))

    def unpack(i, dst, shifted):
        for j in range(7):
            at = pl.ds(256 + 128 * j, 128)
            for t in range(2):
                part = turn(hr_buf[i, 8 * j : 8 * j + 8, 128 * t : 128 * t + 128])
                if t == 1 and shifted:
                    rows = [jnp.zeros((4, 128), F32)] + [cst_ref[10 + 7 * h + j : 11 + 7 * h + j, :] for h in range(3)]
                    part = part + jnp.concatenate(rows + [jnp.zeros((1, 128), F32)], axis=0)
                dst[8 * t : 8 * t + 8, at] = part

    def pack_back(i, con):
        for j in range(7):
            for t in range(2):
                part = con[8 * t : 8 * t + 8, 128 * j : 128 * j + 128]
                hs_buf[i, 8 * j : 8 * j + 8, 128 * t : 128 * t + 128] = turn(part)

    def unpack_back(i):
        hi, mid, lo = split3(hr_buf[i])
        flat = (mm(collect, lo) + mm(collect, mid)) + mm(collect, hi)
        both = jnp.concatenate([turn(flat[:, 0:128]), turn(flat[:, 128:256])], axis=0)
        return sum3(mm(rows3(both), ghost[...], ((1,), (1,))))

    def gram_rows(left, right):
        out = jnp.zeros((4, 128), F32)
        for w in range(4):
            prod = left[0:4, :] * right[w : w + 1, :]
            for c in (1, 2):
                prod = prod + left[4 * c : 4 * c + 4, :] * right[4 * c + w : 4 * c + w + 1, :]
            total = jnp.sum(prod, axis=1, keepdims=True) * scale_ip
            out = jnp.where(lane8[:4] == w, total, out)
        return out

    def entries(tile, row):
        out = [[None] * 4 for _ in range(4)]
        for w in range(4):
            col = jnp.broadcast_to(tile[:, w : w + 1], (8, 128))
            for u in range(4):
                out[u][w] = jnp.broadcast_to(col[row + u : row + u + 1, :], (8, 128))
        return out

    def place(vals):
        out = jnp.zeros((8, 128), F32)
        for n, val in enumerate(vals):
            if val is not None:
                out = jnp.where(sub8 == n, val, out)
        return out[0:4, 0:1]

    def matrix(get):
        out = jnp.zeros((8, 128), F32)
        for u in range(4):
            for w in range(4):
                val = get(u, w)
                if val is not None:
                    out = jnp.where((sub8 == u) & (lane8 == w), val, out)
        return out[0:4, 0:4]

    def cholesky(g):
        low = [[None] * 4 for _ in range(4)]
        inv_d = [None] * 4
        for j in range(4):
            total = g[j][j]
            for m in range(j):
                total = total - low[j][m] * low[j][m]
            inv_d[j] = lax.rsqrt(total)
            low[j][j] = total * inv_d[j]
            for u in range(j + 1, 4):
                total = g[u][j]
                for m in range(j):
                    total = total - low[u][m] * low[j][m]
                low[u][j] = total * inv_d[j]
        inv = [[None] * 4 for _ in range(4)]
        for j in range(4):
            inv[j][j] = inv_d[j]
            for u in range(j + 1, 4):
                total = low[u][j] * inv[j][j]
                for m in range(j + 1, u):
                    total = total + low[u][m] * inv[m][j]
                inv[u][j] = -total * inv_d[u]
        return low, inv

    def columns_of(mat):
        return [place([mat[u][w] for u in range(4)]) for w in range(4)]

    def combine(cols, src, c):
        total = cols[0] * src[4 * c : 4 * c + 1, :]
        for w in range(1, 4):
            total = total + cols[w] * src[4 * c + w : 4 * c + w + 1, :]
        return total

    for copy in fetch:
        copy.wait()

    for c in range(3):
        own[4 * c : 4 * c + 4, :] = sb_ref[c]
        own[12 + c : 13 + c, :] = pos_ref[c]
    own[15:16, :] = spc_ref[...].astype(F32)
    glw[...] = jnp.zeros((8, 128), jnp.int32)
    for n in range(8):
        glw[n : n + 1, 0:16] = gl_ref[n // 4, n // 2 % 2, n % 2 : n % 2 + 1, :]
    names = glw[0:1, :]
    for n in range(1, 8):
        names = names + pltpu.roll(glw[n : n + 1, :], 16 * n, 1)
    atom_rows = lax.broadcasted_iota(jnp.int32, (ATOMS, 128), 0)
    ghost[...] = jnp.where(atom_rows == names, 1.0, 0.0).astype(BF16)
    wpad[1] = jnp.zeros((128, 128), F32)
    wpad[1, 0:32, :] = cst_ref[...]
    wpad[1] = wpad[1].T
    octant_col = wpad[1, 0:GHOST, 9:10]
    lane24 = lax.rem(lax.broadcasted_iota(jnp.int32, (GHOST, 24), 1), 8).astype(F32)
    spread = jnp.where(lane24 == octant_col, 1.0, 0.0).astype(BF16)
    collect = jnp.where(sub8.astype(F32) == cst_ref[9:10, :], 1.0, 0.0).astype(BF16)[:, 0:GHOST]
    pack(0, own[...])
    zeros4 = jnp.zeros((4, 128), F32)
    tile = jnp.concatenate([gram_rows(own, own), zeros4], axis=0)

    pl.semaphore_wait(barrier, len(CELLS) + len(groups[0]) + len(groups[1]))
    halo_send(0, -1)
    ar_send(0, 0, tile)

    atom_lane = lax.broadcasted_iota(jnp.int32, (128, ATOMS), 1).astype(F32)

    def build(j, is_own):
        name = wpad[1, :, j : j + 1]
        for k in range(FAN):
            part = jnp.where(nbr_ref[k].astype(F32) == name, 1.0, 0.0)
            if is_own:
                part = part - jnp.where(atom_lane == name, 1.0, 0.0)
            inc[128 * j : 128 * j + 128, ATOMS * k : ATOMS * k + ATOMS] = part.astype(BF16)

    atom_sub = lax.broadcasted_iota(jnp.int32, (128, 128), 0).astype(F32)

    def build_t(k, l):
        at = pl.ds(ATOMS * k + 128 * l, 128)
        name = wpad[2 + l, :, k : k + 1]
        for j in range(9):
            entry = cst_ref[j : j + 1, :]
            part = jnp.where(entry == name, 1.0, 0.0)
            if j < 2:
                part = part - jnp.where(atom_sub + 128.0 * l == entry, 1.0, 0.0)
            inc_t[at, 128 * j : 128 * j + 128] = part.astype(BF16)

    wpad[0] = jnp.zeros((128, 128), F32)
    hi, mid, lo = (x.astype(F32) for x in split3(rin_ref[...]))
    for n, part in enumerate((hi, mid, lo, hi, mid, hi)):
        wpad[0, 8 * n : 8 * n + 8, :] = part
    wpad[0, 48:50, 0:CH] = emb_ref[...]
    wpad[0, 50:51, 0:CH] = rdo_ref[...]
    wpad[0] = wpad[0].T
    embc[:, 0:3] = wpad[0, 0:CH, 48:51]
    hi, mid, lo = split3(rout_ref[...])
    w2[...] = jnp.concatenate([hi, mid, hi], axis=1)
    epv[...] = jnp.where(own[15:16, :] < 0.5, embc[:, 0:1], embc[:, 1:2])
    for l in range(2):
        wpad[2 + l] = jnp.zeros((128, 128), F32)
        for k in range(FAN):
            wpad[2 + l, k : k + 1, :] = nbr_ref[k, :, 128 * l : 128 * l + 128].astype(F32)
        wpad[2 + l] = wpad[2 + l].T
    for j in range(9):
        build(j, j < 2)
    for k in range(FAN):
        for l in range(2):
            build_t(k, l)
    ar_send(0, 1, ar_recv(0, 0))
    tab[:, 0:256] = own[...]
    halo_wait(0)
    unpack(0, tab, True)

    def gather(src):
        got = sum3(mm(rows3(src), inc[...]))
        for k in range(FAN):
            for l in range(2):
                at = ATOMS * k + 128 * l
                dt[l, 16 * k : 16 * k + 16, :] = got[:, at : at + 128]

    def edge(n):
        return jnp.concatenate([dt[l, pl.ds(n, 8, stride=16), :] for l in range(2)], axis=1)

    gather(tab[...])

    d3 = [edge(12 + h) for h in range(3)]
    dist2 = d3[0] * d3[0] + d3[1] * d3[1] + d3[2] * d3[2]
    dist = jnp.sqrt(dist2 + SOFTEN)
    inv_r = 1.0 / dist
    unit = [d * inv_r for d in d3]
    for h in range(3):
        geo[h] = unit[h]
    geo[3] = dist
    geo[4] = inv_r
    geo[5] = edge(15) + own[15:16, :]
    for h in range(3):
        for k in range(FAN):
            row = jnp.broadcast_to(unit[h][k : k + 1, :], (8, ATOMS))
            for l in range(2):
                ub[l, h * FAN + k] = row[:, 128 * l : 128 * l + 128]

    def tangents(product):
        for v in range(4):
            dv = [edge(4 * c + v) for c in range(3)]
            rp = geo[0] * dv[0] + geo[1] * dv[1] + geo[2] * dv[2]
            parts = [rp] + [(dv[h] - geo[h] * rp) * geo[4] for h in range(3)]
            for g in range(4):
                for k in range(FAN):
                    row = jnp.broadcast_to(parts[g][k : k + 1, :], (8, ATOMS))
                    for l in range(2):
                        bv[2 * v + l, g * FAN + k] = row[:, 128 * l : 128 * l + 128]

    tangents(0)

    order8 = (lax.broadcasted_iota(jnp.int32, (8, ATOMS), 0) + 1).astype(F32) * (math.pi / CUTOFF)

    PAIR = 3
    order_w = jnp.concatenate([order8] * PAIR, axis=1)

    def features(pair, z):
        rows = [[geo[n, pl.ds(PAIR * pair + m, 1), :] for m in range(PAIR)] for n in (3, 4, 5)]
        r, ir, kind = (jnp.concatenate(x, axis=1) for x in rows)
        s, c = sin_cos(order_w * r)
        b0 = s * ir
        b1 = (order_w * c - b0) * ir
        b2 = -(order_w * order_w) * b0 - 2.0 * b1 * ir
        rin_t = wpad[0, :, 0:48].astype(BF16)

        def first(b):
            hi, mid, lo = split3(b)
            return mm(rin_t, stack([hi, hi, hi, mid, mid, lo]))

        def second(h):
            hi = h.astype(BF16)
            mid = (h - hi.astype(F32)).astype(BF16)
            return mm(w2[...], jnp.concatenate([hi, hi, mid], axis=0))

        z0, z1, z2 = first(b0), first(b1), first(b2)
        sg = 1.0 / (1.0 + jnp.exp(-z0))
        sd = sg * (1.0 - sg)
        s1 = sg + z0 * sd
        s2 = sd * (2.0 + z0 * (1.0 - 2.0 * sg))
        r0, r1_, r2 = second(z0 * sg), second(s1 * z1), second(s2 * z1 * z1 + s1 * z2)
        q = r * r * (1.0 / (CUTOFF * CUTOFF))
        sixth = FAN ** -0.5
        e0 = (1.0 - q) * (1.0 - q) * sixth
        e1 = (-4.0 / (CUTOFF * CUTOFF)) * r * (1.0 - q) * sixth
        e2 = (-4.0 / (CUTOFF * CUTOFF)) * (1.0 - 3.0 * q) * sixth
        w = jnp.concatenate([epv[...]] * PAIR, axis=1) * jnp.where(kind < 0.5, embc[:, 0:1], embc[:, 1:2])
        f0 = r0 * e0 * w
        f1 = (r1_ * e0 + r0 * e1) * w
        f2 = (r2 * e0 + 2.0 * r1_ * e1 + r0 * e2) * w
        for slot, val in ((SF, f0), (SF1, f1), (SF2, f2)):
            for m in range(PAIR):
                for l in range(2):
                    for t in range(8):
                        at = ATOMS * m + 128 * l
                        fs[8 * l + t, slot + PAIR * pair + m] = val[8 * t : 8 * t + 8, at : at + 128]
        return z

    lax.fori_loop(0, FAN // PAIR, features, 0)

    ks = range(FAN)
    hs = range(3)

    def base_pass(i, z):
        l = i // 8
        t = lax.rem(i, 8)
        f = [fs[i, SF + k] for k in ks]
        f1 = [fs[i, SF1 + k] for k in ks]
        u = [[ub[l, h * FAN + k] for k in ks] for h in hs]
        rho = jnp.broadcast_to(embc[pl.ds(pl.multiple_of(t * 8, 8), 8), 2:3], (8, 128))
        e0 = sum(f[1:], f[0])
        e = [sum((f[k] * u[h][k] for k in ks[1:]), f[0] * u[h][0]) for h in hs]
        p, a, n = [], [], []
        for k in ks:
            pk = e0 + (e[0] * u[0][k] + e[1] * u[1][k] + e[2] * u[2][k])
            m = f[k] * pk
            sg = 1.0 / (1.0 + jnp.exp(-m))
            sd = sg * (1.0 - sg)
            ak = rho * (sg + m * sd)
            fs[i, SP + k] = pk
            fs[i, SA + k] = ak
            bk = rho * (sd * (2.0 + m * (1.0 - 2.0 * sg)))
            nk = ak * f[k]
            fs[i, SB + k] = bk * f[k]
            fs[i, SBP + k] = bk * (f1[k] * pk)
            fs[i, SN + k] = nk
            p.append(pk)
            a.append(ak)
            n.append(nk)
        for h in hs:
            fs[i, SE + h] = e[h]
        q0 = sum(n[1:], n[0])
        q = [sum((n[k] * u[h][k] for k in ks[1:]), n[0] * u[h][0]) for h in hs]
        for k in ks:
            fk = a[k] * p[k] + q0 + (q[0] * u[0][k] + q[1] * u[1][k] + q[2] * u[2][k])
            acc[l, k] += fk * f1[k]
            acc[2 + l, k] += fk * fs[i, SF2 + k]
            for h in hs:
                acc[l, FAN * (h + 1) + k] += n[k] * e[h] + f[k] * q[h]
                acc[2 + l, FAN * (h + 1) + k] += f1[k] * q[h]
        return z

    def clear():
        def zero(i, z):
            acc[i] = jnp.zeros((24, 8, 128), F32)
            return z
        lax.fori_loop(0, 8, zero, 0)

    one_row = lax.broadcasted_iota(jnp.int32, (32, 192), 0)
    one_col = lax.broadcasted_iota(jnp.int32, (32, 192), 1) // 8
    ones = jnp.where((one_row % 8 < FAN) & (one_row // 8 * FAN + one_row % 8 == one_col), 1.0, 0.0).astype(BF16)

    def fold(v):
        out = []
        for l in range(2):
            hi, mid, lo = split3(acc[2 * v + l].reshape(192, 128))
            out.append((mm(ones, lo) + mm(ones, mid)) + mm(ones, hi))
        return jnp.concatenate(out, axis=1)

    clear()
    lax.fori_loop(0, 16, base_pass, 0, unroll=2)
    first, second = fold(0), fold(1)
    alpha, beta = first[0:8], second[0:8]
    force = [first[8 * h + 8 : 8 * h + 16] for h in hs]
    cross = [second[8 * h + 8 : 8 * h + 16] for h in hs]
    uv = unit[0] * force[0] + unit[1] * force[1] + unit[2] * force[2]
    sums[0] = alpha
    sums[1] = beta
    sums[2] = uv
    for h in hs:
        sums[3 + h] = force[h]
        sums[6 + h] = cross[h]

    def hvp(i, z):
        v = i // 16
        ch = lax.rem(i, 16)
        vl = 2 * v + ch // 8
        l = ch // 8
        f = [fs[ch, SF + k] for k in ks]
        rp = [bv[vl, k] for k in ks]
        u = lambda h, k: ub[l, h * FAN + k]
        du = lambda h, k: bv[vl, (h + 1) * FAN + k]
        df = [fs[ch, SF1 + k] * rp[k] for k in ks]
        de0 = sum(df[1:], df[0])
        de = []
        for h in hs:
            total = df[0] * u(h, 0) + f[0] * du(h, 0)
            for k in ks[1:]:
                total = total + (df[k] * u(h, k) + f[k] * du(h, k))
            de.append(total)
        e = [fs[ch, SE + h] for h in hs]
        dn, dfeat, n = [], [], []
        for k in ks:
            dp = de0
            for h in hs:
                dp = dp + (de[h] * u(h, k) + e[h] * du(h, k))
            pk, ak = fs[ch, SP + k], fs[ch, SA + k]
            da = fs[ch, SBP + k] * rp[k] + fs[ch, SB + k] * dp
            dn.append(da * f[k] + ak * df[k])
            n.append(fs[ch, SN + k])
            dfeat.append(da * pk + ak * dp)
        dq0 = sum(dn[1:], dn[0])
        dq = []
        for h in hs:
            total = dn[0] * u(h, 0) + n[0] * du(h, 0)
            for k in ks[1:]:
                total = total + (dn[k] * u(h, k) + n[k] * du(h, k))
            dq.append(total)
        for k in ks:
            tot = dfeat[k] + dq0 + (dq[0] * u(0, k) + dq[1] * u(1, k) + dq[2] * u(2, k))
            acc[vl, k] += fs[ch, SF1 + k] * tot
            for h in hs:
                acc[vl, FAN * (h + 1) + k] += (dn[k] * e[h] + n[k] * de[h]) + f[k] * dq[h]
        return z

    grs[...] = jnp.zeros((2, 128, 128), F32)

    def finish_hvp():
        u3 = [geo[h] for h in hs]
        ir = geo[4]
        for v in range(4):
            got = fold(v)
            dv = [edge(4 * c + v) for c in range(3)]
            rp = u3[0] * dv[0] + u3[1] * dv[1] + u3[2] * dv[2]
            du = [(dv[h] - u3[h] * rp) * ir for h in hs]
            al, be, w0 = sums[0], sums[1], sums[2]
            fo = [sums[3 + h] for h in hs]
            cr = [sums[6 + h] for h in hs]
            dal = got[0:8] + be * rp + (cr[0] * du[0] + cr[1] * du[1] + cr[2] * du[2])
            dfo = [got[8 * h + 8 : 8 * h + 16] + rp * cr[h] for h in hs]
            duv = sum((du[h] * fo[h] + u3[h] * dfo[h] for h in hs[1:]), du[0] * fo[0] + u3[0] * dfo[0])
            back = rp * ir
            for h in hs:
                val = dal * u3[h] + al * du[h]
                val = val + ir * ((dfo[h] - du[h] * w0 - u3[h] * duv) - back * (fo[h] - u3[h] * w0))
                for l in range(2):
                    grs[l, pl.ds(4 * h + v, 8, stride=16), :] = val[:, 128 * l : 128 * l + 128]
        for k in ks:
            cb[:, ATOMS * k : ATOMS * k + ATOMS] = rows3(jnp.concatenate([grs[l, 16 * k : 16 * k + 16, :] for l in range(2)], axis=1))

    def scatter(at):
        return sum3(mm(cb[...], inc_t[:, at]))

    def give_back(i):
        finish_hvp()
        pack_back(i, scatter(pl.ds(256, COLS - 256)))
        halo_send(i, 1)
        return scatter(pl.ds(0, 256))

    def combine_all(dst, cols, src, minus=None):
        for c in range(3):
            got = combine(cols, src, c)
            dst[4 * c : 4 * c + 4, :] = got if minus is None else minus[4 * c : 4 * c + 4, :] - got

    def transposed(proj):
        return [place([proj[u][w] for w in range(4)]) for u in range(4)]

    def less(gram, *projs):
        out = [[None] * 4 for _ in range(4)]
        for u in range(4):
            for w in range(u + 1):
                total = gram[u][w]
                for proj in projs:
                    for m in range(4):
                        total = total - proj[m][u] * proj[m][w]
                out[u][w] = total
        return out

    clear()
    lax.fori_loop(0, 64, hvp, 0, unroll=2)
    local = give_back(1)
    low, inv0 = cholesky(entries(ar_recv(0, 1), 0))
    cols0 = columns_of(inv0)
    combine_all(v1, cols0, own)
    halo_wait(1)
    own[...] = local + unpack_back(1)
    pack(2, own[...])
    halo_send(2, -1)
    combine_all(w1, cols0, own)
    tile = gram_rows(v1, w1) + pltpu.roll(gram_rows(w1, w1), 4, 1)
    ar_send(1, 0, jnp.concatenate([tile, zeros4], axis=0))
    tab[:, 0:256] = own[...]
    clear()
    ar_send(1, 1, ar_recv(1, 0))
    halo_wait(2)
    unpack(2, tab, False)

    gather(tab[...])
    tangents(1)
    lax.fori_loop(0, 64, hvp, 0, unroll=2)
    local = give_back(3)
    tile = ar_recv(1, 1)
    proj = entries(tile, 0)
    low, inv = cholesky(less(entries(pltpu.roll(tile, 124, 1), 0), proj))
    small_ref[0] = matrix(lambda u, w: proj[u][w])
    small_ref[2] = matrix(lambda u, w: low[w][u] if w >= u else None)
    cols1, cols_a = columns_of(inv), transposed(proj)
    combine_all(r1, cols_a, v1, w1)
    combine_all(v2, cols1, r1)
    combine_all(r1, cols_a, w1)
    combine_all(w1, cols1, r1)
    both = [[None] * 4 for _ in range(4)]
    for u in range(4):
        for w in range(u + 1):
            both[u][w] = sum((inv[u][m] * inv0[m][w] for m in range(w + 1, u + 1)), inv[u][w] * inv0[w][w])
    cols01 = columns_of(both)
    for i in range(4):
        halo_all(i).wait_send()
    for i in range(2):
        for g in range(2):
            ar_all(i, g).wait_send()
    halo_wait(3)
    tab[:, 0:256] = local + unpack_back(3)
    combine_all(own, cols01, tab.at[:, 0:256])
    own[0:12, :] = own[0:12, :] - w1[0:12, :]
    gram_w = pltpu.roll(jnp.concatenate([gram_rows(own, own), zeros4], axis=0), 4, 1)
    tile = jnp.concatenate([gram_rows(v2, own), gram_rows(v1, own)], axis=0) + gram_w
    for g in range(2):
        ar_send(2, g, tile)
        tile = ar_recv(2, g)
    proj = entries(tile, 0)
    prev = entries(tile, 4)
    gram = less(entries(pltpu.roll(tile, 124, 1), 0), proj, prev)
    combine_all(r1, transposed(proj), v2, own)
    combine_all(own, transposed(prev), v1, r1)
    low, inv = cholesky(gram)
    cols = columns_of(inv)
    for c in range(3):
        next_ref[c] = combine(cols, own, c)
    small_ref[1] = matrix(lambda u, w: proj[u][w])
    small_ref[3] = matrix(lambda u, w: low[w][u] if w >= u else None)
    for g in range(2):
        ar_all(2, g).wait_send()


def solution(mesh):
    sizes = tuple(mesh.shape[a] for a in AXES)
    cst = constants()
    slots = 2 * sizes[0] + sizes[1] * sizes[2] // 2

    def on_device(positions, species, start_block, neighbors, ghost_lists, embedding, radial_in, radial_out, readout):
        vmem = pl.BlockSpec(memory_space=pltpu.VMEM)
        vm = lambda *shape: pltpu.VMEM(shape, F32)
        dma = lambda *shape: pltpu.SemaphoreType.DMA(shape)
        operands = (
            positions.reshape(3, 1, ATOMS), species.reshape(1, ATOMS),
            jnp.transpose(start_block[0, 0, 0], (1, 0, 2)), neighbors.reshape(FAN, 1, ATOMS),
            ghost_lists, embedding, radial_in, radial_out.T, readout[None], jnp.asarray(cst),
        )
        out = pl.pallas_call(
            functools.partial(kernel, sizes),
            out_shape=(
                jax.ShapeDtypeStruct((3, 4, ATOMS), F32),
                jax.ShapeDtypeStruct((4, 4, 4), F32),
            ),
            in_specs=[pl.BlockSpec(memory_space=pltpu.HBM)] * 10,
            out_specs=(vmem, vmem),
            scratch_shapes=[dma(10)]
            + [pltpu.VMEM(x.shape, x.dtype) for x in operands]
            + [
                vm(ROWS, ATOMS),
                pltpu.VMEM((COLS, FAN * ATOMS), BF16),
                pltpu.VMEM((FAN * ATOMS, COLS), BF16),
                vm(ROWS, COLS),
                vm(ROWS, ATOMS), vm(ROWS, ATOMS), vm(ROWS, ATOMS), vm(ROWS, ATOMS),
                vm(2, 128, 128), vm(2, 128, 128),
                vm(6, 8, ATOMS), vm(9, 8, ATOMS),
                vm(2, 18, 8, 128), vm(8, 24, 8, 128),
                vm(16, 51, 8, 128), vm(8, 24, 8, 128),
                vm(CH, ATOMS), vm(4, 128, 128),
                pltpu.VMEM((CH, 3 * HID), BF16), vm(CH, 128),
                pltpu.VMEM((ATOMS, 128), BF16), pltpu.VMEM((8, 128), jnp.int32),
                pltpu.VMEM((3 * ROWS, FAN * ATOMS), BF16),
                vm(4, GHOST, 256), vm(4, GHOST, 256),
                vm(3, slots, 8, 128),
                dma(4), dma(4), dma(3, 2), dma(3, 2),
            ],
            compiler_params=pltpu.CompilerParams(
                collective_id=0, has_side_effects=True, vmem_limit_bytes=48 * 1024 * 1024
            ),
        )(*(pltpu.with_memory_space_constraint(x, pltpu.HBM) for x in operands))
        return jnp.transpose(out[0], (1, 0, 2))[None, None, None], out[1][:2], out[1][2:]

    return jax.shard_map(
        on_device,
        mesh=mesh,
        in_specs=(
            P("gx", "gy", "gz", None, None),
            P("gx", "gy", "gz", None),
            P("gx", "gy", "gz", None, None, None),
            P("gx", "gy", "gz", None, None),
            P("gx", "gy", "gz", None),
            P(), P(), P(), P(),
        ),
        out_specs=(P("gx", "gy", "gz", None, None, None), P(), P()),
        check_vma=False,
    )
```

```python
import functools
import itertools
import math

import jax
import jax.numpy as jnp
import numpy as np
from jax import lax
from jax.experimental import pallas as pl
from jax.experimental.pallas import tpu as pltpu
from jax.sharding import PartitionSpec as P

AXES = ("gx", "gy", "gz")
SOFTEN = 0.25
CUTOFF = 4.0
F32 = jnp.float32
BF16 = jnp.bfloat16
ATOMS = 256
FAN = 6
CH = 64
HID = 128
NB = 8
COLS = 1152
ROWS = 16
HIGHEST = lax.Precision.HIGHEST
MESH = pl.DeviceIdType.MESH

SF, SF1, SF2, SP, SA, SB, SE, SN, SBP = 0, 6, 12, 18, 24, 30, 36, 39, 45


def neighbour_cells():
    shifts = [s for s in itertools.product((-1, 0, 1), repeat=3) if any(s)]
    shifts.sort(key=lambda s: sum(map(abs, s)))
    out, first = [], 0
    for s in shifts:
        octants = list(itertools.product(*[{1: (0,), -1: (1,), 0: (0, 1)}[x] for x in s]))
        out.append((s, first, octants))
        first += len(octants)
    return out


CELLS = neighbour_cells()
GHOST = 56


def constants():
    order = {}
    for number in range(64):
        m = (number // 16, number // 4 % 4, number % 4)
        if not all(x in (1, 2) for x in m):
            order[m] = len(order)
    out = np.zeros((32, 128), np.float32)
    ids = list(range(256))
    moves = []
    octant_of = []
    for s, _, octants in CELLS:
        for o in octants:
            m = tuple(2 * x + y + 1 for x, y in zip(s, o))
            ids += [256 + 16 * order[m] + r for r in range(16)]
            moves += [s] * 16
            octant_of.append(4 * o[0] + 2 * o[1] + o[2])
    assert sorted(ids) == list(range(COLS))
    out[0:9] = np.array(ids).reshape(9, 128)
    out[9] = -1.0
    out[9, :GHOST] = octant_of
    out[10:31] = np.array(moves).T.reshape(21, 128)
    return out


def split3(x):
    high = x.astype(BF16)
    rest = x - high.astype(F32)
    mid = rest.astype(BF16)
    low = (rest - mid.astype(F32)).astype(BF16)
    return high, mid, low


def stack(parts):
    return jnp.concatenate([x.astype(F32) for x in parts], axis=0).astype(BF16)


def rows3(x):
    return stack(split3(x))


def sum3(y):
    n = y.shape[0] // 3
    return (y[2 * n :] + y[n : 2 * n]) + y[:n]


def mm(a, b, contract=((1,), (0,))):
    return lax.dot_general(a, b, (contract, ((), ())), preferred_element_type=F32)


def mm_high(a, b):
    return jnp.dot(a, b, precision=HIGHEST, preferred_element_type=F32)


def sin_cos(x):
    q = jnp.floor(x * (2.0 / math.pi) + 0.5)
    y = x - q * 1.5703125
    y = y - q * 4.837512969970703125e-4
    y = y - q * 7.549789948768648e-8
    y2 = y * y
    s = y + y * y2 * (-1.6666654611e-1 + y2 * (8.3321608736e-3 - y2 * 1.9515295891e-4))
    c = 1.0 - 0.5 * y2 + y2 * y2 * (4.166664568298827e-2 + y2 * (-1.388731625493765e-3 + y2 * 2.443315711809948e-5))
    h = q - 4.0 * jnp.floor(q * 0.25)
    odd = (h == 1.0) | (h == 3.0)
    ss = jnp.where(odd, c, s)
    cc = jnp.where(odd, s, c)
    ss = jnp.where(h >= 2.0, -ss, ss)
    cc = jnp.where((h == 1.0) | (h == 2.0), -cc, cc)
    return ss, cc


def kernel(
    sizes, *refs,
):
    hbm, (next_ref, small_ref) = refs[:10], refs[10:12]
    arrived, *local = refs[12:23]
    pos_ref, spc_ref, sb_ref, nbr_ref, gl_ref, emb_ref, rin_ref, rout_ref, rdo_ref, cst_ref = local
    (
        own, inc, inc_t, tab, v1, w1, r1, v2, dt, grs, geo, sums, ub, bv, fs, acc, epv, wpad, w2, embc, ghost, glw, cb,
        hs_buf, hr_buf, arb, hsend, hrecv, asend, arecv,
    ) = refs[23:]
    fetch = [pltpu.make_async_copy(a, b, arrived.at[n]) for n, (a, b) in enumerate(zip(hbm, local))]
    for copy in fetch:
        copy.start()
    gx, gy, gz = (lax.axis_index(a) for a in AXES)
    scale_ip = 1.0 / (3.0 * ATOMS * sizes[0] * sizes[1] * sizes[2])

    def beside(s):
        return {
            a: lax.rem(i + (x + n), n) for a, i, x, n in zip(AXES, (gx, gy, gz), s, sizes) if x
        }

    nx, ny, nz = sizes[0] // 2, sizes[1], sizes[2] // 2
    groups = (
        [o for o in itertools.product(range(nx), range(2), (0,), (0,), range(2)) if any(o)],
        [o for o in itertools.product((0,), (0,), range(ny), range(nz), (0,)) if any(o)],
    )
    starts = (0, len(groups[0]) + 1)

    def partner(o):
        a = lax.rem(gx // 2 + o[0], nx)
        b = lax.rem(lax.rem(gx, 2) + o[1], 2)
        c = lax.rem(gy + o[2], ny)
        d = lax.rem(gz // 2 + o[3], nz)
        e = lax.rem(lax.rem(gz, 2) + o[4], 2)
        return {"gx": 2 * a + b, "gy": c, "gz": 2 * d + e}, (4 * a + 2 * b + e, nz * c + d)

    far = sorted(CELLS, key=lambda x: -(5 * abs(x[0][2]) + 2 * abs(x[0][1]) + abs(x[0][0])))
    for group in groups:
        group.sort(key=lambda o: -(min(o[2], ny - o[2]) + min(o[3], nz - o[3]) + o[0] + 2 * o[4]))
    barrier = pltpu.get_barrier_semaphore()
    for s, _, _ in far:
        pl.semaphore_signal(barrier, inc=1, device_id=beside(s), device_id_type=MESH)
    for group in groups:
        for o in group:
            pl.semaphore_signal(barrier, inc=1, device_id=partner(o)[0], device_id_type=MESH)

    lane8 = lax.broadcasted_iota(jnp.int32, (8, 128), 1)
    sub8 = lax.broadcasted_iota(jnp.int32, (8, 128), 0)

    def ar_send(i, g, tile):
        mine = starts[g] + partner((0,) * 5)[1][g]
        arb[i, mine] = tile
        for o in groups[g]:
            pltpu.make_async_remote_copy(
                src_ref=arb.at[i, mine], dst_ref=arb.at[i, mine],
                send_sem=asend.at[i, g], recv_sem=arecv.at[i, g],
                device_id=partner(o)[0], device_id_type=MESH,
            ).start()

    def ar_all(i, g):
        part = arb.at[i, pl.ds(starts[g], len(groups[g]))]
        return pltpu.make_async_remote_copy(
            src_ref=part, dst_ref=part, send_sem=asend.at[i, g], recv_sem=arecv.at[i, g],
            device_id=partner(groups[g][0])[0], device_id_type=MESH,
        )

    def ar_recv(i, g):
        ar_all(i, g).wait_recv()
        parts = [arb[i, starts[g] + j] for j in range(len(groups[g]) + 1)]
        while len(parts) > 1:
            parts = [a + b for a, b in zip(parts[::2], parts[1::2])] + parts[len(parts) // 2 * 2 :]
        return parts[0]

    def halo_send(i, sign):
        for s, first, octants in far:
            at = pl.ds(first, len(octants))
            pltpu.make_async_remote_copy(
                src_ref=hs_buf.at[i, at], dst_ref=hr_buf.at[i, at],
                send_sem=hsend.at[i], recv_sem=hrecv.at[i],
                device_id=beside(tuple(sign * x for x in s)), device_id_type=MESH,
            ).start()

    def halo_all(i):
        return pltpu.make_async_remote_copy(
            src_ref=hs_buf.at[i], dst_ref=hr_buf.at[i], send_sem=hsend.at[i], recv_sem=hrecv.at[i],
            device_id=beside(CELLS[0][0]), device_id_type=MESH,
        )

    def halo_wait(i):
        halo_all(i).wait_recv()

    def turn(x):
        for b in (2, 1, 0):
            by = 1 << b
            sbit = (sub8 & by) != 0
            lbit = (lane8 & (16 * by)) != 0
            low = pltpu.roll(pltpu.roll(x, by, 0), 128 - 16 * by, 1)
            high = low if b == 2 else pltpu.roll(pltpu.roll(x, 8 - by, 0), 16 * by, 1)
            x = jnp.where(sbit == lbit, x, jnp.where(sbit, low, high))
        return x

    def pack(i, src):
        got = sum3(mm(rows3(src), ghost[...]))
        flat = jnp.concatenate([turn(got[0:8]), turn(got[8:16])], axis=1)
        hs_buf[i] = mm(spread, rows3(flat))

    def unpack(i, dst, shifted):
        for j in range(7):
            at = pl.ds(256 + 128 * j, 128)
            for t in range(2):
                part = turn(hr_buf[i, 8 * j : 8 * j + 8, 128 * t : 128 * t + 128])
                if t == 1 and shifted:
                    rows = [jnp.zeros((4, 128), F32)] + [cst_ref[10 + 7 * h + j : 11 + 7 * h + j, :] for h in range(3)]
                    part = part + jnp.concatenate(rows + [jnp.zeros((1, 128), F32)], axis=0)
                dst[8 * t : 8 * t + 8, at] = part

    def pack_back(i, con):
        for j in range(7):
            for t in range(2):
                part = con[8 * t : 8 * t + 8, 128 * j : 128 * j + 128]
                hs_buf[i, 8 * j : 8 * j + 8, 128 * t : 128 * t + 128] = turn(part)

    def unpack_back(i):
        hi, mid, lo = split3(hr_buf[i])
        flat = (mm(collect, lo) + mm(collect, mid)) + mm(collect, hi)
        both = jnp.concatenate([turn(flat[:, 0:128]), turn(flat[:, 128:256])], axis=0)
        return sum3(mm(rows3(both), ghost[...], ((1,), (1,))))

    def gram_rows(left, right):
        out = jnp.zeros((4, 128), F32)
        for w in range(4):
            prod = left[0:4, :] * right[w : w + 1, :]
            for c in (1, 2):
                prod = prod + left[4 * c : 4 * c + 4, :] * right[4 * c + w : 4 * c + w + 1, :]
            total = jnp.sum(prod, axis=1, keepdims=True) * scale_ip
            out = jnp.where(lane8[:4] == w, total, out)
        return out

    def entries(tile, row):
        out = [[None] * 4 for _ in range(4)]
        for w in range(4):
            col = jnp.broadcast_to(tile[:, w : w + 1], (8, 128))
            for u in range(4):
                out[u][w] = jnp.broadcast_to(col[row + u : row + u + 1, :], (8, 128))
        return out

    def place(vals):
        out = jnp.zeros((8, 128), F32)
        for n, val in enumerate(vals):
            if val is not None:
                out = jnp.where(sub8 == n, val, out)
        return out[0:4, 0:1]

    def matrix(get):
        out = jnp.zeros((8, 128), F32)
        for u in range(4):
            for w in range(4):
                val = get(u, w)
                if val is not None:
                    out = jnp.where((sub8 == u) & (lane8 == w), val, out)
        return out[0:4, 0:4]

    def cholesky(g):
        low = [[None] * 4 for _ in range(4)]
        inv_d = [None] * 4
        for j in range(4):
            total = g[j][j]
            for m in range(j):
                total = total - low[j][m] * low[j][m]
            inv_d[j] = lax.rsqrt(total)
            low[j][j] = total * inv_d[j]
            for u in range(j + 1, 4):
                total = g[u][j]
                for m in range(j):
                    total = total - low[u][m] * low[j][m]
                low[u][j] = total * inv_d[j]
        inv = [[None] * 4 for _ in range(4)]
        for j in range(4):
            inv[j][j] = inv_d[j]
            for u in range(j + 1, 4):
                total = low[u][j] * inv[j][j]
                for m in range(j + 1, u):
                    total = total + low[u][m] * inv[m][j]
                inv[u][j] = -total * inv_d[u]
        return low, inv

    def columns_of(mat):
        return [place([mat[u][w] for u in range(4)]) for w in range(4)]

    def combine(cols, src, c):
        total = cols[0] * src[4 * c : 4 * c + 1, :]
        for w in range(1, 4):
            total = total + cols[w] * src[4 * c + w : 4 * c + w + 1, :]
        return total

    for copy in fetch:
        copy.wait()

    for c in range(3):
        own[4 * c : 4 * c + 4, :] = sb_ref[c]
        own[12 + c : 13 + c, :] = pos_ref[c]
    own[15:16, :] = spc_ref[...].astype(F32)
    glw[...] = jnp.zeros((8, 128), jnp.int32)
    for n in range(8):
        glw[n : n + 1, 0:16] = gl_ref[n // 4, n // 2 % 2, n % 2 : n % 2 + 1, :]
    names = glw[0:1, :]
    for n in range(1, 8):
        names = names + pltpu.roll(glw[n : n + 1, :], 16 * n, 1)
    atom_rows = lax.broadcasted_iota(jnp.int32, (ATOMS, 128), 0)
    ghost[...] = jnp.where(atom_rows == names, 1.0, 0.0).astype(BF16)
    wpad[1] = jnp.zeros((128, 128), F32)
    wpad[1, 0:32, :] = cst_ref[...]
    wpad[1] = wpad[1].T
    octant_col = wpad[1, 0:GHOST, 9:10]
    lane24 = lax.rem(lax.broadcasted_iota(jnp.int32, (GHOST, 24), 1), 8).astype(F32)
    spread = jnp.where(lane24 == octant_col, 1.0, 0.0).astype(BF16)
    collect = jnp.where(sub8.astype(F32) == cst_ref[9:10, :], 1.0, 0.0).astype(BF16)[:, 0:GHOST]
    pack(0, own[...])
    zeros4 = jnp.zeros((4, 128), F32)
    tile = jnp.concatenate([gram_rows(own, own), zeros4], axis=0)

    pl.semaphore_wait(barrier, len(CELLS) + len(groups[0]) + len(groups[1]))
    halo_send(0, -1)
    ar_send(0, 0, tile)

    atom_lane = lax.broadcasted_iota(jnp.int32, (128, ATOMS), 1).astype(F32)

    def build(j, is_own):
        name = wpad[1, :, j : j + 1]
        for k in range(FAN):
            part = jnp.where(nbr_ref[k].astype(F32) == name, 1.0, 0.0)
            if is_own:
                part = part - jnp.where(atom_lane == name, 1.0, 0.0)
            inc[128 * j : 128 * j + 128, ATOMS * k : ATOMS * k + ATOMS] = part.astype(BF16)

    atom_sub = lax.broadcasted_iota(jnp.int32, (128, 128), 0).astype(F32)

    def build_t(k, l):
        at = pl.ds(ATOMS * k + 128 * l, 128)
        name = wpad[2 + l, :, k : k + 1]
        for j in range(9):
            entry = cst_ref[j : j + 1, :]
            part = jnp.where(entry == name, 1.0, 0.0)
            if j < 2:
                part = part - jnp.where(atom_sub + 128.0 * l == entry, 1.0, 0.0)
            inc_t[at, 128 * j : 128 * j + 128] = part.astype(BF16)

    wpad[0] = jnp.zeros((128, 128), F32)
    hi, mid, lo = (x.astype(F32) for x in split3(rin_ref[...]))
    for n, part in enumerate((hi, mid, lo, hi, mid, hi)):
        wpad[0, 8 * n : 8 * n + 8, :] = part
    wpad[0, 48:50, 0:CH] = emb_ref[...]
    wpad[0, 50:51, 0:CH] = rdo_ref[...]
    wpad[0] = wpad[0].T
    embc[:, 0:3] = wpad[0, 0:CH, 48:51]
    hi, mid, lo = split3(rout_ref[...])
    w2[...] = jnp.concatenate([hi, mid, hi], axis=1)
    epv[...] = jnp.where(own[15:16, :] < 0.5, embc[:, 0:1], embc[:, 1:2])
    for l in range(2):
        wpad[2 + l] = jnp.zeros((128, 128), F32)
        for k in range(FAN):
            wpad[2 + l, k : k + 1, :] = nbr_ref[k, :, 128 * l : 128 * l + 128].astype(F32)
        wpad[2 + l] = wpad[2 + l].T
    for j in range(9):
        build(j, j < 2)
    for k in range(FAN):
        for l in range(2):
            build_t(k, l)
    ar_send(0, 1, ar_recv(0, 0))
    tab[:, 0:256] = own[...]
    halo_wait(0)
    unpack(0, tab, True)

    def gather(src):
        got = sum3(mm(rows3(src), inc[...]))
        for k in range(FAN):
            for l in range(2):
                at = ATOMS * k + 128 * l
                dt[l, 16 * k : 16 * k + 16, :] = got[:, at : at + 128]

    def edge(n):
        return jnp.concatenate([dt[l, pl.ds(n, 8, stride=16), :] for l in range(2)], axis=1)

    gather(tab[...])

    d3 = [edge(12 + h) for h in range(3)]
    dist2 = d3[0] * d3[0] + d3[1] * d3[1] + d3[2] * d3[2]
    dist = jnp.sqrt(dist2 + SOFTEN)
    inv_r = 1.0 / dist
    unit = [d * inv_r for d in d3]
    for h in range(3):
        geo[h] = unit[h]
    geo[3] = dist
    geo[4] = inv_r
    geo[5] = edge(15) + own[15:16, :]
    for h in range(3):
        for k in range(FAN):
            row = jnp.broadcast_to(unit[h][k : k + 1, :], (8, ATOMS))
            for l in range(2):
                ub[l, h * FAN + k] = row[:, 128 * l : 128 * l + 128]

    def tangents(product):
        for v in range(4):
            dv = [edge(4 * c + v) for c in range(3)]
            rp = geo[0] * dv[0] + geo[1] * dv[1] + geo[2] * dv[2]
            parts = [rp] + [(dv[h] - geo[h] * rp) * geo[4] for h in range(3)]
            for g in range(4):
                for k in range(FAN):
                    row = jnp.broadcast_to(parts[g][k : k + 1, :], (8, ATOMS))
                    for l in range(2):
                        bv[2 * v + l, g * FAN + k] = row[:, 128 * l : 128 * l + 128]

    tangents(0)

    order8 = (lax.broadcasted_iota(jnp.int32, (8, ATOMS), 0) + 1).astype(F32) * (math.pi / CUTOFF)

    PAIR = 3
    order_w = jnp.concatenate([order8] * PAIR, axis=1)

    def features(pair, z):
        rows = [[geo[n, pl.ds(PAIR * pair + m, 1), :] for m in range(PAIR)] for n in (3, 4, 5)]
        r, ir, kind = (jnp.concatenate(x, axis=1) for x in rows)
        s, c = sin_cos(order_w * r)
        b0 = s * ir
        b1 = (order_w * c - b0) * ir
        b2 = -(order_w * order_w) * b0 - 2.0 * b1 * ir
        rin_t = wpad[0, :, 0:48].astype(BF16)

        def first(b):
            hi, mid, lo = split3(b)
            return mm(rin_t, stack([hi, hi, hi, mid, mid, lo]))

        def second(h):
            hi = h.astype(BF16)
            mid = (h - hi.astype(F32)).astype(BF16)
            return mm(w2[...], jnp.concatenate([hi, hi, mid], axis=0))

        z0, z1, z2 = first(b0), first(b1), first(b2)
        sg = 1.0 / (1.0 + jnp.exp(-z0))
        sd = sg * (1.0 - sg)
        s1 = sg + z0 * sd
        s2 = sd * (2.0 + z0 * (1.0 - 2.0 * sg))
        r0, r1_, r2 = second(z0 * sg), second(s1 * z1), second(s2 * z1 * z1 + s1 * z2)
        q = r * r * (1.0 / (CUTOFF * CUTOFF))
        sixth = FAN ** -0.5
        e0 = (1.0 - q) * (1.0 - q) * sixth
        e1 = (-4.0 / (CUTOFF * CUTOFF)) * r * (1.0 - q) * sixth
        e2 = (-4.0 / (CUTOFF * CUTOFF)) * (1.0 - 3.0 * q) * sixth
        w = jnp.concatenate([epv[...]] * PAIR, axis=1) * jnp.where(kind < 0.5, embc[:, 0:1], embc[:, 1:2])
        f0 = r0 * e0 * w
        f1 = (r1_ * e0 + r0 * e1) * w
        f2 = (r2 * e0 + 2.0 * r1_ * e1 + r0 * e2) * w
        for slot, val in ((SF, f0), (SF1, f1), (SF2, f2)):
            for m in range(PAIR):
                for l in range(2):
                    for t in range(8):
                        at = ATOMS * m + 128 * l
                        fs[8 * l + t, slot + PAIR * pair + m] = val[8 * t : 8 * t + 8, at : at + 128]
        return z

    lax.fori_loop(0, FAN // PAIR, features, 0)

    ks = range(FAN)
    hs = range(3)

    def base_pass(i, z):
        l = i // 8
        t = lax.rem(i, 8)
        f = [fs[i, SF + k] for k in ks]
        f1 = [fs[i, SF1 + k] for k in ks]
        u = [[ub[l, h * FAN + k] for k in ks] for h in hs]
        rho = jnp.broadcast_to(embc[pl.ds(pl.multiple_of(t * 8, 8), 8), 2:3], (8, 128))
        e0 = sum(f[1:], f[0])
        e = [sum((f[k] * u[h][k] for k in ks[1:]), f[0] * u[h][0]) for h in hs]
        p, a, n = [], [], []
        for k in ks:
            pk = e0 + (e[0] * u[0][k] + e[1] * u[1][k] + e[2] * u[2][k])
            m = f[k] * pk
            sg = 1.0 / (1.0 + jnp.exp(-m))
            sd = sg * (1.0 - sg)
            ak = rho * (sg + m * sd)
            fs[i, SP + k] = pk
            fs[i, SA + k] = ak
            bk = rho * (sd * (2.0 + m * (1.0 - 2.0 * sg)))
            nk = ak * f[k]
            fs[i, SB + k] = bk * f[k]
            fs[i, SBP + k] = bk * (f1[k] * pk)
            fs[i, SN + k] = nk
            p.append(pk)
            a.append(ak)
            n.append(nk)
        for h in hs:
            fs[i, SE + h] = e[h]
        q0 = sum(n[1:], n[0])
        q = [sum((n[k] * u[h][k] for k in ks[1:]), n[0] * u[h][0]) for h in hs]
        for k in ks:
            fk = a[k] * p[k] + q0 + (q[0] * u[0][k] + q[1] * u[1][k] + q[2] * u[2][k])
            acc[l, k] += fk * f1[k]
            acc[2 + l, k] += fk * fs[i, SF2 + k]
            for h in hs:
                acc[l, FAN * (h + 1) + k] += n[k] * e[h] + f[k] * q[h]
                acc[2 + l, FAN * (h + 1) + k] += f1[k] * q[h]
        return z

    def clear():
        def zero(i, z):
            acc[i] = jnp.zeros((24, 8, 128), F32)
            return z
        lax.fori_loop(0, 8, zero, 0)

    one_row = lax.broadcasted_iota(jnp.int32, (32, 192), 0)
    one_col = lax.broadcasted_iota(jnp.int32, (32, 192), 1) // 8
    ones = jnp.where((one_row % 8 < FAN) & (one_row // 8 * FAN + one_row % 8 == one_col), 1.0, 0.0).astype(BF16)

    def fold(v):
        out = []
        for l in range(2):
            hi, mid, lo = split3(acc[2 * v + l].reshape(192, 128))
            out.append((mm(ones, lo) + mm(ones, mid)) + mm(ones, hi))
        return jnp.concatenate(out, axis=1)

    clear()
    lax.fori_loop(0, 16, base_pass, 0, unroll=2)
    first, second = fold(0), fold(1)
    alpha, beta = first[0:8], second[0:8]
    force = [first[8 * h + 8 : 8 * h + 16] for h in hs]
    cross = [second[8 * h + 8 : 8 * h + 16] for h in hs]
    uv = unit[0] * force[0] + unit[1] * force[1] + unit[2] * force[2]
    sums[0] = alpha
    sums[1] = beta
    sums[2] = uv
    for h in hs:
        sums[3 + h] = force[h]
        sums[6 + h] = cross[h]

    def hvp(i, z):
        v = i // 16
        ch = lax.rem(i, 16)
        vl = 2 * v + ch // 8
        l = ch // 8
        f = [fs[ch, SF + k] for k in ks]
        rp = [bv[vl, k] for k in ks]
        u = lambda h, k: ub[l, h * FAN + k]
        du = lambda h, k: bv[vl, (h + 1) * FAN + k]
        df = [fs[ch, SF1 + k] * rp[k] for k in ks]
        de0 = sum(df[1:], df[0])
        de = []
        for h in hs:
            total = df[0] * u(h, 0) + f[0] * du(h, 0)
            for k in ks[1:]:
                total = total + (df[k] * u(h, k) + f[k] * du(h, k))
            de.append(total)
        e = [fs[ch, SE + h] for h in hs]
        dn, dfeat, n = [], [], []
        for k in ks:
            dp = de0
            for h in hs:
                dp = dp + (de[h] * u(h, k) + e[h] * du(h, k))
            pk, ak = fs[ch, SP + k], fs[ch, SA + k]
            da = fs[ch, SBP + k] * rp[k] + fs[ch, SB + k] * dp
            dn.append(da * f[k] + ak * df[k])
            n.append(fs[ch, SN + k])
            dfeat.append(da * pk + ak * dp)
        dq0 = sum(dn[1:], dn[0])
        dq = []
        for h in hs:
            total = dn[0] * u(h, 0) + n[0] * du(h, 0)
            for k in ks[1:]:
                total = total + (dn[k] * u(h, k) + n[k] * du(h, k))
            dq.append(total)
        for k in ks:
            tot = dfeat[k] + dq0 + (dq[0] * u(0, k) + dq[1] * u(1, k) + dq[2] * u(2, k))
            acc[vl, k] += fs[ch, SF1 + k] * tot
            for h in hs:
                acc[vl, FAN * (h + 1) + k] += (dn[k] * e[h] + n[k] * de[h]) + f[k] * dq[h]
        return z

    grs[...] = jnp.zeros((2, 128, 128), F32)

    def finish_hvp():
        u3 = [geo[h] for h in hs]
        ir = geo[4]
        for v in range(4):
            got = fold(v)
            dv = [edge(4 * c + v) for c in range(3)]
            rp = u3[0] * dv[0] + u3[1] * dv[1] + u3[2] * dv[2]
            du = [(dv[h] - u3[h] * rp) * ir for h in hs]
            al, be, w0 = sums[0], sums[1], sums[2]
            fo = [sums[3 + h] for h in hs]
            cr = [sums[6 + h] for h in hs]
            dal = got[0:8] + be * rp + (cr[0] * du[0] + cr[1] * du[1] + cr[2] * du[2])
            dfo = [got[8 * h + 8 : 8 * h + 16] + rp * cr[h] for h in hs]
            duv = sum((du[h] * fo[h] + u3[h] * dfo[h] for h in hs[1:]), du[0] * fo[0] + u3[0] * dfo[0])
            back = rp * ir
            for h in hs:
                val = dal * u3[h] + al * du[h]
                val = val + ir * ((dfo[h] - du[h] * w0 - u3[h] * duv) - back * (fo[h] - u3[h] * w0))
                for l in range(2):
                    grs[l, pl.ds(4 * h + v, 8, stride=16), :] = val[:, 128 * l : 128 * l + 128]
        for k in ks:
            cb[:, ATOMS * k : ATOMS * k + ATOMS] = rows3(jnp.concatenate([grs[l, 16 * k : 16 * k + 16, :] for l in range(2)], axis=1))

    def scatter(at):
        return sum3(mm(cb[...], inc_t[:, at]))

    def give_back(i):
        finish_hvp()
        pack_back(i, scatter(pl.ds(256, COLS - 256)))
        halo_send(i, 1)
        return scatter(pl.ds(0, 256))

    def combine_all(dst, cols, src, minus=None):
        for c in range(3):
            got = combine(cols, src, c)
            dst[4 * c : 4 * c + 4, :] = got if minus is None else minus[4 * c : 4 * c + 4, :] - got

    def transposed(proj):
        return [place([proj[u][w] for w in range(4)]) for u in range(4)]

    def less(gram, *projs):
        out = [[None] * 4 for _ in range(4)]
        for u in range(4):
            for w in range(u + 1):
                total = gram[u][w]
                for proj in projs:
                    for m in range(4):
                        total = total - proj[m][u] * proj[m][w]
                out[u][w] = total
        return out

    clear()
    lax.fori_loop(0, 64, hvp, 0, unroll=4)
    local = give_back(1)
    low, inv0 = cholesky(entries(ar_recv(0, 1), 0))
    cols0 = columns_of(inv0)
    combine_all(v1, cols0, own)
    halo_wait(1)
    own[...] = local + unpack_back(1)
    pack(2, own[...])
    halo_send(2, -1)
    combine_all(w1, cols0, own)
    tile = gram_rows(v1, w1) + pltpu.roll(gram_rows(w1, w1), 4, 1)
    ar_send(1, 0, jnp.concatenate([tile, zeros4], axis=0))
    tab[:, 0:256] = own[...]
    clear()
    ar_send(1, 1, ar_recv(1, 0))
    halo_wait(2)
    unpack(2, tab, False)

    gather(tab[...])
    tangents(1)
    lax.fori_loop(0, 64, hvp, 0, unroll=4)
    local = give_back(3)
    tile = ar_recv(1, 1)
    proj = entries(tile, 0)
    low, inv = cholesky(less(entries(pltpu.roll(tile, 124, 1), 0), proj))
    small_ref[0] = matrix(lambda u, w: proj[u][w])
    small_ref[2] = matrix(lambda u, w: low[w][u] if w >= u else None)
    cols1, cols_a = columns_of(inv), transposed(proj)
    combine_all(r1, cols_a, v1, w1)
    combine_all(v2, cols1, r1)
    combine_all(r1, cols_a, w1)
    combine_all(w1, cols1, r1)
    both = [[None] * 4 for _ in range(4)]
    for u in range(4):
        for w in range(u + 1):
            both[u][w] = sum((inv[u][m] * inv0[m][w] for m in range(w + 1, u + 1)), inv[u][w] * inv0[w][w])
    cols01 = columns_of(both)
    for i in range(4):
        halo_all(i).wait_send()
    for i in range(2):
        for g in range(2):
            ar_all(i, g).wait_send()
    halo_wait(3)
    tab[:, 0:256] = local + unpack_back(3)
    combine_all(own, cols01, tab.at[:, 0:256])
    own[0:12, :] = own[0:12, :] - w1[0:12, :]
    gram_w = pltpu.roll(jnp.concatenate([gram_rows(own, own), zeros4], axis=0), 4, 1)
    tile = jnp.concatenate([gram_rows(v2, own), gram_rows(v1, own)], axis=0) + gram_w
    for g in range(2):
        ar_send(2, g, tile)
        tile = ar_recv(2, g)
    proj = entries(tile, 0)
    prev = entries(tile, 4)
    gram = less(entries(pltpu.roll(tile, 124, 1), 0), proj, prev)
    combine_all(r1, transposed(proj), v2, own)
    combine_all(own, transposed(prev), v1, r1)
    low, inv = cholesky(gram)
    cols = columns_of(inv)
    for c in range(3):
        next_ref[c] = combine(cols, own, c)
    small_ref[1] = matrix(lambda u, w: proj[u][w])
    small_ref[3] = matrix(lambda u, w: low[w][u] if w >= u else None)
    for g in range(2):
        ar_all(2, g).wait_send()


def solution(mesh):
    sizes = tuple(mesh.shape[a] for a in AXES)
    cst = constants()
    slots = 2 * sizes[0] + sizes[1] * sizes[2] // 2

    def on_device(positions, species, start_block, neighbors, ghost_lists, embedding, radial_in, radial_out, readout):
        vmem = pl.BlockSpec(memory_space=pltpu.VMEM)
        vm = lambda *shape: pltpu.VMEM(shape, F32)
        dma = lambda *shape: pltpu.SemaphoreType.DMA(shape)
        operands = (
            positions.reshape(3, 1, ATOMS), species.reshape(1, ATOMS),
            jnp.transpose(start_block[0, 0, 0], (1, 0, 2)), neighbors.reshape(FAN, 1, ATOMS),
            ghost_lists, embedding, radial_in, radial_out.T, readout[None], jnp.asarray(cst),
        )
        out = pl.pallas_call(
            functools.partial(kernel, sizes),
            out_shape=(
                jax.ShapeDtypeStruct((3, 4, ATOMS), F32),
                jax.ShapeDtypeStruct((4, 4, 4), F32),
            ),
            in_specs=[pl.BlockSpec(memory_space=pltpu.HBM)] * 10,
            out_specs=(vmem, vmem),
            scratch_shapes=[dma(10)]
            + [pltpu.VMEM(x.shape, x.dtype) for x in operands]
            + [
                vm(ROWS, ATOMS),
                pltpu.VMEM((COLS, FAN * ATOMS), BF16),
                pltpu.VMEM((FAN * ATOMS, COLS), BF16),
                vm(ROWS, COLS),
                vm(ROWS, ATOMS), vm(ROWS, ATOMS), vm(ROWS, ATOMS), vm(ROWS, ATOMS),
                vm(2, 128, 128), vm(2, 128, 128),
                vm(6, 8, ATOMS), vm(9, 8, ATOMS),
                vm(2, 18, 8, 128), vm(8, 24, 8, 128),
                vm(16, 51, 8, 128), vm(8, 24, 8, 128),
                vm(CH, ATOMS), vm(4, 128, 128),
                pltpu.VMEM((CH, 3 * HID), BF16), vm(CH, 128),
                pltpu.VMEM((ATOMS, 128), BF16), pltpu.VMEM((8, 128), jnp.int32),
                pltpu.VMEM((3 * ROWS, FAN * ATOMS), BF16),
                vm(4, GHOST, 256), vm(4, GHOST, 256),
                vm(3, slots, 8, 128),
                dma(4), dma(4), dma(3, 2), dma(3, 2),
            ],
            compiler_params=pltpu.CompilerParams(
                collective_id=0, has_side_effects=True, vmem_limit_bytes=48 * 1024 * 1024
            ),
        )(*(pltpu.with_memory_space_constraint(x, pltpu.HBM) for x in operands))
        return jnp.transpose(out[0], (1, 0, 2))[None, None, None], out[1][:2], out[1][2:]

    return jax.shard_map(
        on_device,
        mesh=mesh,
        in_specs=(
            P("gx", "gy", "gz", None, None),
            P("gx", "gy", "gz", None),
            P("gx", "gy", "gz", None, None, None),
            P("gx", "gy", "gz", None, None),
            P("gx", "gy", "gz", None),
            P(), P(), P(), P(),
        ),
        out_specs=(P("gx", "gy", "gz", None, None, None), P(), P()),
        check_vma=False,
    )
```
